32 devices in a mesh: dp: 16 (over z, y, x), mp: 2 (over core).
Axes of the slice: x: 2, y: 2, z: 4, core: 2. Of those that a mesh axis runs over, the one named last changes fastest.
Arguments:
- log_rows: bfloat16 [98304, 256], P('dp'), may hold values from -6 to 6
- query_ids: int32 [98304], P('dp'), may hold values from 0 to 191, as said below
- doc_ranks: int32 [98304], P('dp'), may hold values from 0 to 511, as said below
- row_counts: int32 [16, 16], P('dp'), may hold values from 0 to 384, as said below
- list_lengths: int32 [192], P('dp'), may hold values from 64 to 512, as said below
- gains: float32 [192, 512], P('dp'), may hold values from 0.01 to 1
- weight_in: float32 [256, 4096], P(None, 'mp'), may hold values from -0.375 to 0.375
- bias_in: float32 [4096], P('mp'), may hold values from -3 to 3
- weight_out: float32 [4096], P('mp'), may hold values from -0.3 to 0.3
- moment_w: float32 [256, 4096], P(None, 'mp'), may hold values from -0.6 to 0.6
- second_w: float32 [256, 4096], P(None, 'mp'), may hold values from 0.05 to 2
- moment_b: float32 [4096], P('mp'), may hold values from -0.6 to 0.6
- second_b: float32 [4096], P('mp'), may hold values from 0.05 to 2
- moment_o: float32 [4096], P('mp'), may hold values from -0.6 to 0.6
- second_o: float32 [4096], P('mp'), may hold values from 0.05 to 2
Outputs:
- doc_lambdas: float32 [192, 512], P('dp')
- weight_in_next: float32 [256, 4096], P(None, 'mp')
- moment_w_next: float32 [256, 4096], P(None, 'mp')
- second_w_next: float32 [256, 4096], P(None, 'mp')
- bias_in_next: float32 [4096], P('mp')
- moment_b_next: float32 [4096], P('mp')
- second_b_next: float32 [4096], P('mp')
- weight_out_next: float32 [4096], P('mp')
- moment_o_next: float32 [4096], P('mp')
- second_o_next: float32 [4096], P('mp')
The draws below stay inside these ranges and needn't reach their ends.
Inputs may be any that keep to these rules, and one draw needn't show every extreme that they name: row_counts[s, j] is at most 384; the live rows that all shards hold for owner j number list_lengths summed over owner j's queries j * 12 to j * 12 + 11; some owner receives 384 live rows from every shard. `query_ids`: A live row of the block for owner j belongs to one of owner j's queries; rows that are not live carry arbitrary ids. `doc_ranks`: the live rows of query q carry the ranks 0 to list_lengths[q] - 1, each once; rows that are not live carry arbitrary ranks. `list_lengths`: every owner has a list of 512 documents.
All inputs are finite; a program needn't handle non-finite values.
Results may differ from the reference program's by a relative error of at most 0.0049.
Values may be sent and summed in bfloat16 or wider, within the bound.
A program may use at most 192 MiB of HBM per device.

```python
import math
import jax
import jax.numpy as jnp
from jax import lax

F = 256
H = 4096
LIST = 512
Q_DEV = 12
QUERIES = 192
CAP = 384
LOG_DEV = 6144
N_DP = 16


def layout(key):
    shard_count = QUERIES // Q_DEV
    key = jax.random.fold_in(key, 11)
    subkeys = jax.random.split(key, 8)
    owners = jnp.arange(shard_count)
    list_index = jnp.arange(Q_DEV)
    lengths = jax.random.randint(subkeys[0], (shard_count, Q_DEV), LIST // 8, LIST + 1)
    longest = jax.random.randint(subkeys[1], (shard_count,), 0, Q_DEV)
    lengths = jnp.where(list_index[None, :] == longest[:, None], LIST, lengths)
    full_owner = jax.random.randint(subkeys[2], (), 0, shard_count)
    lengths = jnp.where(owners[:, None] == full_owner, LIST, lengths)
    short_owner = (full_owner + 1 + jax.random.randint(subkeys[3], (), 0, shard_count - 1)) % shard_count
    short_list = (longest[short_owner] + 1) % Q_DEV
    lengths = jnp.where((owners[:, None] == short_owner) & (list_index[None, :] == short_list), LIST // 8, lengths)
    totals = jnp.sum(lengths, axis=1)
    order_keys = jax.random.randint(subkeys[4], (shard_count, shard_count), 0, 1 << 20) * shard_count + owners[None, :]
    source_order = jnp.argsort(order_keys, axis=1)
    position = jnp.argsort(source_order, axis=1)
    counts = jnp.clip(totals[:, None] - CAP * position, 0, CAP).T
    row_index = jnp.arange(CAP)
    doc_index = position.T[:, :, None] * CAP + row_index[None, None, :]
    starts = jnp.cumsum(lengths, axis=1) - lengths
    list_of_doc = jnp.sum((doc_index[..., None] >= starts[None, :, None, 1:]).astype(jnp.int32), axis=-1)
    inner_pos = doc_index - starts.reshape(-1)[owners[None, :, None] * Q_DEV + list_of_doc]
    shuffle_keys = jax.random.randint(subkeys[5], (QUERIES, LIST), 0, 1 << 20) * LIST + jnp.arange(LIST)[None, :]
    shuffled = jnp.argsort(shuffle_keys, axis=1)
    is_kept = shuffled < lengths.reshape(-1)[:, None]
    kept_first = jnp.argsort(jnp.where(is_kept, 0, 1) * LIST + jnp.arange(LIST)[None, :], axis=1)
    rank_table = jnp.take_along_axis(shuffled, kept_first, axis=1)
    live_query = owners[None, :, None] * Q_DEV + list_of_doc
    table_index = live_query * LIST + jnp.clip(inner_pos, 0, LIST - 1)
    live_rank = rank_table.reshape(-1)[table_index]
    is_live = row_index[None, None, :] < counts[:, :, None]
    pad_query = jax.random.randint(subkeys[6], is_live.shape, 0, QUERIES)
    pad_rank = jax.random.randint(subkeys[7], is_live.shape, 0, LIST)
    query_out = jnp.where(is_live, live_query, pad_query).astype(jnp.int32)
    rank_out = jnp.where(is_live, live_rank, pad_rank).astype(jnp.int32)
    return (counts.astype(jnp.int32), query_out.reshape(-1), rank_out.reshape(-1), lengths.reshape(-1).astype(jnp.int32))


def draw_row_counts(key, part):
    return layout(key)[0]


def draw_query_ids(key, part):
    return layout(key)[1]


def draw_doc_ranks(key, part):
    return layout(key)[2]


def draw_list_lengths(key, part):
    return layout(key)[3]


def levels(key, dims, shards, least, largest):
    def one(dim, shards_of):
        heights = jax.random.uniform(jax.random.fold_in(jax.random.fold_in(key, 6), dim), (shards_of,), jnp.float32, least / len(shards), largest / len(shards))
        return jnp.repeat(jnp.exp(heights), dims[dim] // shards_of).reshape((-1,) + (1,) * (len(dims) - dim - 1))

    factor_of = one(*shards[0])
    for cut in shards[1:]:
        factor_of = factor_of * one(*cut)
    return factor_of


def bell_draw(key, extent, width, limit, cuts=(), dtype=jnp.bfloat16):
    array = width * jax.random.normal(key, extent, jnp.float32)
    if cuts:
        array = array * levels(key, extent, cuts, -0.22, 0.18)
    return jnp.clip(array, -limit, limit).astype(dtype)


def setup_inputs(seed: int = 0) -> dict:
    key_list = jax.random.split(jax.random.key(seed), 16)
    return {
        "log_rows": bell_draw(key_list[0], (N_DP * LOG_DEV, F), 1.0, 6.0, ((0, 16),)),
        "query_ids": draw_query_ids(jax.random.fold_in(key_list[15], 71), 0),
        "doc_ranks": draw_doc_ranks(jax.random.fold_in(key_list[15], 71), 0),
        "row_counts": draw_row_counts(jax.random.fold_in(key_list[15], 71), 0),
        "list_lengths": draw_list_lengths(jax.random.fold_in(key_list[15], 71), 0),
        "gains": jnp.clip(jnp.exp(math.log(1.0) - 4.6051702 * jax.random.uniform(key_list[5], (QUERIES, LIST), jnp.float32) ** levels(key_list[5], (QUERIES, LIST), ((0, 16),), -0.2, 0.2)), 0.01, 1.0),
        "weight_in": bell_draw(key_list[6], (F, H), F ** -0.5, 0.375, ((1, 2),), jnp.float32),
        "bias_in": bell_draw(key_list[7], (H,), 0.5, 3.0, ((0, 2),), jnp.float32),
        "weight_out": bell_draw(key_list[8], (H,), 0.05, 0.3, ((0, 2),), jnp.float32),
        "moment_w": bell_draw(key_list[9], (F, H), 0.1, 0.6, ((1, 2),), jnp.float32),
        "second_w": jnp.clip(jnp.exp(math.log(2.0) - 3.6888794 * jax.random.uniform(key_list[10], (F, H), jnp.float32) ** levels(key_list[10], (F, H), ((1, 2),), -0.2, 0.2)), 0.05, 2.0),
        "moment_b": bell_draw(key_list[11], (H,), 0.1, 0.6, ((0, 2),), jnp.float32),
        "second_b": jnp.clip(jnp.exp(math.log(2.0) - 3.6888794 * jax.random.uniform(key_list[12], (H,), jnp.float32) ** levels(key_list[12], (H,), ((0, 2),), -0.2, 0.2)), 0.05, 2.0),
        "moment_o": bell_draw(key_list[13], (H,), 0.1, 0.6, ((0, 2),), jnp.float32),
        "second_o": jnp.clip(jnp.exp(math.log(2.0) - 3.6888794 * jax.random.uniform(key_list[14], (H,), jnp.float32) ** levels(key_list[14], (H,), ((0, 2),), -0.2, 0.2)), 0.05, 2.0),
    }


beta_one = 0.9
beta_two = 0.95
learn_rate = 0.001
adam_eps = 1e-08

def gelu_tanh(values):
    return jax.nn.gelu(values, approximate=True)

def list_lambdas(score_rows, gain_rows, lengths):
    list_width = gain_rows.shape[1]
    positions = jnp.arange(list_width)
    discount = 1.0 / jnp.log2(2.0 + positions.astype(jnp.float32))
    keep_mask = (positions[None, :] < lengths[:, None]).astype(jnp.float32)

    def per_list(triple):
        row_score, row_gain, row_keep = triple
        delta_s = row_score[:, None] - row_score[None, :]
        delta_g = row_gain[:, None] - row_gain[None, :]
        weight = jnp.abs(discount[:, None] - discount[None, :]) * row_keep[:, None] * row_keep[None, :]
        pair_term = jnp.maximum(delta_g, 0.0) * jax.nn.sigmoid(-delta_s) - jnp.maximum(-delta_g, 0.0) * jax.nn.sigmoid(delta_s)
        return -lax.optimization_barrier(jnp.sum(weight * pair_term, axis=1))
    return lax.map(per_list, (score_rows, gain_rows, keep_mask))

def adam_step(weights, moment, second, gradient):
    moment_next = beta_one * moment + (1.0 - beta_one) * gradient
    second_next = beta_two * second + (1.0 - beta_two) * gradient * gradient
    weights_next = weights - learn_rate * moment_next / (jnp.sqrt(second_next) + adam_eps)
    return (weights_next, moment_next, second_next)

def reference(log_rows, query_ids, doc_ranks, row_counts, list_lengths, gains, weight_in, bias_in, weight_out, moment_w, second_w, moment_b, second_b, moment_o, second_o):
    shard_count = QUERIES // Q_DEV
    owner_rows = Q_DEV * LIST
    blocks = log_rows.reshape(shard_count, shard_count, CAP, F)
    is_live = jnp.arange(CAP)[None, None, :] < row_counts[:, :, None]
    slot_index = jnp.where(is_live, query_ids.reshape(shard_count, shard_count, CAP) % Q_DEV * LIST + doc_ranks.reshape(shard_count, shard_count, CAP), owner_rows)
    w_low = weight_in.astype(jnp.bfloat16)
    per_owner_inputs = (jnp.swapaxes(blocks, 0, 1), jnp.swapaxes(slot_index, 0, 1), list_lengths.reshape(shard_count, Q_DEV), gains.reshape(shard_count, Q_DEV, LIST))

    def per_owner(totals, pieces):
        owner_blocks, owner_slots, owner_lengths, owner_gains = pieces
        placed = jnp.zeros((owner_rows, F), jnp.bfloat16).at[owner_slots.reshape(-1)].set(owner_blocks.reshape(-1, F), mode='drop')
        pre_act = jnp.dot(placed, w_low, preferred_element_type=jnp.float32) + bias_in
        hidden, gelu_back = jax.vjp(gelu_tanh, pre_act)
        scores = lax.optimization_barrier(jnp.sum(hidden * weight_out, axis=1))
        lambdas = list_lambdas(scores.reshape(Q_DEV, LIST), owner_gains, owner_lengths)
        row_lambdas = lambdas.reshape(-1) / QUERIES
        grad_pre = gelu_back(row_lambdas[:, None] * weight_out)[0]
        grad_w = lax.dot_general(placed, grad_pre.astype(jnp.bfloat16), (((0,), (0,)), ((), ())), preferred_element_type=jnp.float32)
        grad_b = lax.optimization_barrier(jnp.sum(grad_pre, axis=0))
        grad_o = lax.optimization_barrier(jnp.sum(row_lambdas[:, None] * hidden, axis=0))
        return ((totals[0] + grad_w, totals[1] + grad_b, totals[2] + grad_o), lambdas)
    start_totals = (jnp.zeros((F, H), jnp.float32), jnp.zeros((H,), jnp.float32), jnp.zeros((H,), jnp.float32))
    sums, lambdas = lax.scan(per_owner, start_totals, per_owner_inputs)
    doc_lambdas = lambdas.reshape(QUERIES, LIST)
    weight_next, moment_w_next, second_w_next = adam_step(weight_in, moment_w, second_w, sums[0])
    bias_next, moment_b_next, second_b_next = adam_step(bias_in, moment_b, second_b, sums[1])
    out_next, moment_o_next, second_o_next = adam_step(weight_out, moment_o, second_o, sums[2])
    return (doc_lambdas, weight_next, moment_w_next, second_w_next, bias_next, moment_b_next, second_b_next, out_next, moment_o_next, second_o_next)
```

```python
import functools
import math

import jax
import jax.numpy as jnp
from jax import lax
from jax.experimental import pallas as pl
from jax.experimental.pallas import tpu as pltpu
from jax.sharding import PartitionSpec as P

beta_one = 0.9
beta_two = 0.95
learn_rate = 0.001
adam_eps = 1e-08

C0 = math.sqrt(2.0 / math.pi)
C1 = C0 * 0.044715
MESH = pl.DeviceIdType.MESH
LANES = 128
BLOCK = 512
WIDE = 256
BF = jnp.bfloat16
F32 = jnp.float32


def split_three(values):
    first = values.astype(BF)
    rest = values - first.astype(F32)
    second = rest.astype(BF)
    third = (rest - second.astype(F32)).astype(BF)
    return first, second, third


def score_kernel(
    n, cores, scale, x_ref, w_ref, b_ref, wo_ref, slot_ref, gain_ref, keep_ref, weight_ref,
    h_ref, g_ref, doc_ref, lam_ref,
    w_low, msg_ref, arrive, lam_out, lam_in, s_row, l_row, s_col, g_col, lam_t,
    send_a, recv_a, send_l, recv_l,
):
    me = lax.axis_index("dp")
    core = lax.axis_index("mp")
    high_rows = gain_ref.shape[0]
    per_list = weight_ref.shape[0]
    lists = high_rows // per_list
    cap = msg_ref.shape[2]
    step = pl.program_id(0)
    barrier = pltpu.get_barrier_semaphore()

    @pl.when(step == 0)
    def _():
        @pl.loop(1, n)
        def _(k):
            peer = lax.rem(me + k, n)
            for d in range(cores):
                pl.semaphore_signal(
                    barrier, inc=1, device_id=(peer, lax.rem(core + d, cores)), device_id_type=MESH
                )

        for d in range(1, cores):
            pl.semaphore_signal(
                barrier, inc=1, device_id=(me, lax.rem(core + d, cores)), device_id_type=MESH
            )
        w_low[...] = w_ref[...].astype(BF)

    x = x_ref[...]
    acc = jnp.zeros((cap, LANES), F32)
    for k in range(h_ref.shape[0]):
        cols = slice(k * WIDE, (k + 1) * WIDE)
        v = (jnp.dot(x, w_low[:, cols], preferred_element_type=F32) + b_ref[:, cols]).astype(BF)
        v2 = v * v
        t = jnp.tanh(v * (BF(C1) * v2 + BF(C0)))
        up = BF(1.0) + t
        hb = v * up
        h_ref[k] = hb
        g_ref[k] = up + (hb * (BF(1.0) - t)) * (BF(3.0 * C1) * v2 + BF(C0))
        acc = acc + jnp.dot(hb, wo_ref[cols, :], preferred_element_type=F32)
    msg_ref[step, 0:1, :] = jnp.sum(acc.T, axis=0, keepdims=True)
    msg_ref[step, 1:3, :] = slot_ref[0]

    @pl.when(step == 0)
    def _():
        pl.semaphore_wait(barrier, cores * n - 1)

    def score_copy(peer, d):
        return pltpu.make_async_remote_copy(
            src_ref=msg_ref.at[peer],
            dst_ref=arrive.at[core, me],
            send_sem=send_a.at[d, peer],
            recv_sem=recv_a.at[core, me],
            device_id=(peer, lax.rem(core + d, cores)),
            device_id_type=MESH,
        )

    def arrival(from_core, peer):
        return pltpu.make_async_remote_copy(
            src_ref=msg_ref.at[peer],
            dst_ref=arrive.at[from_core, peer],
            send_sem=send_a.at[0, peer],
            recv_sem=recv_a.at[from_core, peer],
            device_id=(peer, from_core),
            device_id_type=MESH,
        )

    def finish():
        arrive[core, me] = msg_ref[me]
        high_iota = lax.broadcasted_iota(jnp.int32, (LANES, cap), 0).astype(F32)

        def absorb(shard, total):
            first = arrive[0, shard]
            value = first[0:1]
            for c in range(1, cores):
                value = value + arrive[c, shard][0:1]
            low = (first[2:3] == high_iota).astype(F32).astype(BF)
            at_high = first[1:2] == high_iota[:high_rows]
            spread = jnp.concatenate(
                [jnp.where(at_high, piece.astype(F32), 0.0).astype(BF) for piece in split_three(value)],
                axis=0,
            )
            sums = lax.dot_general(
                spread, low, (((1,), (1,)), ((), ())), preferred_element_type=F32
            )
            return total + (
                sums[:high_rows] + sums[high_rows : 2 * high_rows] + sums[2 * high_rows :]
            )

        for d in range(1, cores):
            arrival(lax.rem(core + d, cores), me).wait_recv()
        total = absorb(me, jnp.zeros((high_rows, LANES), F32))

        def take(k, total):
            for j in range(3):
                for c in range(cores):
                    arrival(c, lax.rem(me + 1 + 3 * k + j, n)).wait_recv()
            for j in range(3):
                total = absorb(lax.rem(me + 1 + 3 * k + j, n), total)
            return total

        total = lax.fori_loop(0, (n - 1) // 3, take, total)
        scores = jnp.where(keep_ref[...] > 0.0, 0.5 * total, -1e30)
        s_row[...] = scores
        padding = jnp.zeros((LANES - high_rows, LANES), F32)
        s_turn = jnp.concatenate([scores, padding], axis=0).T
        g_turn = jnp.concatenate([gain_ref[...], padding], axis=0).T
        for i in range(high_rows):
            s_col[i] = s_turn[:, i : i + 1]
            g_col[i] = g_turn[:, i : i + 1]

        def one_list(q, carry):
            base = q * per_list
            row_s = jnp.concatenate([s_row[pl.ds(base + k, 1), :] for k in range(per_list)], axis=1)
            row_g = jnp.concatenate([gain_ref[pl.ds(base + k, 1), :] for k in range(per_list)], axis=1)
            sums = jnp.zeros((8, row_s.shape[1]), F32)
            for k in range(per_list):
                col_s = s_col[base + k]
                col_g = g_col[base + k]
                for r in range(0, LANES, 8):
                    delta_g = col_g[r : r + 8] - row_g
                    delta_t = jnp.tanh(col_s[r : r + 8] - row_s)
                    sums = sums + weight_ref[k, r : r + 8, :] * (delta_g - jnp.abs(delta_g) * delta_t)
            lam = 0.5 * jnp.sum(sums, axis=0, keepdims=True)
            for k in range(per_list):
                l_row[pl.ds(base + k, 1), :] = lam[:, k * LANES : (k + 1) * LANES]
            return carry

        lax.fori_loop(0, lists, one_list, 0)
        doc_ref[...] = l_row[...]
        turned = jnp.concatenate([l_row[...] * scale, padding], axis=0).T
        lam_t[...] = jnp.concatenate(split_three(turned), axis=1)

        def answer(shard):
            info = arrive[core, shard]
            low = info[2:3] == high_iota
            high = (info[1:2] == high_iota).astype(F32).astype(BF)
            spread = jnp.dot(
                lam_t[...], jnp.concatenate([high] * 3, axis=0), preferred_element_type=F32
            )
            return jnp.sum(jnp.where(low, spread, 0.0), axis=0, keepdims=True)

        def lam_copy(peer):
            return pltpu.make_async_remote_copy(
                src_ref=lam_out.at[peer],
                dst_ref=lam_in.at[me],
                send_sem=send_l.at[peer],
                recv_sem=recv_l.at[me],
                device_id=(peer, core),
                device_id_type=MESH,
            )

        def lam_arrival(peer):
            return pltpu.make_async_remote_copy(
                src_ref=lam_out.at[peer],
                dst_ref=lam_in.at[peer],
                send_sem=send_l.at[peer],
                recv_sem=recv_l.at[peer],
                device_id=(peer, core),
                device_id_type=MESH,
            )

        @pl.loop(0, (n - 1) // 3)
        def _(k):
            peers = [lax.rem(me + 1 + 3 * k + j, n) for j in range(3)]
            replies = [answer(peer) for peer in peers]
            for peer, reply in zip(peers, replies):
                lam_out[peer] = reply
            for peer in peers:
                lam_copy(peer).start()

        lam_ref[me] = answer(me)

        @pl.loop(1, n)
        def _(k):
            peer = lax.rem(me + k, n)
            lam_arrival(peer).wait_recv()
            lam_ref[peer] = lam_in[peer]

        @pl.loop(1, n)
        def _(k):
            peer = lax.rem(me + k, n)
            for d in range(cores):
                score_copy(peer, d).wait_send()
            lam_copy(peer).wait_send()

        for d in range(1, cores):
            score_copy(me, d).wait_send()

    for d in range(1, cores):
        score_copy(step, d).start()

    @pl.when(step != me)
    def _():
        score_copy(step, 0).start()

    pl.when(step == n - 1)(finish)


def score(n, cores, rows, weights, bias, wo_pair, slots, gain_rows, keep_rows, pair_weights, total_lists):
    total, features = rows.shape
    hidden = weights.shape[1]
    groups = hidden // WIDE
    cap = total // n
    high_rows = gain_rows.shape[0]

    def whole(array):
        return pl.BlockSpec(array.shape, lambda i: (0,) * array.ndim)

    block = pl.BlockSpec((groups, cap, WIDE), lambda i: (0, i, 0))
    kept = jax.ShapeDtypeStruct((groups, total, WIDE), BF)
    return pl.pallas_call(
        functools.partial(score_kernel, n, cores, 1.0 / total_lists),
        grid=(n,),
        in_specs=[
            pl.BlockSpec((cap, features), lambda i: (i, 0)),
            whole(weights), whole(bias), whole(wo_pair),
            pl.BlockSpec((1, 2, cap), lambda i: (i, 0, 0)),
            whole(gain_rows), whole(keep_rows), whole(pair_weights),
        ],
        out_specs=[
            block, block,
            pl.BlockSpec((high_rows, LANES), lambda i: (0, 0)),
            pl.BlockSpec((n, 1, cap), lambda i: (0, 0, 0)),
        ],
        out_shape=[
            kept, kept,
            jax.ShapeDtypeStruct((high_rows, LANES), F32),
            jax.ShapeDtypeStruct((n, 1, cap), F32),
        ],
        scratch_shapes=[
            pltpu.VMEM((features, hidden), BF),
            pltpu.VMEM((n, 3, cap), F32),
            pltpu.VMEM((cores, n, 3, cap), F32),
            pltpu.VMEM((n, 1, cap), F32),
            pltpu.VMEM((n, 1, cap), F32),
            pltpu.VMEM((high_rows, LANES), F32),
            pltpu.VMEM((high_rows, LANES), F32),
            pltpu.VMEM((high_rows, LANES, 1), F32),
            pltpu.VMEM((high_rows, LANES, 1), F32),
            pltpu.VMEM((LANES, 3 * LANES), BF),
            pltpu.SemaphoreType.DMA((cores, n)),
            pltpu.SemaphoreType.DMA((cores, n)),
            pltpu.SemaphoreType.DMA((n,)),
            pltpu.SemaphoreType.DMA((n,)),
        ],
        compiler_params=pltpu.CompilerParams(
            collective_id=0, has_side_effects=True, vmem_limit_bytes=48 << 20
        ),
    )(rows, weights, bias, wo_pair, slots, gain_rows, keep_rows, pair_weights)


def tail_rows(grad_b, grad_o):
    spot = lax.broadcasted_iota(jnp.int32, (16, grad_b.shape[1]), 0)
    top_b = grad_b.astype(BF).astype(F32)
    top_o = grad_o.astype(BF).astype(F32)
    tail = jnp.where(spot == 0, top_b, jnp.where(spot == 1, top_o, 0.0))
    tail = jnp.where(spot == 2, grad_b - top_b, jnp.where(spot == 3, grad_o - top_o, tail))
    return tail.astype(BF)


def grad_kernel(
    n, parts_per_span, x_ref, lam_ref, wo_ref, h_hbm, g_hbm, out_ref,
    left, h_buf, g_buf, parts, arrive, mine, full,
    fetch_sem, send_a, recv_a, send_b, recv_b,
):
    me = lax.axis_index("dp")
    core = lax.axis_index("mp")
    groups = h_hbm.shape[0]
    features = x_ref.shape[1]
    chunk_rows = parts.shape[1]
    padded = chunk_rows * parts_per_span
    per_group = WIDE // LANES * parts_per_span
    first = me // per_group + 1

    def fetches(k):
        group = lax.rem(first + k, groups)
        slot = lax.rem(k, 2)
        return (
            pltpu.make_async_copy(g_hbm.at[group], g_buf.at[slot], fetch_sem.at[slot, 0]),
            pltpu.make_async_copy(h_hbm.at[group], h_buf.at[slot], fetch_sem.at[slot, 1]),
        )

    for one in fetches(0):
        one.start()

    barrier = pltpu.get_barrier_semaphore()

    @pl.loop(1, n)
    def _(k):
        peer = lax.rem(me + k, n)
        pl.semaphore_signal(barrier, inc=1, device_id=(peer, core), device_id_type=MESH)

    @pl.loop(0, lam_ref.shape[0])
    def _(i):
        lam = lam_ref[i]
        top = lam.astype(BF).astype(F32)
        place = lax.broadcasted_iota(jnp.int32, (16, BLOCK), 0)
        pair = jnp.where(place == 0, top, jnp.where(place == 1, lam - top, 0.0)).astype(BF)
        at = pl.ds(pl.multiple_of(i * BLOCK, BLOCK), BLOCK)
        left[:features, at] = (x_ref[at, :].astype(F32).T * lam).astype(BF)
        left[features:, at] = pair

    pl.semaphore_wait(barrier, n - 1)

    def copy(source, target, send, recvs, peer, slot):
        return pltpu.make_async_remote_copy(
            src_ref=source,
            dst_ref=target.at[slot],
            send_sem=send,
            recv_sem=recvs.at[slot],
            device_id=(peer, core),
            device_id_type=MESH,
        )

    @pl.loop(0, groups)
    def _(k):
        for one in fetches(k):
            one.wait()

        @pl.when(k + 1 < groups)
        def _():
            for one in fetches(k + 1):
                one.start()

        group = lax.rem(first + k, groups)
        slot = lax.rem(k, 2)
        half_wo = wo_ref[group]
        sums = jnp.dot(left[...], g_buf[slot], preferred_element_type=F32)
        sums_o = jnp.dot(left[features:, :], h_buf[slot], preferred_element_type=F32)
        grad_b = jnp.sum(sums[features:], axis=0, keepdims=True) * half_wo
        grad_o = 0.5 * jnp.sum(sums_o, axis=0, keepdims=True)
        pieces = [
            (sums[:features] * half_wo).astype(BF),
            tail_rows(grad_b, grad_o),
        ]
        if padded > features + 16:
            pieces.append(jnp.zeros((padded - features - 16, WIDE), BF))
        block = jnp.concatenate(pieces, axis=0)
        for j in range(per_group):
            span, part = j // parts_per_span, j % parts_per_span
            parts[group * per_group + j] = block[
                part * chunk_rows : (part + 1) * chunk_rows, span * LANES : (span + 1) * LANES
            ]
        for j in range(per_group):
            owner = group * per_group + j

            @pl.when(owner != me)
            def _():
                copy(parts.at[owner], arrive, send_a.at[owner], recv_a, owner, me).start()

    def take(k, total):
        peer = lax.rem(me + n - k, n)
        copy(parts.at[peer], arrive, send_a.at[peer], recv_a, peer, peer).wait_recv()
        return total + arrive[peer].astype(F32)

    total = lax.fori_loop(1, n, take, parts[me].astype(F32))
    mine[...] = total.astype(BF)

    @pl.when(lax.rem(me, parts_per_span) == features // chunk_rows)
    def _():
        at = features % chunk_rows
        mine[at : at + 16, :] = tail_rows(
            total[at : at + 1] + total[at + 2 : at + 3],
            total[at + 1 : at + 2] + total[at + 3 : at + 4],
        )

    inner = 4
    outer = n // inner
    row, col = me // inner, lax.rem(me, inner)

    def outer_peer(i):
        return lax.rem(row + i, outer) * inner + col

    def inner_peer(j):
        return row * inner + lax.rem(col + j, inner)

    def send_outer(i):
        peer = outer_peer(i)
        return copy(mine, full, send_b.at[0, peer], recv_b, peer, me)

    def send_inner(j):
        return copy(mine, full, send_b.at[j, me], recv_b, inner_peer(j), me)

    def pass_on(i, j):
        chunk = outer_peer(outer - i)
        return copy(full.at[chunk], full, send_b.at[j, chunk], recv_b, inner_peer(j), chunk)

    def landed(chunk):
        return copy(mine, full, send_b.at[0, chunk], recv_b, me, chunk)

    for i in range(1, outer):
        send_outer(i).start()
    for j in range(1, inner):
        send_inner(j).start()
    out_ref[me] = mine[...]
    for i in range(1, outer):
        chunk = outer_peer(outer - i)
        landed(chunk).wait_recv()
        for j in range(1, inner):
            pass_on(i, j).start()
        out_ref[chunk] = full[chunk]
    for i in range(outer):
        for j in range(1, inner):
            chunk = lax.rem(row + outer - i, outer) * inner + lax.rem(col + j, inner)
            landed(chunk).wait_recv()
            out_ref[chunk] = full[chunk]

    @pl.loop(1, n)
    def _(k):
        peer = lax.rem(me + k, n)
        copy(parts.at[peer], arrive, send_a.at[peer], recv_a, peer, me).wait_send()

    for i in range(1, outer):
        send_outer(i).wait_send()
        for j in range(1, inner):
            pass_on(i, j).wait_send()
    for j in range(1, inner):
        send_inner(j).wait_send()


def gradients(n, rows, hid, slope, lam, wo_half, parts_per_span, chunk_rows):
    total, features = rows.shape
    groups = hid.shape[0]
    vmem = pl.BlockSpec(memory_space=pltpu.VMEM)
    hbm = pl.BlockSpec(memory_space=pl.ANY)
    shape = (n, chunk_rows, LANES)
    return pl.pallas_call(
        functools.partial(grad_kernel, n, parts_per_span),
        in_specs=[vmem, vmem, vmem, hbm, hbm],
        out_specs=vmem,
        out_shape=jax.ShapeDtypeStruct(shape, BF),
        scratch_shapes=[
            pltpu.VMEM((features + 16, total), BF),
            pltpu.VMEM((2, total, WIDE), BF),
            pltpu.VMEM((2, total, WIDE), BF),
            pltpu.VMEM(shape, BF),
            pltpu.VMEM(shape, BF),
            pltpu.VMEM(shape[1:], BF),
            pltpu.VMEM(shape, BF),
            pltpu.SemaphoreType.DMA((2, 2)),
            pltpu.SemaphoreType.DMA((n,)),
            pltpu.SemaphoreType.DMA((n,)),
            pltpu.SemaphoreType.DMA((4, n)),
            pltpu.SemaphoreType.DMA((n,)),
        ],
        compiler_params=pltpu.CompilerParams(
            collective_id=1, has_side_effects=True, vmem_limit_bytes=48 << 20
        ),
    )(rows, lam, wo_half, hid, slope)


def adam_step(weights, moment, second, gradient):
    moment_next = beta_one * moment + (1.0 - beta_one) * gradient
    second_next = beta_two * second + (1.0 - beta_two) * gradient * gradient
    weights_next = weights - learn_rate * moment_next / (jnp.sqrt(second_next) + adam_eps)
    return (weights_next, moment_next, second_next)


def adam_kernel(g_ref, w_ref, m_ref, s_ref, w_out, m_out, s_out):
    features = w_ref.shape[0]
    for k in range(g_ref.shape[0]):
        cols = slice(k * LANES, (k + 1) * LANES)
        grad = g_ref[k, :features, :].astype(F32)
        w_out[:, cols], m_out[:, cols], s_out[:, cols] = adam_step(
            w_ref[:, cols], m_ref[:, cols], s_ref[:, cols], grad
        )


def adam_matrix(grads, weights, moment, second):
    features, hidden = weights.shape
    group = 4
    block = pl.BlockSpec((features, group * LANES), lambda i: (0, i))
    return pl.pallas_call(
        adam_kernel,
        grid=(hidden // (group * LANES),),
        in_specs=[pl.BlockSpec((group,) + grads.shape[1:], lambda i: (i, 0, 0))] + [block] * 3,
        out_specs=[block] * 3,
        out_shape=[jax.ShapeDtypeStruct(weights.shape, F32)] * 3,
    )(grads, weights, moment, second)


def per_device(
    log_rows, query_ids, doc_ranks, row_counts, list_lengths, gains,
    weight_in, bias_in, weight_out, moment_w, second_w,
    moment_b, second_b, moment_o, second_o,
):
    n = lax.axis_size("dp")
    total, features = log_rows.shape
    cap = total // n
    hidden = weight_in.shape[1]
    list_count, list_width = gains.shape
    high_rows = list_count * list_width // LANES
    per_list = list_width // LANES

    is_live = jnp.arange(cap)[None, :] < row_counts.reshape(n, 1)
    slots = query_ids.reshape(n, cap) % list_count * list_width + doc_ranks.reshape(n, cap)
    high = jnp.where(is_live, slots // LANES, -1).astype(F32)
    low = (slots % LANES).astype(F32)

    positions = jnp.arange(list_width)
    discount = 1.0 / jnp.log2(2.0 + positions.astype(F32))
    weights = jnp.abs(discount[:, None] - discount[None, :]).reshape(per_list, LANES, list_width)
    keep = positions[None, :] < list_lengths[:, None]
    gain_rows = jnp.where(keep, gains, 0.0).reshape(high_rows, LANES)
    keep_rows = keep.astype(F32).reshape(high_rows, LANES)

    wo_half = 0.5 * weight_out
    wo_top = lax.reduce_precision(wo_half, exponent_bits=8, mantissa_bits=7)
    wo_rest = (wo_half - wo_top).astype(BF)
    wo_top = wo_top.astype(BF)
    lane = jnp.arange(LANES)[None, :]
    wo_pair = jnp.where(
        lane == 0, wo_top[:, None], jnp.where(lane == 1, wo_rest[:, None], jnp.zeros((), BF))
    )

    hid, slope, doc_rows, lam = score(
        n, lax.axis_size("mp"), log_rows, weight_in, bias_in.reshape(1, hidden), wo_pair,
        jnp.stack([high, low], axis=1), gain_rows, keep_rows, weights, list_count * n,
    )
    lambdas = doc_rows.reshape(list_count, list_width)

    spans = hidden // LANES
    row_parts = max(1, n // spans)
    unit = 16 * row_parts
    padded = (features + 16 + unit - 1) // unit * unit
    grads = gradients(
        n, log_rows, hid, slope, lam.reshape(total // BLOCK, 1, BLOCK),
        wo_half.reshape(hidden // WIDE, 1, WIDE), row_parts, padded // row_parts,
    )
    grads = grads.reshape(spans, padded, LANES)
    tail = grads[:, features : features + 4, :].astype(F32)
    grad_b = (tail[:, 0] + tail[:, 2]).reshape(hidden)
    grad_o = (tail[:, 1] + tail[:, 3]).reshape(hidden)
    return (
        lambdas,
        *adam_matrix(grads, weight_in, moment_w, second_w),
        *adam_step(bias_in, moment_b, second_b, grad_b),
        *adam_step(weight_out, moment_o, second_o, grad_o),
    )


def solution(mesh):
    dp, mp, both = P("dp"), P("mp"), P(None, "mp")
    rows = P("dp", None)
    return jax.shard_map(
        per_device,
        mesh=mesh,
        in_specs=(rows, dp, dp, rows, dp, rows, both, mp, mp, both, both, mp, mp, mp, mp),
        out_specs=(rows, both, both, both, mp, mp, mp, mp, mp, mp),
        check_vma=False,
    )
```

```python
import functools
import math

import jax
import jax.numpy as jnp
import numpy as np
from jax import lax
from jax.experimental import pallas as pl
from jax.experimental.pallas import tpu as pltpu
from jax.sharding import PartitionSpec as P

beta_one = 0.9
beta_two = 0.95
learn_rate = 0.001
adam_eps = 1e-08

C0 = math.sqrt(2.0 / math.pi)
C1 = C0 * 0.044715
MESH = pl.DeviceIdType.MESH
LANES = 128
WIDE = 256
PLANE = 4
BF = jnp.bfloat16
F32 = jnp.float32


def flip(index, mask):
    bit = 1
    while bit <= mask:
        if mask & bit:
            index = index + bit - 2 * bit * lax.rem(index // bit, 2)
        bit *= 2
    return index


def columns(row):
    return jnp.broadcast_to(row, (LANES, LANES)).T


def two_pieces(values):
    top = values.astype(BF).astype(F32)
    return top, values - top


def tail_rows(grad_b, grad_o):
    spot = lax.broadcasted_iota(jnp.int32, (16, grad_b.shape[1]), 0)
    top_b, rest_b = two_pieces(grad_b)
    top_o, rest_o = two_pieces(grad_o)
    tail = jnp.where(spot == 0, top_b, jnp.where(spot == 1, top_o, 0.0))
    tail = jnp.where(spot == 2, rest_b, jnp.where(spot == 3, rest_o, tail))
    return tail.astype(BF)


def step_kernel(
    n, cores, scale, parts_per_span,
    x_hbm, w_hbm, b_ref, wo_ref, qid_ref, rank_ref, gain_ref, disc_ref, counts, lengths,
    out_ref, doc_ref,
    x_buf, w_buf, w_low, wo_pair, pair_w, h_all, g_all, left,
    msg, arrive, s_row, l_row, tab_out, tab_in,
    parts, arr_xy, mid, arr_z, own,
    x_sem, w_sem, send_s, recv_s, send_l, recv_l,
    send_p, recv_p, send_m, recv_m, send_z, recv_z, send_n, recv_n, send_d, recv_d,
):
    me = lax.axis_index("dp")
    core = lax.axis_index("mp")
    side = lax.rem(core, 2)
    pair_core = core + 1 - 2 * side
    outer = n // PLANE
    plane, place = me // PLANE, lax.rem(me, PLANE)

    total_rows, features = x_hbm.shape
    groups = g_all.shape[0]
    step_rows = x_buf.shape[1]
    steps = total_rows // step_rows
    units, _, unit = qid_ref.shape
    step_units = step_rows // unit
    cap = total_rows // n
    unit_owners = unit // cap
    lists, list_width = gain_ref.shape
    per_list = list_width // LANES
    half_rows = lists * per_list // 2
    half_lists = lists // 2
    first_step = me // (step_units * unit_owners) + 1

    def remote(source, target, send, recv, peer, to_core):
        return pltpu.make_async_remote_copy(
            src_ref=source, dst_ref=target, send_sem=send, recv_sem=recv,
            device_id=(peer, to_core), device_id_type=MESH,
        )

    barrier = pltpu.get_barrier_semaphore()

    def x_fetch(s):
        at = lax.rem(first_step + s, steps) * step_rows
        slot = lax.rem(s, 2)
        return pltpu.make_async_copy(
            x_hbm.at[pl.ds(pl.multiple_of(at, step_rows), step_rows), :], x_buf.at[slot], x_sem.at[slot]
        )

    def w_fetch(k):
        return pltpu.make_async_copy(
            w_hbm.at[:, k * WIDE : (k + 1) * WIDE], w_buf.at[k % 2], w_sem.at[k % 2]
        )

    w_fetch(0).start()
    x_fetch(0).start()
    w_fetch(1).start()

    @pl.loop(1, n)
    def _(k):
        peer = lax.rem(me + k, n)
        for d in range(cores):
            pl.semaphore_signal(
                barrier, inc=1, device_id=(peer, lax.rem(core + d, cores)), device_id_type=MESH
            )

    for d in range(1, cores):
        pl.semaphore_signal(
            barrier, inc=1, device_id=(me, lax.rem(core + d, cores)), device_id_type=MESH
        )

    lane = lax.broadcasted_iota(jnp.int32, (LANES, LANES), 1)
    for k in range(groups * WIDE // LANES):
        at = k * LANES
        wo_row = 0.5 * wo_ref[at // WIDE, :, at % WIDE : at % WIDE + LANES]
        top, rest = two_pieces(columns(wo_row))
        wo_pair[at : at + LANES, :] = jnp.where(lane == 0, top, jnp.where(lane == 1, rest, 0.0)).astype(BF)
    for k in range(per_list):
        col = columns(disc_ref[:, k * LANES : (k + 1) * LANES])
        for m in range(per_list):
            cut = slice(m * LANES, (m + 1) * LANES)
            pair_w[k, :, cut] = jnp.abs(col - disc_ref[:, cut])
    for k in range(groups):
        w_fetch(k).wait()
        w_low[:, k * WIDE : (k + 1) * WIDE] = w_buf[k % 2].astype(BF)
        if k + 2 < groups:
            w_fetch(k + 2).start()

    unit_iota = lax.broadcasted_iota(jnp.int32, (1, unit), 1)
    low_iota = lax.broadcasted_iota(jnp.int32, (LANES, unit), 0)

    def unit_low(u):
        low = lax.rem(rank_ref[u], LANES)
        return (low == low_iota).astype(F32).astype(BF)

    def unit_high(u, o):
        owner = u * unit_owners + o
        live = (unit_iota >= o * cap) & (unit_iota < o * cap + counts[0, owner])
        high = (qid_ref[u] - owner * lists) * per_list + rank_ref[u] // LANES
        return jnp.where(live, high, -1)

    def score_copy(peer, c):
        return remote(
            msg.at[peer, c % 2], arrive.at[core, me], send_s.at[c, peer], recv_s.at[core, me], peer, c
        )

    def score_arrival(c, shard):
        return remote(
            msg.at[shard, 0], arrive.at[c, shard], send_s.at[0, shard], recv_s.at[c, shard], shard, c
        )

    hi_iota = lax.broadcasted_iota(jnp.int32, (2 * half_rows, unit), 0)

    @pl.loop(0, steps)
    def _(s):
        p = lax.rem(first_step + s, steps)
        slot = lax.rem(s, 2)

        @pl.when(s + 1 < steps)
        def _():
            x_fetch(s + 1).start()

        x_fetch(s).wait()
        at = pl.ds(pl.multiple_of(p * step_rows, step_rows), step_rows)
        x = x_buf[slot]
        left[:features, at] = x.T
        acc = jnp.zeros((step_rows, LANES), F32)
        for k in range(groups):
            cols = slice(k * WIDE, (k + 1) * WIDE)
            v = (jnp.dot(x, w_low[:, cols], preferred_element_type=F32) + b_ref[:, cols]).astype(BF)
            v2 = v * v
            t = jnp.tanh(v * (BF(C1) * v2 + BF(C0)))
            up = BF(1.0) + t
            h = v * up
            h_all[k, at, :] = h
            g_all[k, at, :] = up + (h * (BF(1.0) - t)) * (BF(3.0 * C1) * v2 + BF(C0))
            acc = acc + jnp.dot(h, wo_pair[cols, :], preferred_element_type=F32)
        values = jnp.sum(acc.T, axis=0, keepdims=True)
        for i in range(step_units):
            u = p * step_units + i
            low = unit_low(u)
            top, rest = two_pieces(values[:, i * unit : (i + 1) * unit])
            for o in range(unit_owners):
                hit = unit_high(u, o) == hi_iota
                spread = jnp.concatenate(
                    [jnp.where(hit, top, 0.0).astype(BF), jnp.where(hit, rest, 0.0).astype(BF)], axis=0
                )
                sums = lax.dot_general(
                    spread, low, (((1,), (1,)), ((), ())), preferred_element_type=F32
                )
                placed = sums[: 2 * half_rows] + sums[2 * half_rows :]
                msg[u * unit_owners + o, 0] = placed[:half_rows]
                msg[u * unit_owners + o, 1] = placed[half_rows:]

        @pl.when(s == 0)
        def _():
            pl.semaphore_wait(barrier, cores * n - 1)

        for i in range(step_units * unit_owners):
            owner = p * step_units * unit_owners + i
            for c in range(cores):
                @pl.when((owner != me) | (c != core))
                def _():
                    score_copy(owner, c).start()

    for d in range(1, cores):
        score_arrival(lax.rem(core + d, cores), me).wait_recv()
    arrive[core, me] = msg[me, side]

    total = arrive[0, me]
    for c in range(1, cores):
        total = total + arrive[c, me]

    def take(k, total):
        shard = lax.rem(me + k, n)
        for c in range(cores):
            score_arrival(c, shard).wait_recv()
        for c in range(cores):
            total = total + arrive[c, shard]
        return total

    s_row[...] = 0.5 * lax.fori_loop(1, n, take, total)
    lane_row = lax.broadcasted_iota(jnp.int32, (1, LANES), 1)

    @pl.loop(0, half_lists)
    def _(q):
        base = q * per_list
        length = lengths[side * half_lists + q]
        rows_s, rows_g = [], []
        gain = gain_ref[pl.ds(side * half_lists + q, 1), :]
        for k in range(per_list):
            keep = lane_row + k * LANES < length
            rows_s.append(jnp.where(keep, s_row[pl.ds(base + k, 1), :], -1e30))
            rows_g.append(jnp.where(keep, gain[:, k * LANES : (k + 1) * LANES], 0.0))
        row_s = jnp.concatenate(rows_s, axis=1)
        row_g = jnp.concatenate(rows_g, axis=1)
        sums = jnp.zeros((8, list_width), F32)
        for k in range(per_list):
            col_s = columns(rows_s[k])
            col_g = columns(rows_g[k])
            for r in range(0, LANES, 8):
                cs = jnp.concatenate([col_s[r : r + 8]] * per_list, axis=1)
                cg = jnp.concatenate([col_g[r : r + 8]] * per_list, axis=1)
                delta_g = cg - row_g
                delta_t = jnp.tanh(cs - row_s)
                sums = sums + pair_w[k, r : r + 8, :] * (delta_g - jnp.abs(delta_g) * delta_t)
        lam = 0.5 * jnp.sum(sums, axis=0, keepdims=True)
        for k in range(per_list):
            l_row[pl.ds(base + k, 1), :] = lam[:, k * LANES : (k + 1) * LANES]

    table = jnp.concatenate(two_pieces(l_row[...]), axis=0).astype(BF)
    tab_out[...] = table

    def lam_copy(peer, c, e):
        return remote(
            tab_out, tab_in.at[me, side], send_l.at[e, peer], recv_l.at[side, me], peer, c
        )

    def lam_arrival(half, peer):
        return remote(
            tab_out, tab_in.at[peer, half], send_l.at[0, peer], recv_l.at[half, peer], peer, core
        )

    lam_copy(me, pair_core, 1).start()

    @pl.loop(1, n)
    def _(k):
        peer = lax.rem(me + k, n)
        lam_copy(peer, core, 0).start()
        lam_copy(peer, pair_core, 1).start()

    tab_in[me, side] = table
    lam_arrival(1 - side, me).wait_recv()
    for half in range(2):
        pieces = tab_in[me, half].astype(F32)
        rows = pieces[:half_rows] + pieces[half_rows:]
        for q in range(half_lists):
            for k in range(per_list):
                doc_ref[half * half_lists + q : half * half_lists + q + 1, k * LANES : (k + 1) * LANES] = (
                    rows[q * per_list + k : q * per_list + k + 1]
                )

    spot = lax.broadcasted_iota(jnp.int32, (4 * half_rows, unit), 0)
    which = jnp.where(spot >= 2 * half_rows, spot - half_rows, spot)
    which = jnp.where((spot >= half_rows) & (spot < 2 * half_rows), spot - half_rows, which)
    which = jnp.where(spot >= 3 * half_rows, spot - 2 * half_rows, which)
    tail_spot = lax.broadcasted_iota(jnp.int32, (16, unit), 0)

    @pl.loop(0, units)
    def _(i):
        u = lax.rem(me // unit_owners + i, units)
        for o in range(unit_owners):
            owner = u * unit_owners + o

            @pl.when(owner != me)
            def _():
                for half in range(2):
                    lam_arrival(half, owner).wait_recv()

        low = unit_low(u)
        lam = jnp.zeros((1, unit), F32)
        for o in range(unit_owners):
            owner = u * unit_owners + o
            tables = jnp.concatenate([tab_in[owner, 0], tab_in[owner, 1]], axis=0)
            found = jnp.dot(tables, low, preferred_element_type=F32)
            hit = unit_high(u, o) == which
            lam = lam + jnp.sum(jnp.where(hit, found, 0.0), axis=0, keepdims=True)
        lam = lam * scale
        at = pl.ds(pl.multiple_of(u * unit, LANES), unit)
        left[:features, at] = (left[:features, at].astype(F32) * lam).astype(BF)
        top, rest = two_pieces(lam)
        left[features:, at] = jnp.where(
            tail_spot == 0, top, jnp.where(tail_spot == 1, rest, 0.0)
        ).astype(BF)

    chunk_rows = parts.shape[1]
    padded = chunk_rows * parts_per_span
    per_group = WIDE // LANES * parts_per_span
    round_groups = max(1, PLANE // per_group)
    round_planes = max(1, per_group // PLANE)
    rounds = groups // round_groups
    tail_part, tail_at = features // chunk_rows, features % chunk_rows

    def part_copy(owner):
        at, q = owner // PLANE, lax.rem(owner, PLANE)
        return remote(
            parts.at[owner], arr_xy.at[at, place], send_p.at[owner], recv_p.at[at, place],
            plane * PLANE + q, core,
        )

    def part_arrival(at, q):
        return remote(
            parts.at[at * PLANE + q], arr_xy.at[at, q], send_p.at[at * PLANE + q], recv_p.at[at, q],
            plane * PLANE + q, core,
        )

    def mid_copy(at):
        return remote(
            mid.at[at], arr_z.at[plane], send_m.at[at], recv_m.at[plane], at * PLANE + place, core
        )

    def mid_arrival(at):
        return remote(
            mid.at[at], arr_z.at[at], send_m.at[at], recv_m.at[at], at * PLANE + place, core
        )

    def tail_of(total):
        rows = total[tail_at : tail_at + 4]
        return tail_rows(rows[0:1] + rows[2:3], rows[1:2] + rows[3:4])

    def round_of(i):
        return lax.rem(plane // round_planes + 1 + i, rounds)

    def reduce_round(i):
        for j in range(round_planes):
            at = round_of(i) * round_planes + j
            total = parts[at * PLANE + place].astype(F32)
            for d in range(1, PLANE):
                q = lax.rem(place + d, PLANE)
                part_arrival(at, q).wait_recv()
                total = total + arr_xy[at, q].astype(F32)

            @pl.when(at == plane)
            def _():
                own[...] = total

            @pl.when(at != plane)
            def _():
                mid[at] = total.astype(BF)

                @pl.when(lax.rem(at * PLANE + place, parts_per_span) == tail_part)
                def _():
                    mid[at, tail_at : tail_at + 16, :] = tail_of(total)

                mid_copy(at).start()

    @pl.loop(0, rounds)
    def _(i):
        for gg in range(round_groups):
            group = round_of(i) * round_groups + gg
            half_wo = 0.5 * wo_ref[group]
            sums = jnp.dot(left[...], g_all[group], preferred_element_type=F32)
            sums_o = jnp.dot(left[features:, :], h_all[group], preferred_element_type=F32)
            grad_b = jnp.sum(sums[features:], axis=0, keepdims=True) * half_wo
            grad_o = 0.5 * jnp.sum(sums_o, axis=0, keepdims=True)
            pieces = [(sums[:features] * half_wo).astype(BF), tail_rows(grad_b, grad_o)]
            if padded > features + 16:
                pieces.append(jnp.zeros((padded - features - 16, WIDE), BF))
            block = jnp.concatenate(pieces, axis=0)
            for j in range(per_group):
                span, part = j // parts_per_span, j % parts_per_span
                parts[group * per_group + j] = block[
                    part * chunk_rows : (part + 1) * chunk_rows, span * LANES : (span + 1) * LANES
                ]
            for j in range(per_group):
                owner = group * per_group + j

                @pl.when(lax.rem(owner, PLANE) != place)
                def _():
                    part_copy(owner).start()

            if gg == 0:
                @pl.when(i > 0)
                def _():
                    reduce_round(i - 1)

    reduce_round(rounds - 1)

    total = own[...]
    for i in range(1, outer):
        at = flip(plane, i)
        mid_arrival(at).wait_recv()
        total = total + arr_z[at].astype(F32)
    out_ref[me] = total.astype(BF)

    @pl.when(lax.rem(me, parts_per_span) == tail_part)
    def _():
        out_ref[me, tail_at : tail_at + 16, :] = tail_of(total)

    cut = chunk_rows // 32 * 16
    near = [flip(place, 1), flip(place, 2)]
    halves = [pl.ds(0, cut), pl.ds(cut, chunk_rows - cut)]

    def across(i):
        return remote(
            out_ref.at[me], out_ref.at[me], send_z.at[i], recv_z.at[plane], flip(plane, i) * PLANE + place, core
        )

    def across_arrival(at):
        chunk = at * PLANE + place
        return remote(out_ref.at[chunk], out_ref.at[chunk], send_z.at[0], recv_z.at[at], chunk, core)

    def beside(at, w):
        chunk = at * PLANE + place
        return remote(
            out_ref.at[chunk], out_ref.at[chunk], send_n.at[w, at], recv_n.at[w, at],
            plane * PLANE + near[w], core,
        )

    def beside_arrival(at, w):
        chunk = at * PLANE + near[w]
        return remote(
            out_ref.at[chunk], out_ref.at[chunk], send_n.at[w, at], recv_n.at[w, at],
            plane * PLANE + near[w], core,
        )

    def passed(at, w):
        rows = out_ref.at[at * PLANE + near[w], halves[w]]
        return remote(
            rows, rows, send_d.at[w, at], recv_d.at[w, at], plane * PLANE + near[1 - w], core
        )

    def passed_arrival(at, w):
        rows = out_ref.at[at * PLANE + flip(place, 3), halves[w]]
        return remote(
            rows, rows, send_d.at[w, at], recv_d.at[w, at], plane * PLANE + near[1 - w], core
        )

    order = [flip(plane, i) for i in range(outer)]
    for i in range(1, outer):
        across(i).start()
    for i in range(outer + 1):
        if i < outer:
            if i > 0:
                across_arrival(order[i]).wait_recv()
            for w in range(2):
                beside(order[i], w).start()
        if i > 0:
            for w in range(2):
                beside_arrival(order[i - 1], w).wait_recv()
                passed(order[i - 1], w).start()
    for i in range(outer):
        for w in range(2):
            passed_arrival(order[i], w).wait_recv()

    for i in range(1, outer):
        across(i).wait_send()
    for i in range(outer):
        for w in range(2):
            beside(order[i], w).wait_send()
            passed(order[i], w).wait_send()

    @pl.loop(0, n)
    def _(owner):
        for c in range(cores):
            @pl.when((owner != me) | (c != core))
            def _():
                score_copy(owner, c).wait_send()

        @pl.when(owner != me)
        def _():
            lam_copy(owner, core, 0).wait_send()

        lam_copy(owner, pair_core, 1).wait_send()

        @pl.when(lax.rem(owner, PLANE) != place)
        def _():
            part_copy(owner).wait_send()

    @pl.loop(0, outer)
    def _(at):
        @pl.when(at != plane)
        def _():
            mid_copy(at).wait_send()


def gradients(n, cores, rows, weights, bias, wo, qid, rank, gains, disc, counts, lengths, parts_per_span, chunk_rows):
    total, features = rows.shape
    hidden = weights.shape[1]
    groups = hidden // WIDE
    lists, list_width = gains.shape
    per_list = list_width // LANES
    half_rows = lists * per_list // 2
    units, _, unit = qid.shape
    step_rows = 2 * unit if units % 2 == 0 else unit
    outer = n // PLANE
    vmem = pl.BlockSpec(memory_space=pltpu.VMEM)
    smem = pl.BlockSpec(memory_space=pltpu.SMEM)
    hbm = pl.BlockSpec(memory_space=pl.ANY)
    chunk = (chunk_rows, LANES)
    dma = pltpu.SemaphoreType.DMA
    return pl.pallas_call(
        functools.partial(step_kernel, n, cores, 1.0 / (lists * n), parts_per_span),
        in_specs=[hbm, hbm, vmem, vmem, vmem, vmem, vmem, vmem, smem, smem],
        out_specs=[vmem, vmem],
        out_shape=[
            jax.ShapeDtypeStruct((n,) + chunk, BF),
            jax.ShapeDtypeStruct((lists, list_width), F32),
        ],
        scratch_shapes=[
            pltpu.VMEM((2, step_rows, features), BF),
            pltpu.VMEM((2, features, WIDE), F32),
            pltpu.VMEM((features, hidden), BF),
            pltpu.VMEM((hidden, LANES), BF),
            pltpu.VMEM((per_list, LANES, list_width), F32),
            pltpu.VMEM((groups, total, WIDE), BF),
            pltpu.VMEM((groups, total, WIDE), BF),
            pltpu.VMEM((features + 16, total), BF),
            pltpu.VMEM((n, 2, half_rows, LANES), F32),
            pltpu.VMEM((cores, n, half_rows, LANES), F32),
            pltpu.VMEM((half_rows, LANES), F32),
            pltpu.VMEM((half_rows, LANES), F32),
            pltpu.VMEM((2 * half_rows, LANES), BF),
            pltpu.VMEM((n, 2, 2 * half_rows, LANES), BF),
            pltpu.VMEM((n,) + chunk, BF),
            pltpu.VMEM((outer, PLANE) + chunk, BF),
            pltpu.VMEM((outer,) + chunk, BF),
            pltpu.VMEM((outer,) + chunk, BF),
            pltpu.VMEM(chunk, F32),
            dma((2,)), dma((2,)),
            dma((cores, n)), dma((cores, n)), dma((2, n)), dma((2, n)),
            dma((n,)), dma((outer, PLANE)), dma((outer,)), dma((outer,)),
            dma((outer,)), dma((outer,)), dma((2, outer)), dma((2, outer)), dma((2, outer)), dma((2, outer)),
        ],
        compiler_params=pltpu.CompilerParams(
            collective_id=0, has_side_effects=True, vmem_limit_bytes=63 << 20
        ),
    )(rows, weights, bias, wo, qid, rank, gains, disc, counts, lengths)


def adam_step(weights, moment, second, gradient):
    moment_next = beta_one * moment + (1.0 - beta_one) * gradient
    second_next = beta_two * second + (1.0 - beta_two) * gradient * gradient
    weights_next = weights - learn_rate * moment_next / (jnp.sqrt(second_next) + adam_eps)
    return (weights_next, moment_next, second_next)


def adam_kernel(
    g_ref, d_ref, w_ref, mw_ref, sw_ref, b_ref, mb_ref, sb_ref, o_ref, mo_ref, so_ref,
    d_out, w_out, mw_out, sw_out, b_out, mb_out, sb_out, o_out, mo_out, so_out,
):
    features = w_ref.shape[0]

    @pl.when(pl.program_id(0) == 0)
    def _():
        d_out[...] = d_ref[...]

    for k in range(g_ref.shape[0]):
        cols = slice(k * LANES, (k + 1) * LANES)
        w_out[:, cols], mw_out[:, cols], sw_out[:, cols] = adam_step(
            w_ref[:, cols], mw_ref[:, cols], sw_ref[:, cols], g_ref[k, :features, :].astype(F32)
        )
        tail = g_ref[k, features : features + 16, :].astype(F32)
        b_out[:, cols], mb_out[:, cols], sb_out[:, cols] = adam_step(
            b_ref[:, cols], mb_ref[:, cols], sb_ref[:, cols], tail[0:1] + tail[2:3]
        )
        o_out[:, cols], mo_out[:, cols], so_out[:, cols] = adam_step(
            o_ref[:, cols], mo_ref[:, cols], so_ref[:, cols], tail[1:2] + tail[3:4]
        )


def adam(grads, doc, matrices, vectors):
    features, hidden = matrices[0].shape
    group = 4
    block = pl.BlockSpec((features, group * LANES), lambda i: (0, i))
    row = pl.BlockSpec((1, group * LANES), lambda i: (0, i))
    whole = pl.BlockSpec(doc.shape, lambda i: (0, 0))
    specs = [whole] + [block] * 3 + [row] * 6
    operands = [doc, *matrices, *(v.reshape(1, hidden) for v in vectors)]
    outs = pl.pallas_call(
        adam_kernel,
        grid=(hidden // (group * LANES),),
        in_specs=[pl.BlockSpec((group,) + grads.shape[1:], lambda i: (i, 0, 0))] + specs,
        out_specs=specs,
        out_shape=[jax.ShapeDtypeStruct(a.shape, F32) for a in operands],
    )(grads, *operands)
    return (*outs[:4], *(v.reshape(hidden) for v in outs[4:]))


def per_device(
    log_rows, query_ids, doc_ranks, row_counts, list_lengths, gains,
    weight_in, bias_in, weight_out, moment_w, second_w,
    moment_b, second_b, moment_o, second_o,
):
    n, cores = lax.axis_size("dp"), lax.axis_size("mp")
    total, features = log_rows.shape
    cap = total // n
    hidden = weight_in.shape[1]
    list_width = gains.shape[1]
    unit = math.lcm(cap, LANES)
    units = total // unit

    disc = (1.0 / np.log2(2.0 + np.arange(list_width))).astype(np.float32).reshape(1, list_width)
    spans = hidden // LANES
    row_parts = max(1, n // spans)
    whole_tile = 16 * row_parts
    padded = (features + 16 + whole_tile - 1) // whole_tile * whole_tile
    grads, doc = gradients(
        n, cores, log_rows, weight_in, bias_in.reshape(1, hidden), weight_out.reshape(hidden // WIDE, 1, WIDE),
        query_ids.reshape(units, 1, unit), doc_ranks.reshape(units, 1, unit),
        gains, jnp.asarray(disc), row_counts, list_lengths, row_parts, padded // row_parts,
    )
    return adam(
        grads.reshape(spans, padded, LANES), doc, (weight_in, moment_w, second_w),
        (bias_in, moment_b, second_b, weight_out, moment_o, second_o),
    )


def solution(mesh):
    dp, mp, both = P("dp"), P("mp"), P(None, "mp")
    rows = P("dp", None)
    return jax.shard_map(
        per_device,
        mesh=mesh,
        in_specs=(rows, dp, dp, rows, dp, rows, both, mp, mp, both, both, mp, mp, mp, mp),
        out_specs=(rows, both, both, both, mp, mp, mp, mp, mp, mp),
        check_vma=False,
    )
```

```python
import functools
import math

import jax
import jax.numpy as jnp
import numpy as np
from jax import lax
from jax.experimental import pallas as pl
from jax.experimental.pallas import tpu as pltpu
from jax.sharding import PartitionSpec as P

beta_one = 0.9
beta_two = 0.95
learn_rate = 0.001
adam_eps = 1e-08

C0 = math.sqrt(2.0 / math.pi)
C1 = C0 * 0.044715
MESH = pl.DeviceIdType.MESH
LANES = 128
WIDE = 256
PLANE = 4
BF = jnp.bfloat16
F32 = jnp.float32


def flip(index, mask):
    bit = 1
    while bit <= mask:
        if mask & bit:
            index = index + bit - 2 * bit * lax.rem(index // bit, 2)
        bit *= 2
    return index


def columns(row):
    return jnp.broadcast_to(row, (LANES, LANES)).T


def two_pieces(values):
    top = values.astype(BF).astype(F32)
    return top, values - top


def tail_rows(grad_b, grad_o):
    spot = lax.broadcasted_iota(jnp.int32, (16, grad_b.shape[1]), 0)
    top_b, rest_b = two_pieces(grad_b)
    top_o, rest_o = two_pieces(grad_o)
    tail = jnp.where(spot == 0, top_b, jnp.where(spot == 1, top_o, 0.0))
    tail = jnp.where(spot == 2, rest_b, jnp.where(spot == 3, rest_o, tail))
    return tail.astype(BF)


def step_kernel(
    n, cores, scale, parts_per_span,
    x_hbm, w_hbm, b_ref, wo_ref, qid_ref, rank_ref, gain_ref, disc_ref, counts, lengths,
    out_ref, doc_ref,
    x_buf, w_buf, w_low, wo_pair, pair_w, h_all, g_all, left,
    slot_out, slot_in, msg, arrive, s_row, l_row, doc_in, ans_out, ans_in,
    parts, arr_xy, mid, arr_z, own,
    x_sem, w_sem, send_i, recv_i, send_s, recv_s, doc_sem, send_l, recv_l,
    send_p, recv_p, send_m, recv_m, send_z, recv_z, send_n, recv_n, send_d, recv_d,
):
    me = lax.axis_index("dp")
    core = lax.axis_index("mp")
    side = lax.rem(core, 2)
    pair_core = core + 1 - 2 * side
    outer = n // PLANE
    plane, place = me // PLANE, lax.rem(me, PLANE)

    total_rows, features = x_hbm.shape
    groups = g_all.shape[0]
    step_rows = x_buf.shape[1]
    steps = total_rows // step_rows
    units, _, unit = qid_ref.shape
    step_units = step_rows // unit
    cap = total_rows // n
    unit_owners = unit // cap
    lists, list_width = gain_ref.shape
    per_list = list_width // LANES
    half_rows = lists * per_list // 2
    half_lists = lists // 2
    first_step = me // (step_units * unit_owners) + 1

    def remote(source, target, send, recv, peer, to_core):
        return pltpu.make_async_remote_copy(
            src_ref=source, dst_ref=target, send_sem=send, recv_sem=recv,
            device_id=(peer, to_core), device_id_type=MESH,
        )

    barrier = pltpu.get_barrier_semaphore()

    def x_fetch(s):
        at = lax.rem(first_step + s, steps) * step_rows
        slot = lax.rem(s, 2)
        return pltpu.make_async_copy(
            x_hbm.at[pl.ds(pl.multiple_of(at, step_rows), step_rows), :], x_buf.at[slot], x_sem.at[slot]
        )

    staging = [w_buf.at[0], w_buf.at[1], pair_w.at[:features], pair_w.at[features : 2 * features]]
    pieces = weight_pieces(groups)
    span = groups * WIDE // pieces

    def w_fetch(k):
        return pltpu.make_async_copy(
            w_hbm.at[:, k * span : (k + 1) * span], staging[k], w_sem.at[k]
        )

    for k in range(pieces):
        w_fetch(k).start()
    x_fetch(0).start()

    @pl.loop(1, n)
    def _(k):
        peer = lax.rem(me + k, n)
        for d in range(cores):
            pl.semaphore_signal(
                barrier, inc=1, device_id=(peer, lax.rem(core + d, cores)), device_id_type=MESH
            )

    for d in range(1, cores):
        pl.semaphore_signal(
            barrier, inc=1, device_id=(me, lax.rem(core + d, cores)), device_id_type=MESH
        )

    lane = lax.broadcasted_iota(jnp.int32, (LANES, LANES), 1)
    for k in range(groups * WIDE // LANES):
        at = k * LANES
        wo_row = 0.5 * wo_ref[at // WIDE, :, at % WIDE : at % WIDE + LANES]
        top, rest = two_pieces(columns(wo_row))
        wo_pair[at : at + LANES, :] = jnp.where(lane == 0, top, jnp.where(lane == 1, rest, 0.0)).astype(BF)
    for k in range(pieces):
        w_fetch(k).wait()
        w_low[:, k * span : (k + 1) * span] = staging[k][...].astype(BF)
    for k in range(per_list):
        col = columns(disc_ref[:, k * LANES : (k + 1) * LANES])
        for m in range(per_list):
            at = slice(m * LANES, (m + 1) * LANES)
            pair_w[k * LANES : (k + 1) * LANES, at] = jnp.abs(col - disc_ref[:, at])

    unit_iota = lax.broadcasted_iota(jnp.int32, (1, unit), 1)
    low_iota = lax.broadcasted_iota(jnp.int32, (LANES, unit), 0)

    @pl.loop(0, units)
    def _(u):
        for o in range(unit_owners):
            owner = u * unit_owners + o
            live = (unit_iota >= o * cap) & (unit_iota < o * cap + counts[0, owner])
            slot = (qid_ref[u] - owner * lists) * list_width + rank_ref[u]
            slot_out[owner] = jnp.where(live, slot, -1)

    slot_in[me] = slot_out[me]

    def low_of(slot):
        return ((slot & (LANES - 1)) == low_iota).astype(F32).astype(BF)

    def high_of(slot):
        return lax.shift_right_arithmetic(slot, LANES.bit_length() - 1)

    def slot_copy(peer):
        return remote(slot_out.at[peer], slot_in.at[me], send_i.at[peer], recv_i.at[me], peer, core)

    def slot_arrival(peer):
        return remote(slot_out.at[peer], slot_in.at[peer], send_i.at[peer], recv_i.at[peer], peer, core)

    def score_copy(peer, c):
        return remote(
            msg.at[peer, c % 2], arrive.at[core, me], send_s.at[c, peer], recv_s.at[core, me], peer, c
        )

    def score_arrival(c, shard):
        return remote(
            msg.at[shard, 0], arrive.at[c, shard], send_s.at[0, shard], recv_s.at[c, shard], shard, c
        )

    hi_iota = lax.broadcasted_iota(jnp.int32, (2 * half_rows, unit), 0)

    @pl.loop(0, steps)
    def _(s):
        p = lax.rem(first_step + s, steps)
        slot = lax.rem(s, 2)

        @pl.when(s + 1 < steps)
        def _():
            x_fetch(s + 1).start()

        x_fetch(s).wait()
        at = pl.ds(pl.multiple_of(p * step_rows, step_rows), step_rows)
        x = x_buf[slot]
        left[:features, at] = x.T
        acc = jnp.zeros((step_rows, LANES), F32)
        for k in range(groups):
            cols = slice(k * WIDE, (k + 1) * WIDE)
            v = (jnp.dot(x, w_low[:, cols], preferred_element_type=F32) + b_ref[:, cols]).astype(BF)
            v2 = v * v
            t = jnp.tanh(v * (BF(C1) * v2 + BF(C0)))
            up = BF(1.0) + t
            h = v * up
            h_all[k, at, :] = h
            g_all[k, at, :] = up + (h * (BF(1.0) - t)) * (BF(3.0 * C1) * v2 + BF(C0))
            acc = acc + jnp.dot(h, wo_pair[cols, :], preferred_element_type=F32)
        values = jnp.sum(acc.T, axis=0, keepdims=True)
        for i in range(step_units):
            top, rest = two_pieces(values[:, i * unit : (i + 1) * unit])
            for o in range(unit_owners):
                owner = (p * step_units + i) * unit_owners + o
                slot = slot_out[owner]
                hit = high_of(slot) == hi_iota
                spread = jnp.concatenate(
                    [jnp.where(hit, top, 0.0).astype(BF), jnp.where(hit, rest, 0.0).astype(BF)], axis=0
                )
                sums = lax.dot_general(
                    spread, low_of(slot), (((1,), (1,)), ((), ())), preferred_element_type=F32
                )
                placed = sums[: 2 * half_rows] + sums[2 * half_rows :]
                msg[owner, 0] = placed[:half_rows]
                msg[owner, 1] = placed[half_rows:]

        @pl.when(s == 0)
        def _():
            pl.semaphore_wait(barrier, cores * n - 1)

            @pl.loop(1, n)
            def _(k):
                slot_copy(lax.rem(me + k, n)).start()

        for i in range(step_units * unit_owners):
            owner = p * step_units * unit_owners + i
            for c in range(cores):
                @pl.when((owner != me) | (c != core))
                def _():
                    score_copy(owner, c).start()

    for d in range(1, cores):
        score_arrival(lax.rem(core + d, cores), me).wait_recv()
    arrive[core, me] = msg[me, side]

    total = arrive[0, me]
    for c in range(1, cores):
        total = total + arrive[c, me]

    def take(k, total):
        shard = lax.rem(me + k, n)
        for c in range(cores):
            score_arrival(c, shard).wait_recv()
        for c in range(cores):
            total = total + arrive[c, shard]
        return total

    s_row[...] = 0.5 * lax.fori_loop(1, n, take, total)
    lane_row = lax.broadcasted_iota(jnp.int32, (1, LANES), 1)

    @pl.loop(0, half_lists)
    def _(q):
        base = q * per_list
        length = lengths[side * half_lists + q]
        rows_s, rows_g = [], []
        gain = gain_ref[pl.ds(side * half_lists + q, 1), :]
        for k in range(per_list):
            keep = lane_row + k * LANES < length
            rows_s.append(jnp.where(keep, s_row[pl.ds(base + k, 1), :], -1e30))
            rows_g.append(jnp.where(keep, gain[:, k * LANES : (k + 1) * LANES], 0.0))
        row_s = jnp.concatenate(rows_s, axis=1)
        row_g = jnp.concatenate(rows_g, axis=1)
        sums = jnp.zeros((8, list_width), F32)
        for k in range(per_list):
            col_s = columns(rows_s[k])
            col_g = columns(rows_g[k])
            for r in range(0, LANES, 8):
                cs = jnp.concatenate([col_s[r : r + 8]] * per_list, axis=1)
                cg = jnp.concatenate([col_g[r : r + 8]] * per_list, axis=1)
                delta_g = cg - row_g
                delta_t = jnp.tanh(cs - row_s)
                sums = sums + pair_w[k * LANES + r : k * LANES + r + 8, :] * (delta_g - jnp.abs(delta_g) * delta_t)
        lam = 0.5 * jnp.sum(sums, axis=0, keepdims=True)
        for k in range(per_list):
            l_row[pl.ds(base + k, 1), :] = lam[:, k * LANES : (k + 1) * LANES]

    def doc_copy():
        return remote(l_row, doc_in, doc_sem.at[0], doc_sem.at[1], me, pair_core)

    doc_copy().start()
    table = jnp.concatenate(two_pieces(l_row[...] * scale), axis=0).astype(BF)
    spot = lax.broadcasted_iota(jnp.int32, (2 * half_rows, unit), 0)
    spot = jnp.where(spot >= half_rows, spot - half_rows, spot) + side * half_rows

    def lam_copy(peer, c, e):
        return remote(
            ans_out.at[peer], ans_in.at[side, me], send_l.at[e, peer], recv_l.at[side, me], peer, c
        )

    def lam_arrival(half, peer):
        return remote(
            ans_out.at[peer], ans_in.at[half, peer], send_l.at[0, peer], recv_l.at[half, peer], peer, core
        )

    def answer(shard):
        slot = slot_in[shard]
        found = jnp.dot(table, low_of(slot), preferred_element_type=F32)
        return jnp.sum(jnp.where(high_of(slot) == spot, found, 0.0), axis=0, keepdims=True)

    @pl.loop(0, (n - 1) // 3)
    def _(k):
        peers = [lax.rem(me + 1 + 3 * k + j, n) for j in range(3)]
        for peer in peers:
            slot_arrival(peer).wait_recv()
        replies = [answer(peer) for peer in peers]
        for peer, reply in zip(peers, replies):
            ans_out[peer] = reply
        for peer in peers:
            lam_copy(peer, core, 0).start()
            lam_copy(peer, pair_core, 1).start()

    ans_out[me] = answer(me)
    lam_copy(me, pair_core, 1).start()
    ans_in[side, me] = ans_out[me]
    lam_arrival(1 - side, me).wait_recv()
    doc_copy().wait_recv()
    mine_first = jnp.full((half_rows, LANES), side) == 0
    ordered = [
        jnp.where(mine_first, l_row[...], doc_in[...]), jnp.where(mine_first, doc_in[...], l_row[...])
    ]
    for half in range(2):
        for q in range(half_lists):
            for k in range(per_list):
                doc_ref[half * half_lists + q : half * half_lists + q + 1, k * LANES : (k + 1) * LANES] = (
                    ordered[half][q * per_list + k : q * per_list + k + 1]
                )

    tail_spot = lax.broadcasted_iota(jnp.int32, (16, unit), 0)

    @pl.loop(0, units)
    def _(i):
        u = lax.rem(me // unit_owners + i, units)
        lam = jnp.zeros((1, unit), F32)
        for o in range(unit_owners):
            owner = u * unit_owners + o

            @pl.when(owner != me)
            def _():
                for half in range(2):
                    lam_arrival(half, owner).wait_recv()

            lam = lam + (ans_in[0, owner] + ans_in[1, owner])
        at = pl.ds(pl.multiple_of(u * unit, LANES), unit)
        left[:features, at] = (left[:features, at].astype(F32) * lam).astype(BF)
        top, rest = two_pieces(lam)
        left[features:, at] = jnp.where(
            tail_spot == 0, top, jnp.where(tail_spot == 1, rest, 0.0)
        ).astype(BF)

    chunk_rows = parts.shape[1]
    padded = chunk_rows * parts_per_span
    per_group = WIDE // LANES * parts_per_span
    round_groups = max(1, PLANE // per_group)
    round_planes = max(1, per_group // PLANE)
    rounds = groups // round_groups
    tail_part, tail_at = features // chunk_rows, features % chunk_rows

    def part_copy(owner):
        at, q = owner // PLANE, lax.rem(owner, PLANE)
        return remote(
            parts.at[owner], arr_xy.at[at, place], send_p.at[owner], recv_p.at[at, place],
            plane * PLANE + q, core,
        )

    def part_arrival(at, q):
        return remote(
            parts.at[at * PLANE + q], arr_xy.at[at, q], send_p.at[at * PLANE + q], recv_p.at[at, q],
            plane * PLANE + q, core,
        )

    def mid_copy(at):
        return remote(
            mid.at[at], arr_z.at[plane], send_m.at[at], recv_m.at[plane], at * PLANE + place, core
        )

    def mid_arrival(at):
        return remote(
            mid.at[at], arr_z.at[at], send_m.at[at], recv_m.at[at], at * PLANE + place, core
        )

    def tail_of(total):
        rows = total[tail_at : tail_at + 4]
        return tail_rows(rows[0:1] + rows[2:3], rows[1:2] + rows[3:4])

    def round_of(i):
        return lax.rem(plane // round_planes + 1 + i, rounds)

    def reduce_round(i):
        for j in range(round_planes):
            at = round_of(i) * round_planes + j
            total = parts[at * PLANE + place].astype(F32)
            for d in range(1, PLANE):
                q = lax.rem(place + d, PLANE)
                part_arrival(at, q).wait_recv()
                total = total + arr_xy[at, q].astype(F32)

            @pl.when(at == plane)
            def _():
                own[...] = total

            @pl.when(at != plane)
            def _():
                mid[at] = total.astype(BF)

                @pl.when(lax.rem(at * PLANE + place, parts_per_span) == tail_part)
                def _():
                    mid[at, tail_at : tail_at + 16, :] = tail_of(total)

                mid_copy(at).start()

    @pl.loop(0, rounds)
    def _(i):
        for gg in range(round_groups):
            group = round_of(i) * round_groups + lax.rem(place // 2 + 1 + gg, round_groups)
            half_wo = 0.5 * wo_ref[group]
            sums = jnp.dot(left[...], g_all[group], preferred_element_type=F32)
            sums_o = jnp.dot(left[features:, :], h_all[group], preferred_element_type=F32)
            grad_b = jnp.sum(sums[features:], axis=0, keepdims=True) * half_wo
            grad_o = 0.5 * jnp.sum(sums_o, axis=0, keepdims=True)
            pieces = [(sums[:features] * half_wo).astype(BF), tail_rows(grad_b, grad_o)]
            if padded > features + 16:
                pieces.append(jnp.zeros((padded - features - 16, WIDE), BF))
            block = jnp.concatenate(pieces, axis=0)
            for j in range(per_group):
                span, part = j // parts_per_span, j % parts_per_span
                parts[group * per_group + j] = block[
                    part * chunk_rows : (part + 1) * chunk_rows, span * LANES : (span + 1) * LANES
                ]
            for j in range(per_group):
                owner = group * per_group + j

                @pl.when(lax.rem(owner, PLANE) != place)
                def _():
                    part_copy(owner).start()

        @pl.when(i > 0)
        def _():
            reduce_round(i - 1)

    reduce_round(rounds - 1)

    total = own[...]
    for i in range(1, outer):
        at = flip(plane, i)
        mid_arrival(at).wait_recv()
        total = total + arr_z[at].astype(F32)
    out_ref[me] = total.astype(BF)

    @pl.when(lax.rem(me, parts_per_span) == tail_part)
    def _():
        out_ref[me, tail_at : tail_at + 16, :] = tail_of(total)

    cut = chunk_rows // 32 * 16
    halves = [pl.ds(0, cut), pl.ds(cut, chunk_rows - cut)]
    near = [flip(place, 1), flip(place, 2)]

    def piece(at, q, h):
        return out_ref.at[at * PLANE + q, halves[h]]

    def along(at, h, d, to_plane):
        rows = piece(at, place, h)
        return remote(
            rows, rows, send_z.at[d, h, at], recv_z.at[h, at], to_plane * PLANE + place, core
        )

    def beside(at, h, w):
        rows = piece(at, place, h)
        return remote(
            rows, rows, send_n.at[w, h, at], recv_n.at[w, h, at], plane * PLANE + near[w], core
        )

    def beside_arrival(at, h, w):
        rows = piece(at, near[w], h)
        return remote(
            rows, rows, send_n.at[w, h, at], recv_n.at[w, h, at], plane * PLANE + near[w], core
        )

    def passed(at, w):
        rows = piece(at, near[w], w)
        return remote(
            rows, rows, send_d.at[w, at], recv_d.at[w, at], plane * PLANE + near[1 - w], core
        )

    def passed_arrival(at, w):
        rows = piece(at, flip(place, 3), w)
        return remote(
            rows, rows, send_d.at[w, at], recv_d.at[w, at], plane * PLANE + near[1 - w], core
        )

    def spread_own(h):
        for d, to in ((0, plane + 1), (1, plane - 1)):
            @pl.when((to >= 0) & (to < outer))
            def _():
                along(plane, h, d, to).start()
        for w in range(2):
            beside(plane, h, w).start()

    def spread_far(dist, h):
        for d, sign in ((0, 1), (1, -1)):
            at, to = plane - sign * dist, plane + sign

            @pl.when((at >= 0) & (at < outer))
            def _():
                along(at, h, d, plane).wait_recv()

                @pl.when((to >= 0) & (to < outer))
                def _():
                    along(at, h, d, to).start()

                for w in range(2):
                    beside(at, h, w).start()

    def at_distance(dist, do):
        for sign in (1, -1) if dist else (1,):
            at = plane - sign * dist

            @pl.when((at >= 0) & (at < outer))
            def _():
                do(at)

    def pass_on(at):
        for w in range(2):
            beside_arrival(at, w, w).wait_recv()
            passed(at, w).start()

    def finish(at):
        for w in range(2):
            beside_arrival(at, 1 - w, w).wait_recv()
            passed_arrival(at, w).wait_recv()

    for h in range(2):
        spread_own(h)
    for dist in range(1, outer):
        spread_far(dist, 0)
        at_distance(dist - 1, pass_on)
        spread_far(dist, 1)
    at_distance(outer - 1, pass_on)
    for dist in range(outer):
        at_distance(dist, finish)

    doc_copy().wait_send()

    @pl.loop(0, outer)
    def _(at):
        for h in range(2):
            for d, sign in ((0, 1), (1, -1)):
                to = plane + sign

                @pl.when((to >= 0) & (to < outer) & (sign * (plane - at) >= 0))
                def _():
                    along(at, h, d, to).wait_send()

            for w in range(2):
                beside(at, h, w).wait_send()
        for w in range(2):
            passed(at, w).wait_send()

    @pl.loop(0, n)
    def _(owner):
        for c in range(cores):
            @pl.when((owner != me) | (c != core))
            def _():
                score_copy(owner, c).wait_send()

        @pl.when(owner != me)
        def _():
            slot_copy(owner).wait_send()
            lam_copy(owner, core, 0).wait_send()

        lam_copy(owner, pair_core, 1).wait_send()

        @pl.when(lax.rem(owner, PLANE) != place)
        def _():
            part_copy(owner).wait_send()

    @pl.loop(0, outer)
    def _(at):
        @pl.when(at != plane)
        def _():
            mid_copy(at).wait_send()


def weight_pieces(groups):
    return min(4, groups)


def gradients(n, cores, rows, weights, bias, wo, qid, rank, gains, disc, counts, lengths, parts_per_span, chunk_rows):
    total, features = rows.shape
    hidden = weights.shape[1]
    groups = hidden // WIDE
    lists, list_width = gains.shape
    per_list = list_width // LANES
    half_rows = lists * per_list // 2
    units, _, unit = qid.shape
    step_rows = 2 * unit if units % 2 == 0 else unit
    outer = n // PLANE
    vmem = pl.BlockSpec(memory_space=pltpu.VMEM)
    smem = pl.BlockSpec(memory_space=pltpu.SMEM)
    hbm = pl.BlockSpec(memory_space=pl.ANY)
    chunk = (chunk_rows, LANES)
    dma = pltpu.SemaphoreType.DMA
    return pl.pallas_call(
        functools.partial(step_kernel, n, cores, 1.0 / (lists * n), parts_per_span),
        in_specs=[hbm, hbm, vmem, vmem, vmem, vmem, vmem, vmem, smem, smem],
        out_specs=[vmem, vmem],
        out_shape=[
            jax.ShapeDtypeStruct((n,) + chunk, BF),
            jax.ShapeDtypeStruct((lists, list_width), F32),
        ],
        scratch_shapes=[
            pltpu.VMEM((2, step_rows, features), BF),
            pltpu.VMEM((2, features, hidden // weight_pieces(groups)), F32),
            pltpu.VMEM((features, hidden), BF),
            pltpu.VMEM((hidden, LANES), BF),
            pltpu.VMEM((list_width, list_width), F32),
            pltpu.VMEM((groups, total, WIDE), BF),
            pltpu.VMEM((groups, total, WIDE), BF),
            pltpu.VMEM((features + 16, total), BF),
            pltpu.VMEM((n, 1, unit), jnp.int32),
            pltpu.VMEM((n, 1, unit), jnp.int32),
            pltpu.VMEM((n, 2, half_rows, LANES), F32),
            pltpu.VMEM((cores, n, half_rows, LANES), F32),
            pltpu.VMEM((half_rows, LANES), F32),
            pltpu.VMEM((half_rows, LANES), F32),
            pltpu.VMEM((half_rows, LANES), F32),
            pltpu.VMEM((n, 1, unit), F32),
            pltpu.VMEM((2, n, 1, unit), F32),
            pltpu.VMEM((n,) + chunk, BF),
            pltpu.VMEM((outer, PLANE) + chunk, BF),
            pltpu.VMEM((outer,) + chunk, BF),
            pltpu.VMEM((outer,) + chunk, BF),
            pltpu.VMEM(chunk, F32),
            dma((2,)), dma((4,)), dma((n,)), dma((n,)),
            dma((cores, n)), dma((cores, n)), dma((2,)), dma((2, n)), dma((2, n)),
            dma((n,)), dma((outer, PLANE)), dma((outer,)), dma((outer,)),
            dma((2, 2, outer)), dma((2, outer)), dma((2, 2, outer)), dma((2, 2, outer)), dma((2, outer)), dma((2, outer)),
        ],
        compiler_params=pltpu.CompilerParams(
            collective_id=0, has_side_effects=True, vmem_limit_bytes=63 << 20
        ),
    )(rows, weights, bias, wo, qid, rank, gains, disc, counts, lengths)


def adam_step(weights, moment, second, gradient):
    moment_next = beta_one * moment + (1.0 - beta_one) * gradient
    second_next = beta_two * second + (1.0 - beta_two) * gradient * gradient
    weights_next = weights - learn_rate * moment_next / (jnp.sqrt(second_next) + adam_eps)
    return (weights_next, moment_next, second_next)


def adam_kernel(
    g_ref, d_ref, w_ref, mw_ref, sw_ref, b_ref, mb_ref, sb_ref, o_ref, mo_ref, so_ref,
    d_out, w_out, mw_out, sw_out, b_out, mb_out, sb_out, o_out, mo_out, so_out,
):
    features = w_ref.shape[0]

    @pl.when(pl.program_id(0) == 0)
    def _():
        d_out[...] = d_ref[...]

    for k in range(g_ref.shape[0]):
        cols = slice(k * LANES, (k + 1) * LANES)
        w_out[:, cols], mw_out[:, cols], sw_out[:, cols] = adam_step(
            w_ref[:, cols], mw_ref[:, cols], sw_ref[:, cols], g_ref[k, :features, :].astype(F32)
        )
        tail = g_ref[k, features : features + 16, :].astype(F32)
        b_out[:, cols], mb_out[:, cols], sb_out[:, cols] = adam_step(
            b_ref[:, cols], mb_ref[:, cols], sb_ref[:, cols], tail[0:1] + tail[2:3]
        )
        o_out[:, cols], mo_out[:, cols], so_out[:, cols] = adam_step(
            o_ref[:, cols], mo_ref[:, cols], so_ref[:, cols], tail[1:2] + tail[3:4]
        )


def adam(grads, doc, matrices, vectors):
    features, hidden = matrices[0].shape
    group = 4
    block = pl.BlockSpec((features, group * LANES), lambda i: (0, i))
    row = pl.BlockSpec((1, group * LANES), lambda i: (0, i))
    whole = pl.BlockSpec(doc.shape, lambda i: (0, 0))
    specs = [whole] + [block] * 3 + [row] * 6
    operands = [doc, *matrices, *(v.reshape(1, hidden) for v in vectors)]
    outs = pl.pallas_call(
        adam_kernel,
        grid=(hidden // (group * LANES),),
        in_specs=[pl.BlockSpec((group,) + grads.shape[1:], lambda i: (i, 0, 0))] + specs,
        out_specs=specs,
        out_shape=[jax.ShapeDtypeStruct(a.shape, F32) for a in operands],
    )(grads, *operands)
    return (*outs[:4], *(v.reshape(hidden) for v in outs[4:]))


def per_device(
    log_rows, query_ids, doc_ranks, row_counts, list_lengths, gains,
    weight_in, bias_in, weight_out, moment_w, second_w,
    moment_b, second_b, moment_o, second_o,
):
    n, cores = lax.axis_size("dp"), lax.axis_size("mp")
    total, features = log_rows.shape
    cap = total // n
    hidden = weight_in.shape[1]
    list_width = gains.shape[1]
    unit = math.lcm(cap, LANES)
    units = total // unit

    disc = (1.0 / np.log2(2.0 + np.arange(list_width))).astype(np.float32).reshape(1, list_width)
    spans = hidden // LANES
    row_parts = max(1, n // spans)
    whole_tile = 16 * row_parts
    padded = (features + 16 + whole_tile - 1) // whole_tile * whole_tile
    grads, doc = gradients(
        n, cores, log_rows, weight_in, bias_in.reshape(1, hidden), weight_out.reshape(hidden // WIDE, 1, WIDE),
        query_ids.reshape(units, 1, unit), doc_ranks.reshape(units, 1, unit),
        gains, jnp.asarray(disc), row_counts, list_lengths, row_parts, padded // row_parts,
    )
    return adam(
        grads.reshape(spans, padded, LANES), doc, (weight_in, moment_w, second_w),
        (bias_in, moment_b, second_b, weight_out, moment_o, second_o),
    )


def solution(mesh):
    dp, mp, both = P("dp"), P("mp"), P(None, "mp")
    rows = P("dp", None)
    return jax.shard_map(
        per_device,
        mesh=mesh,
        in_specs=(rows, dp, dp, rows, dp, rows, both, mp, mp, both, both, mp, mp, mp, mp),
        out_specs=(rows, both, both, both, mp, mp, mp, mp, mp, mp),
        check_vma=False,
    )
```

```python
import functools
import math

import jax
import jax.numpy as jnp
import numpy as np
from jax import lax
from jax.experimental import pallas as pl
from jax.experimental.pallas import tpu as pltpu
from jax.sharding import PartitionSpec as P

beta_one = 0.9
beta_two = 0.95
learn_rate = 0.001
adam_eps = 1e-08

C0 = math.sqrt(2.0 / math.pi)
C1 = C0 * 0.044715
MESH = pl.DeviceIdType.MESH
LANES = 128
WIDE = 256
PLANE = 4
BF = jnp.bfloat16
F32 = jnp.float32


def flip(index, mask):
    bit = 1
    while bit <= mask:
        if mask & bit:
            index = index + bit - 2 * bit * lax.rem(index // bit, 2)
        bit *= 2
    return index


def columns(row):
    return jnp.broadcast_to(row, (LANES, LANES)).T


def two_pieces(values):
    top = values.astype(BF).astype(F32)
    return top, values - top


def tail_rows(grad_b, grad_o):
    spot = lax.broadcasted_iota(jnp.int32, (16, grad_b.shape[1]), 0)
    top_b, rest_b = two_pieces(grad_b)
    top_o, rest_o = two_pieces(grad_o)
    tail = jnp.where(spot == 0, top_b, jnp.where(spot == 1, top_o, 0.0))
    tail = jnp.where(spot == 2, rest_b, jnp.where(spot == 3, rest_o, tail))
    return tail.astype(BF)


def step_kernel(
    n, cores, scale, parts_per_span,
    x_hbm, w_hbm, b_ref, wo_ref, qid_ref, rank_ref, gain_ref, disc_ref, counts, lengths,
    out_ref, doc_ref,
    x_buf, w_buf, w_low, wo_pair, pair_w, h_all, g_all, left,
    slot_out, slot_in, msg, arrive, s_row, l_row, doc_in, ans_out, ans_in,
    parts, arr_xy, mid, arr_z, own,
    x_sem, w_sem, send_i, recv_i, send_s, recv_s, doc_sem, send_l, recv_l,
    send_p, recv_p, send_m, recv_m, send_z, recv_z, send_n, recv_n, send_d, recv_d,
):
    me = lax.axis_index("dp")
    core = lax.axis_index("mp")
    side = lax.rem(core, 2)
    pair_core = core + 1 - 2 * side
    outer = n // PLANE
    plane, place = me // PLANE, lax.rem(me, PLANE)

    total_rows, features = x_hbm.shape
    groups = g_all.shape[0]
    step_rows = x_buf.shape[1]
    steps = total_rows // step_rows
    units, _, unit = qid_ref.shape
    step_units = step_rows // unit
    cap = total_rows // n
    unit_owners = unit // cap
    lists, list_width = gain_ref.shape
    per_list = list_width // LANES
    half_rows = lists * per_list // 2
    half_lists = lists // 2
    first_step = me // (step_units * unit_owners) + 1

    def remote(source, target, send, recv, peer, to_core):
        return pltpu.make_async_remote_copy(
            src_ref=source, dst_ref=target, send_sem=send, recv_sem=recv,
            device_id=(peer, to_core), device_id_type=MESH,
        )

    barrier = pltpu.get_barrier_semaphore()

    def x_fetch(s):
        at = lax.rem(first_step + s, steps) * step_rows
        slot = lax.rem(s, 2)
        return pltpu.make_async_copy(
            x_hbm.at[pl.ds(pl.multiple_of(at, step_rows), step_rows), :], x_buf.at[slot], x_sem.at[slot]
        )

    staging = [w_buf.at[0], w_buf.at[1], pair_w.at[:features], pair_w.at[features : 2 * features]]
    pieces = weight_pieces(groups)
    span = groups * WIDE // pieces

    def w_fetch(k):
        return pltpu.make_async_copy(
            w_hbm.at[:, k * span : (k + 1) * span], staging[k], w_sem.at[k]
        )

    for k in range(pieces):
        w_fetch(k).start()
    x_fetch(0).start()

    @pl.loop(1, n)
    def _(k):
        peer = lax.rem(me + k, n)
        for d in range(cores):
            pl.semaphore_signal(
                barrier, inc=1, device_id=(peer, lax.rem(core + d, cores)), device_id_type=MESH
            )

    for d in range(1, cores):
        pl.semaphore_signal(
            barrier, inc=1, device_id=(me, lax.rem(core + d, cores)), device_id_type=MESH
        )

    lane = lax.broadcasted_iota(jnp.int32, (LANES, LANES), 1)
    for k in range(groups * WIDE // LANES):
        at = k * LANES
        wo_row = 0.5 * wo_ref[at // WIDE, :, at % WIDE : at % WIDE + LANES]
        top, rest = two_pieces(columns(wo_row))
        wo_pair[at : at + LANES, :] = jnp.where(lane == 0, top, jnp.where(lane == 1, rest, 0.0)).astype(BF)
    for k in range(pieces):
        w_fetch(k).wait()
        w_low[:, k * span : (k + 1) * span] = staging[k][...].astype(BF)
    for k in range(per_list):
        col = columns(disc_ref[:, k * LANES : (k + 1) * LANES])
        for m in range(per_list):
            at = slice(m * LANES, (m + 1) * LANES)
            pair_w[k * LANES : (k + 1) * LANES, at] = jnp.abs(col - disc_ref[:, at])

    unit_iota = lax.broadcasted_iota(jnp.int32, (1, unit), 1)
    low_iota = lax.broadcasted_iota(jnp.int32, (LANES, unit), 0)

    @pl.loop(0, units)
    def _(u):
        for o in range(unit_owners):
            owner = u * unit_owners + o
            live = (unit_iota >= o * cap) & (unit_iota < o * cap + counts[0, owner])
            slot = (qid_ref[u] - owner * lists) * list_width + rank_ref[u]
            slot_out[owner] = jnp.where(live, slot, -1)

    slot_in[me] = slot_out[me]

    def low_of(slot):
        return ((slot & (LANES - 1)) == low_iota).astype(F32).astype(BF)

    def high_of(slot):
        return lax.shift_right_arithmetic(slot, LANES.bit_length() - 1)

    def slot_copy(peer):
        return remote(slot_out.at[peer], slot_in.at[me], send_i, recv_i, peer, core)

    def all_slots():
        some = slot_in.at[pl.ds(0, n - 1)]
        return remote(some, some, send_i, recv_i, me, core)

    def score_copy(peer, c):
        return remote(msg.at[peer, c % 2], arrive.at[core * n + me], send_s, recv_s, peer, c)

    def all_scores():
        some = arrive.at[pl.ds(0, cores * n - 1)]
        return remote(some, some, send_s, recv_s, me, core)

    hi_iota = lax.broadcasted_iota(jnp.int32, (2 * half_rows, unit), 0)

    @pl.loop(0, steps)
    def _(s):
        p = lax.rem(first_step + s, steps)
        slot = lax.rem(s, 2)

        @pl.when(s + 1 < steps)
        def _():
            x_fetch(s + 1).start()

        x_fetch(s).wait()
        at = pl.ds(pl.multiple_of(p * step_rows, step_rows), step_rows)
        x = x_buf[slot]
        left[:features, at] = x.T
        acc = jnp.zeros((step_rows, LANES), F32)
        for k in range(groups):
            cols = slice(k * WIDE, (k + 1) * WIDE)
            v = (jnp.dot(x, w_low[:, cols], preferred_element_type=F32) + b_ref[:, cols]).astype(BF)
            v2 = v * v
            t = jnp.tanh(v * (BF(C1) * v2 + BF(C0)))
            up = BF(1.0) + t
            h = v * up
            h_all[k, at, :] = h
            g_all[k, at, :] = up + (h * (BF(1.0) - t)) * (BF(3.0 * C1) * v2 + BF(C0))
            acc = acc + jnp.dot(h, wo_pair[cols, :], preferred_element_type=F32)
        values = jnp.sum(acc.T, axis=0, keepdims=True)
        for i in range(step_units):
            top, rest = two_pieces(values[:, i * unit : (i + 1) * unit])
            for o in range(unit_owners):
                owner = (p * step_units + i) * unit_owners + o
                slot = slot_out[owner]
                hit = high_of(slot) == hi_iota
                spread = jnp.concatenate(
                    [jnp.where(hit, top, 0.0).astype(BF), jnp.where(hit, rest, 0.0).astype(BF)], axis=0
                )
                sums = lax.dot_general(
                    spread, low_of(slot), (((1,), (1,)), ((), ())), preferred_element_type=F32
                )
                placed = sums[: 2 * half_rows] + sums[2 * half_rows :]
                msg[owner, 0] = placed[:half_rows]
                msg[owner, 1] = placed[half_rows:]

        @pl.when(s == 0)
        def _():
            pl.semaphore_wait(barrier, cores * n - 1)

            @pl.loop(1, n)
            def _(k):
                slot_copy(lax.rem(me + k, n)).start()

        for i in range(step_units * unit_owners):
            owner = p * step_units * unit_owners + i
            for c in range(cores):
                @pl.when((owner != me) | (c != core))
                def _():
                    score_copy(owner, c).start()

    all_scores().wait_recv()
    arrive[core * n + me] = msg[me, side]
    s_row[...] = 0.5 * lax.fori_loop(
        1, cores * n, lambda k, total: total + arrive[k], arrive[0]
    )
    lane_row = lax.broadcasted_iota(jnp.int32, (1, LANES), 1)

    @pl.loop(0, half_lists)
    def _(q):
        base = q * per_list
        length = lengths[side * half_lists + q]
        rows_s, rows_g = [], []
        gain = gain_ref[pl.ds(side * half_lists + q, 1), :]
        for k in range(per_list):
            keep = lane_row + k * LANES < length
            rows_s.append(jnp.where(keep, s_row[pl.ds(base + k, 1), :], -1e30))
            rows_g.append(jnp.where(keep, gain[:, k * LANES : (k + 1) * LANES], 0.0))
        row_s = jnp.concatenate(rows_s, axis=1)
        row_g = jnp.concatenate(rows_g, axis=1)
        sums = jnp.zeros((8, list_width), F32)
        for k in range(per_list):
            col_s = columns(rows_s[k])
            col_g = columns(rows_g[k])
            for r in range(0, LANES, 8):
                cs = jnp.concatenate([col_s[r : r + 8]] * per_list, axis=1)
                cg = jnp.concatenate([col_g[r : r + 8]] * per_list, axis=1)
                delta_g = cg - row_g
                delta_t = jnp.tanh(cs - row_s)
                sums = sums + pair_w[k * LANES + r : k * LANES + r + 8, :] * (delta_g - jnp.abs(delta_g) * delta_t)
        lam = 0.5 * jnp.sum(sums, axis=0, keepdims=True)
        for k in range(per_list):
            l_row[pl.ds(base + k, 1), :] = lam[:, k * LANES : (k + 1) * LANES]

    def doc_copy():
        return remote(l_row, doc_in, doc_sem.at[0], doc_sem.at[1], me, pair_core)

    doc_copy().start()
    table = jnp.concatenate(two_pieces(l_row[...] * scale), axis=0).astype(BF)
    spot = lax.broadcasted_iota(jnp.int32, (2 * half_rows, unit), 0)
    spot = jnp.where(spot >= half_rows, spot - half_rows, spot) + side * half_rows

    def lam_copy(peer, c):
        return remote(ans_out.at[peer], ans_in.at[side * n + me], send_l, recv_l, peer, c)

    def all_lams():
        some = ans_in.at[pl.ds(0, 2 * n - 1)]
        return remote(some, some, send_l, recv_l, me, core)

    def answer(shard):
        slot = slot_in[shard]
        found = jnp.dot(table, low_of(slot), preferred_element_type=F32)
        return jnp.sum(jnp.where(high_of(slot) == spot, found, 0.0), axis=0, keepdims=True)

    all_slots().wait_recv()

    @pl.loop(0, (n - 1) // 3)
    def _(k):
        peers = [lax.rem(me + 1 + 3 * k + j, n) for j in range(3)]
        replies = [answer(peer) for peer in peers]
        for peer, reply in zip(peers, replies):
            ans_out[peer] = reply
        for peer in peers:
            lam_copy(peer, core).start()
            lam_copy(peer, pair_core).start()

    ans_out[me] = answer(me)
    lam_copy(me, pair_core).start()
    ans_in[side * n + me] = ans_out[me]
    doc_copy().wait_recv()
    mine_first = jnp.full((half_rows, LANES), side) == 0
    ordered = [
        jnp.where(mine_first, l_row[...], doc_in[...]), jnp.where(mine_first, doc_in[...], l_row[...])
    ]
    for half in range(2):
        for q in range(half_lists):
            for k in range(per_list):
                doc_ref[half * half_lists + q : half * half_lists + q + 1, k * LANES : (k + 1) * LANES] = (
                    ordered[half][q * per_list + k : q * per_list + k + 1]
                )

    tail_spot = lax.broadcasted_iota(jnp.int32, (16, unit), 0)

    all_lams().wait_recv()

    @pl.loop(0, units)
    def _(u):
        lam = jnp.zeros((1, unit), F32)
        for o in range(unit_owners):
            owner = u * unit_owners + o
            lam = lam + (ans_in[owner] + ans_in[n + owner])
        at = pl.ds(pl.multiple_of(u * unit, LANES), unit)
        left[:features, at] = (left[:features, at].astype(F32) * lam).astype(BF)
        top, rest = two_pieces(lam)
        left[features:, at] = jnp.where(
            tail_spot == 0, top, jnp.where(tail_spot == 1, rest, 0.0)
        ).astype(BF)

    chunk_rows = parts.shape[1]
    padded = chunk_rows * parts_per_span
    per_group = WIDE // LANES * parts_per_span
    round_groups = max(1, PLANE // per_group)
    round_planes = max(1, per_group // PLANE)
    rounds = groups // round_groups
    tail_part, tail_at = features // chunk_rows, features % chunk_rows

    def part_copy(owner):
        at, q = owner // PLANE, lax.rem(owner, PLANE)
        slot = lax.rem(place + PLANE - q, PLANE) - 1
        return remote(
            parts.at[owner], arr_xy.at[at, slot], send_p, recv_p.at[at], plane * PLANE + q, core
        )

    def part_arrivals(at):
        return remote(arr_xy.at[at], arr_xy.at[at], send_p, recv_p.at[at], me, core)

    def mid_copy(at):
        slot = lax.rem(plane + outer - at, outer) - 1
        return remote(mid.at[at], arr_z.at[slot], send_m, recv_m, at * PLANE + place, core)

    def all_mids():
        return remote(arr_z, arr_z, send_m, recv_m, me, core)

    def tail_of(total):
        rows = total[tail_at : tail_at + 4]
        return tail_rows(rows[0:1] + rows[2:3], rows[1:2] + rows[3:4])

    def round_of(i):
        return lax.rem(plane // round_planes + 1 + i, rounds)

    def reduce_round(i):
        for j in range(round_planes):
            at = round_of(i) * round_planes + j
            total = parts[at * PLANE + place].astype(F32)
            part_arrivals(at).wait_recv()
            for d in range(PLANE - 1):
                total = total + arr_xy[at, d].astype(F32)

            @pl.when(at == plane)
            def _():
                own[...] = total

            @pl.when(at != plane)
            def _():
                mid[at] = total.astype(BF)

                @pl.when(lax.rem(at * PLANE + place, parts_per_span) == tail_part)
                def _():
                    mid[at, tail_at : tail_at + 16, :] = tail_of(total)

                mid_copy(at).start()

    @pl.loop(0, rounds)
    def _(i):
        for gg in range(round_groups):
            group = round_of(i) * round_groups + lax.rem(place // 2 + 1 + gg, round_groups)
            half_wo = 0.5 * wo_ref[group]
            sums = jnp.dot(left[...], g_all[group], preferred_element_type=F32)
            sums_o = jnp.dot(left[features:, :], h_all[group], preferred_element_type=F32)
            grad_b = jnp.sum(sums[features:], axis=0, keepdims=True) * half_wo
            grad_o = 0.5 * jnp.sum(sums_o, axis=0, keepdims=True)
            pieces = [(sums[:features] * half_wo).astype(BF), tail_rows(grad_b, grad_o)]
            if padded > features + 16:
                pieces.append(jnp.zeros((padded - features - 16, WIDE), BF))
            block = jnp.concatenate(pieces, axis=0)
            for j in range(per_group):
                span, part = j // parts_per_span, j % parts_per_span
                parts[group * per_group + j] = block[
                    part * chunk_rows : (part + 1) * chunk_rows, span * LANES : (span + 1) * LANES
                ]
            for j in range(per_group):
                owner = group * per_group + j

                @pl.when(lax.rem(owner, PLANE) != place)
                def _():
                    part_copy(owner).start()

        @pl.when(i > 0)
        def _():
            reduce_round(i - 1)

    reduce_round(rounds - 1)

    total = own[...]
    all_mids().wait_recv()
    for i in range(outer - 1):
        total = total + arr_z[i].astype(F32)
    out_ref[me] = total.astype(BF)

    @pl.when(lax.rem(me, parts_per_span) == tail_part)
    def _():
        out_ref[me, tail_at : tail_at + 16, :] = tail_of(total)

    cut = chunk_rows // 32 * 16
    halves = [pl.ds(0, cut), pl.ds(cut, chunk_rows - cut)]
    near = [flip(place, 1), flip(place, 2)]

    def piece(at, q, h):
        return out_ref.at[at * PLANE + q, halves[h]]

    def along(at, h, d, to_plane):
        rows = piece(at, place, h)
        return remote(
            rows, rows, send_z.at[d, h, at], recv_z.at[h, at], to_plane * PLANE + place, core
        )

    def beside(at, h, w):
        rows = piece(at, place, h)
        return remote(
            rows, rows, send_n, recv_n.at[w, h, at], plane * PLANE + near[w], core
        )

    def beside_arrival(at, h, w):
        rows = piece(at, near[w], h)
        return remote(
            rows, rows, send_n, recv_n.at[w, h, at], plane * PLANE + near[w], core
        )

    def passed(at, w):
        rows = piece(at, near[w], w)
        return remote(
            rows, rows, send_d, recv_d, plane * PLANE + near[1 - w], core
        )

    def all_passed():
        some = out_ref.at[pl.ds(0, outer)]
        return remote(some, some, send_d, recv_d, me, core)

    def spread_own(h):
        for d, to in ((0, plane + 1), (1, plane - 1)):
            @pl.when((to >= 0) & (to < outer))
            def _():
                along(plane, h, d, to).start()
        for w in range(2):
            beside(plane, h, w).start()

    def spread_far(dist, h):
        for d, sign in ((0, 1), (1, -1)):
            at, to = plane - sign * dist, plane + sign

            @pl.when((at >= 0) & (at < outer))
            def _():
                along(at, h, d, plane).wait_recv()

                @pl.when((to >= 0) & (to < outer))
                def _():
                    along(at, h, d, to).start()

                for w in range(2):
                    beside(at, h, w).start()

    def at_distance(dist, do):
        for sign in (1, -1) if dist else (1,):
            at = plane - sign * dist

            @pl.when((at >= 0) & (at < outer))
            def _():
                do(at)

    def pass_on(at):
        for w in range(2):
            beside_arrival(at, w, w).wait_recv()
            passed(at, w).start()

    def finish(at):
        for w in range(2):
            beside_arrival(at, 1 - w, w).wait_recv()

    for h in range(2):
        spread_own(h)
    for dist in range(1, outer):
        spread_far(dist, 0)
        at_distance(dist - 1, pass_on)
        spread_far(dist, 1)
    at_distance(outer - 1, pass_on)
    for dist in range(outer):
        at_distance(dist, finish)
    all_passed().wait_recv()

    doc_copy().wait_send()
    all_slots().wait_send()
    all_scores().wait_send()
    all_lams().wait_send()
    all_mids().wait_send()
    some = parts.at[pl.ds(0, n - outer)]
    remote(some, some, send_p, recv_p.at[0], me, core).wait_send()
    some = out_ref.at[pl.ds(0, 2 * outer)]
    remote(some, some, send_n, recv_n.at[0, 0, 0], me, core).wait_send()
    all_passed().wait_send()

    @pl.loop(0, outer)
    def _(at):
        for h in range(2):
            for d, sign in ((0, 1), (1, -1)):
                to = plane + sign

                @pl.when((to >= 0) & (to < outer) & (sign * (plane - at) >= 0))
                def _():
                    along(at, h, d, to).wait_send()


def weight_pieces(groups):
    return min(4, groups)


def gradients(n, cores, rows, weights, bias, wo, qid, rank, gains, disc, counts, lengths, parts_per_span, chunk_rows):
    total, features = rows.shape
    hidden = weights.shape[1]
    groups = hidden // WIDE
    lists, list_width = gains.shape
    per_list = list_width // LANES
    half_rows = lists * per_list // 2
    units, _, unit = qid.shape
    step_rows = 2 * unit if units % 2 == 0 else unit
    outer = n // PLANE
    vmem = pl.BlockSpec(memory_space=pltpu.VMEM)
    smem = pl.BlockSpec(memory_space=pltpu.SMEM)
    hbm = pl.BlockSpec(memory_space=pl.ANY)
    chunk = (chunk_rows, LANES)
    dma = pltpu.SemaphoreType.DMA
    return pl.pallas_call(
        functools.partial(step_kernel, n, cores, 1.0 / (lists * n), parts_per_span),
        in_specs=[hbm, hbm, vmem, vmem, vmem, vmem, vmem, vmem, smem, smem],
        out_specs=[vmem, vmem],
        out_shape=[
            jax.ShapeDtypeStruct((n,) + chunk, BF),
            jax.ShapeDtypeStruct((lists, list_width), F32),
        ],
        scratch_shapes=[
            pltpu.VMEM((2, step_rows, features), BF),
            pltpu.VMEM((2, features, hidden // weight_pieces(groups)), F32),
            pltpu.VMEM((features, hidden), BF),
            pltpu.VMEM((hidden, LANES), BF),
            pltpu.VMEM((list_width, list_width), F32),
            pltpu.VMEM((groups, total, WIDE), BF),
            pltpu.VMEM((groups, total, WIDE), BF),
            pltpu.VMEM((features + 16, total), BF),
            pltpu.VMEM((n, 1, unit), jnp.int32),
            pltpu.VMEM((n, 1, unit), jnp.int32),
            pltpu.VMEM((n, 2, half_rows, LANES), F32),
            pltpu.VMEM((cores * n, half_rows, LANES), F32),
            pltpu.VMEM((half_rows, LANES), F32),
            pltpu.VMEM((half_rows, LANES), F32),
            pltpu.VMEM((half_rows, LANES), F32),
            pltpu.VMEM((n, 1, unit), F32),
            pltpu.VMEM((2 * n, 1, unit), F32),
            pltpu.VMEM((n,) + chunk, BF),
            pltpu.VMEM((outer, PLANE - 1) + chunk, BF),
            pltpu.VMEM((outer,) + chunk, BF),
            pltpu.VMEM((outer - 1,) + chunk, BF),
            pltpu.VMEM(chunk, F32),
            dma((2,)), dma((4,)), dma, dma,
            dma, dma, dma((2,)), dma, dma,
            dma, dma((outer,)), dma, dma,
            dma((2, 2, outer)), dma((2, outer)), dma, dma((2, 2, outer)), dma, dma,
        ],
        compiler_params=pltpu.CompilerParams(
            collective_id=0, has_side_effects=True, vmem_limit_bytes=63 << 20
        ),
    )(rows, weights, bias, wo, qid, rank, gains, disc, counts, lengths)


def adam_step(weights, moment, second, gradient):
    moment_next = beta_one * moment + (1.0 - beta_one) * gradient
    second_next = beta_two * second + (1.0 - beta_two) * gradient * gradient
    weights_next = weights - learn_rate * moment_next / (jnp.sqrt(second_next) + adam_eps)
    return (weights_next, moment_next, second_next)


def adam_kernel(steps, g_ref, doc_ref, *refs):
    ins, doc_out, outs, bufs, (in_sem, out_sem) = refs[:9], refs[9], refs[10:19], refs[19:28], refs[28:]
    features, hidden = bufs[0].shape
    rows = features // steps

    def matrix_copy(i, r, back):
        at = slice(r * rows, (r + 1) * rows)
        if back:
            return pltpu.make_async_copy(bufs[i].at[at], outs[i].at[at], out_sem.at[i, r])
        return pltpu.make_async_copy(ins[i].at[at], bufs[i].at[at], in_sem.at[i, r])

    def vector_copy(i, back):
        if back:
            return pltpu.make_async_copy(bufs[i], outs[i], out_sem.at[i, 0])
        return pltpu.make_async_copy(ins[i], bufs[i], in_sem.at[i, 0])

    doc_copy = pltpu.make_async_copy(doc_ref, doc_out, out_sem.at[9, 0])
    doc_copy.start()
    for r in range(steps):
        for i in range(3):
            matrix_copy(i, r, False).start()
        if r == 0:
            for i in range(3, 9):
                vector_copy(i, False).start()
    for r in range(steps):
        for i in range(3):
            matrix_copy(i, r, False).wait()
        at = slice(r * rows, (r + 1) * rows)
        for k in range(g_ref.shape[0]):
            cols = slice(k * LANES, (k + 1) * LANES)
            bufs[0][at, cols], bufs[1][at, cols], bufs[2][at, cols] = adam_step(
                bufs[0][at, cols], bufs[1][at, cols], bufs[2][at, cols], g_ref[k, at, :].astype(F32)
            )
        for i in range(3):
            matrix_copy(i, r, True).start()
        if r == 0:
            for i in range(3, 9):
                vector_copy(i, False).wait()
            for k in range(g_ref.shape[0]):
                cols = slice(k * LANES, (k + 1) * LANES)
                tail = g_ref[k, features : features + 16, :].astype(F32)
                for first in (3, 6):
                    row = (first - 3) // 3
                    a, b, c = bufs[first : first + 3]
                    a[:, cols], b[:, cols], c[:, cols] = adam_step(
                        a[:, cols], b[:, cols], c[:, cols], tail[row : row + 1] + tail[row + 2 : row + 3]
                    )
            for i in range(3, 9):
                vector_copy(i, True).start()
    doc_copy.wait()
    for i in range(9):
        if i < 3:
            for r in range(steps):
                matrix_copy(i, r, True).wait()
        else:
            vector_copy(i, True).wait()


def adam(grads, doc, matrices, vectors):
    hidden = matrices[0].shape[1]
    steps = 4
    vmem = pl.BlockSpec(memory_space=pltpu.VMEM)
    hbm = pl.BlockSpec(memory_space=pl.ANY)
    operands = [*matrices, *(v.reshape(1, hidden) for v in vectors)]
    outs = pl.pallas_call(
        functools.partial(adam_kernel, steps),
        in_specs=[vmem, vmem] + [hbm] * 9,
        out_specs=[hbm] * 10,
        out_shape=[jax.ShapeDtypeStruct(a.shape, F32) for a in [doc] + operands],
        scratch_shapes=[pltpu.VMEM(a.shape, F32) for a in operands]
        + [pltpu.SemaphoreType.DMA((9, steps)), pltpu.SemaphoreType.DMA((10, steps))],
        compiler_params=pltpu.CompilerParams(vmem_limit_bytes=60 << 20),
    )(grads, doc, *operands)
    return (*outs[:4], *(v.reshape(hidden) for v in outs[4:]))


def per_device(
    log_rows, query_ids, doc_ranks, row_counts, list_lengths, gains,
    weight_in, bias_in, weight_out, moment_w, second_w,
    moment_b, second_b, moment_o, second_o,
):
    n, cores = lax.axis_size("dp"), lax.axis_size("mp")
    total, features = log_rows.shape
    cap = total // n
    hidden = weight_in.shape[1]
    list_width = gains.shape[1]
    unit = math.lcm(cap, LANES)
    units = total // unit

    disc = (1.0 / np.log2(2.0 + np.arange(list_width))).astype(np.float32).reshape(1, list_width)
    spans = hidden // LANES
    row_parts = max(1, n // spans)
    whole_tile = 16 * row_parts
    padded = (features + 16 + whole_tile - 1) // whole_tile * whole_tile
    grads, doc = gradients(
        n, cores, log_rows, weight_in, bias_in.reshape(1, hidden), weight_out.reshape(hidden // WIDE, 1, WIDE),
        query_ids.reshape(units, 1, unit), doc_ranks.reshape(units, 1, unit),
        gains, jnp.asarray(disc), row_counts, list_lengths, row_parts, padded // row_parts,
    )
    return adam(
        grads.reshape(spans, padded, LANES), doc, (weight_in, moment_w, second_w),
        (bias_in, moment_b, second_b, weight_out, moment_o, second_o),
    )


def solution(mesh):
    dp, mp, both = P("dp"), P("mp"), P(None, "mp")
    rows = P("dp", None)
    return jax.shard_map(
        per_device,
        mesh=mesh,
        in_specs=(rows, dp, dp, rows, dp, rows, both, mp, mp, both, both, mp, mp, mp, mp),
        out_specs=(rows, both, both, both, mp, mp, mp, mp, mp, mp),
        check_vma=False,
    )
```

```python
import functools
import math

import jax
import jax.numpy as jnp
import numpy as np
from jax import lax
from jax.experimental import pallas as pl
from jax.experimental.pallas import tpu as pltpu
from jax.sharding import PartitionSpec as P

beta_one = 0.9
beta_two = 0.95
learn_rate = 0.001
adam_eps = 1e-08

C0 = math.sqrt(2.0 / math.pi)
C1 = C0 * 0.044715
MESH = pl.DeviceIdType.MESH
LANES = 128
WIDE = 256
PLANE = 4
BF = jnp.bfloat16
F32 = jnp.float32


def flip(index, mask):
    bit = 1
    while bit <= mask:
        if mask & bit:
            index = index + bit - 2 * bit * lax.rem(index // bit, 2)
        bit *= 2
    return index


def columns(row):
    return jnp.broadcast_to(row, (LANES, LANES)).T


def two_pieces(values):
    top = values.astype(BF).astype(F32)
    return top, values - top


def tail_rows(grad_b, grad_o):
    spot = lax.broadcasted_iota(jnp.int32, (16, grad_b.shape[1]), 0)
    top_b, rest_b = two_pieces(grad_b)
    top_o, rest_o = two_pieces(grad_o)
    tail = jnp.where(spot == 0, top_b, jnp.where(spot == 1, top_o, 0.0))
    tail = jnp.where(spot == 2, rest_b, jnp.where(spot == 3, rest_o, tail))
    return tail.astype(BF)


def step_kernel(
    n, cores, scale, parts_per_span,
    x_hbm, w_hbm, b_ref, wo_ref, qid_ref, rank_ref, gain_ref, disc_ref, counts, lengths,
    out_ref, doc_ref,
    x_buf, w_buf, w_low, wo_pair, pair_w, h_all, g_all, left,
    slot_out, slot_in, msg, arrive, s_row, l_row, doc_in, ans_out, ans_in,
    parts, arr_xy, mid, arr_z, own,
    x_sem, w_sem, send_i, recv_i, send_s, recv_s, doc_sem, send_l, recv_l,
    send_p, recv_p, send_m, recv_m, send_z, recv_z, send_n, recv_n, send_d, recv_d,
):
    me = lax.axis_index("dp")
    core = lax.axis_index("mp")
    side = lax.rem(core, 2)
    pair_core = core + 1 - 2 * side
    outer = n // PLANE
    plane, place = me // PLANE, lax.rem(me, PLANE)

    total_rows, features = x_hbm.shape
    groups = g_all.shape[0]
    step_rows = x_buf.shape[1]
    steps = total_rows // step_rows
    units, _, unit = qid_ref.shape
    step_units = step_rows // unit
    cap = total_rows // n
    unit_owners = unit // cap
    lists, list_width = gain_ref.shape
    per_list = list_width // LANES
    half_rows = lists * per_list // 2
    half_lists = lists // 2
    first_step = me // (step_units * unit_owners) + 1

    def remote(source, target, send, recv, peer, to_core):
        return pltpu.make_async_remote_copy(
            src_ref=source, dst_ref=target, send_sem=send, recv_sem=recv,
            device_id=(peer, to_core), device_id_type=MESH,
        )

    barrier = pltpu.get_barrier_semaphore()

    def x_fetch(s):
        at = lax.rem(first_step + s, steps) * step_rows
        slot = lax.rem(s, 2)
        return pltpu.make_async_copy(
            x_hbm.at[pl.ds(pl.multiple_of(at, step_rows), step_rows), :], x_buf.at[slot], x_sem.at[slot]
        )

    staging = [w_buf.at[0], w_buf.at[1], pair_w.at[:features], pair_w.at[features : 2 * features]]
    pieces = weight_pieces(groups)
    span = groups * WIDE // pieces

    def w_fetch(k):
        return pltpu.make_async_copy(
            w_hbm.at[:, k * span : (k + 1) * span], staging[k], w_sem.at[k]
        )

    for k in range(pieces):
        w_fetch(k).start()
    x_fetch(0).start()

    @pl.loop(1, n)
    def _(k):
        peer = lax.rem(me + k, n)
        for d in range(cores):
            pl.semaphore_signal(
                barrier, inc=1, device_id=(peer, lax.rem(core + d, cores)), device_id_type=MESH
            )

    for d in range(1, cores):
        pl.semaphore_signal(
            barrier, inc=1, device_id=(me, lax.rem(core + d, cores)), device_id_type=MESH
        )

    lane = lax.broadcasted_iota(jnp.int32, (LANES, LANES), 1)
    for k in range(groups * WIDE // LANES):
        at = k * LANES
        wo_row = 0.5 * wo_ref[at // WIDE, :, at % WIDE : at % WIDE + LANES]
        top, rest = two_pieces(columns(wo_row))
        wo_pair[at : at + LANES, :] = jnp.where(lane == 0, top, jnp.where(lane == 1, rest, 0.0)).astype(BF)
    for k in range(pieces):
        w_fetch(k).wait()
        w_low[:, k * span : (k + 1) * span] = staging[k][...].astype(BF)
    for k in range(per_list):
        col = columns(disc_ref[:, k * LANES : (k + 1) * LANES])
        for m in range(per_list):
            at = slice(m * LANES, (m + 1) * LANES)
            pair_w[k * LANES : (k + 1) * LANES, at] = jnp.abs(col - disc_ref[:, at])

    unit_iota = lax.broadcasted_iota(jnp.int32, (1, unit), 1)
    low_iota = lax.broadcasted_iota(jnp.int32, (LANES, unit), 0)

    @pl.loop(0, units)
    def _(u):
        for o in range(unit_owners):
            owner = u * unit_owners + o
            live = (unit_iota >= o * cap) & (unit_iota < o * cap + counts[0, owner])
            slot = (qid_ref[u] - owner * lists) * list_width + rank_ref[u]
            slot_out[owner] = jnp.where(live, slot, -1)

    slot_in[me] = slot_out[me]

    def low_of(slot):
        return ((slot & (LANES - 1)) == low_iota).astype(F32).astype(BF)

    def high_of(slot):
        return lax.shift_right_arithmetic(slot, LANES.bit_length() - 1)

    def slot_copy(peer):
        return remote(slot_out.at[peer], slot_in.at[me], send_i, recv_i, peer, core)

    def all_slots():
        some = slot_in.at[pl.ds(0, n - 1)]
        return remote(some, some, send_i, recv_i, me, core)

    def score_copy(peer, c):
        return remote(msg.at[peer, c % 2], arrive.at[core * n + me], send_s, recv_s, peer, c)

    def all_scores():
        some = arrive.at[pl.ds(0, cores * n - 1)]
        return remote(some, some, send_s, recv_s, me, core)

    hi_iota = lax.broadcasted_iota(jnp.int32, (2 * half_rows, unit), 0)

    @pl.loop(0, steps)
    def _(s):
        p = lax.rem(first_step + s, steps)
        slot = lax.rem(s, 2)

        @pl.when(s + 1 < steps)
        def _():
            x_fetch(s + 1).start()

        x_fetch(s).wait()
        at = pl.ds(pl.multiple_of(p * step_rows, step_rows), step_rows)
        x = x_buf[slot]
        left[:features, at] = x.T
        acc = jnp.zeros((step_rows, LANES), F32)
        for k in range(groups):
            cols = slice(k * WIDE, (k + 1) * WIDE)
            v = (jnp.dot(x, w_low[:, cols], preferred_element_type=F32) + b_ref[:, cols]).astype(BF)
            v2 = v * v
            t = jnp.tanh(v * (BF(C1) * v2 + BF(C0)))
            up = BF(1.0) + t
            h = v * up
            h_all[k, at, :] = h
            g_all[k, at, :] = up + (h * (BF(1.0) - t)) * (BF(3.0 * C1) * v2 + BF(C0))
            acc = acc + jnp.dot(h, wo_pair[cols, :], preferred_element_type=F32)
        values = jnp.sum(acc.T, axis=0, keepdims=True)
        for i in range(step_units):
            top, rest = two_pieces(values[:, i * unit : (i + 1) * unit])
            for o in range(unit_owners):
                owner = (p * step_units + i) * unit_owners + o
                slot = slot_out[owner]
                hit = high_of(slot) == hi_iota
                spread = jnp.concatenate(
                    [jnp.where(hit, top, 0.0).astype(BF), jnp.where(hit, rest, 0.0).astype(BF)], axis=0
                )
                sums = lax.dot_general(
                    spread, low_of(slot), (((1,), (1,)), ((), ())), preferred_element_type=F32
                )
                placed = sums[: 2 * half_rows] + sums[2 * half_rows :]
                msg[owner, 0] = placed[:half_rows]
                msg[owner, 1] = placed[half_rows:]

        @pl.when(s == 0)
        def _():
            pl.semaphore_wait(barrier, cores * n - 1)

            @pl.loop(1, n)
            def _(k):
                slot_copy(lax.rem(me + k, n)).start()

        for i in range(step_units * unit_owners):
            owner = p * step_units * unit_owners + i
            for c in range(cores):
                @pl.when((owner != me) | (c != core))
                def _():
                    score_copy(owner, c).start()

    all_scores().wait_recv()
    arrive[core * n + me] = msg[me, side]
    s_row[...] = 0.5 * lax.fori_loop(
        1, cores * n, lambda k, total: total + arrive[k], arrive[0]
    )
    lane_row = lax.broadcasted_iota(jnp.int32, (1, LANES), 1)

    @pl.loop(0, half_lists)
    def _(q):
        base = q * per_list
        length = lengths[side * half_lists + q]
        rows_s, rows_g = [], []
        gain = gain_ref[pl.ds(side * half_lists + q, 1), :]
        for k in range(per_list):
            keep = lane_row + k * LANES < length
            rows_s.append(jnp.where(keep, s_row[pl.ds(base + k, 1), :], -1e30))
            rows_g.append(jnp.where(keep, gain[:, k * LANES : (k + 1) * LANES], 0.0))
        row_s = jnp.concatenate(rows_s, axis=1)
        row_g = jnp.concatenate(rows_g, axis=1)
        sums = jnp.zeros((8, list_width), F32)
        for k in range(per_list):
            col_s = columns(rows_s[k])
            col_g = columns(rows_g[k])
            for r in range(0, LANES, 8):
                cs = jnp.concatenate([col_s[r : r + 8]] * per_list, axis=1)
                cg = jnp.concatenate([col_g[r : r + 8]] * per_list, axis=1)
                delta_g = cg - row_g
                delta_t = jnp.tanh(cs - row_s)
                sums = sums + pair_w[k * LANES + r : k * LANES + r + 8, :] * (delta_g - jnp.abs(delta_g) * delta_t)
        lam = 0.5 * jnp.sum(sums, axis=0, keepdims=True)
        for k in range(per_list):
            l_row[pl.ds(base + k, 1), :] = lam[:, k * LANES : (k + 1) * LANES]

    def doc_copy():
        return remote(l_row, doc_in, doc_sem.at[0], doc_sem.at[1], me, pair_core)

    doc_copy().start()
    table = jnp.concatenate(two_pieces(l_row[...] * scale), axis=0).astype(BF)
    spot = lax.broadcasted_iota(jnp.int32, (2 * half_rows, unit), 0)
    spot = jnp.where(spot >= half_rows, spot - half_rows, spot) + side * half_rows

    def lam_copy(peer, c):
        return remote(ans_out.at[peer], ans_in.at[side * n + me], send_l, recv_l, peer, c)

    def all_lams():
        some = ans_in.at[pl.ds(0, 2 * n - 1)]
        return remote(some, some, send_l, recv_l, me, core)

    def answer(shard):
        slot = slot_in[shard]
        found = jnp.dot(table, low_of(slot), preferred_element_type=F32)
        return jnp.sum(jnp.where(high_of(slot) == spot, found, 0.0), axis=0, keepdims=True)

    all_slots().wait_recv()

    @pl.loop(0, (n - 1) // 3)
    def _(k):
        peers = [lax.rem(me + 1 + 3 * k + j, n) for j in range(3)]
        replies = [answer(peer) for peer in peers]
        for peer, reply in zip(peers, replies):
            ans_out[peer] = reply
        for peer in peers:
            lam_copy(peer, core).start()
            lam_copy(peer, pair_core).start()

    ans_out[me] = answer(me)
    lam_copy(me, pair_core).start()
    ans_in[side * n + me] = ans_out[me]
    doc_copy().wait_recv()
    mine_first = jnp.full((half_rows, LANES), side) == 0
    ordered = [
        jnp.where(mine_first, l_row[...], doc_in[...]), jnp.where(mine_first, doc_in[...], l_row[...])
    ]
    for half in range(2):
        for q in range(half_lists):
            for k in range(per_list):
                doc_ref[half * half_lists + q : half * half_lists + q + 1, k * LANES : (k + 1) * LANES] = (
                    ordered[half][q * per_list + k : q * per_list + k + 1]
                )

    tail_spot = lax.broadcasted_iota(jnp.int32, (16, unit), 0)

    all_lams().wait_recv()

    @pl.loop(0, units)
    def _(u):
        lam = jnp.zeros((1, unit), F32)
        for o in range(unit_owners):
            owner = u * unit_owners + o
            lam = lam + (ans_in[owner] + ans_in[n + owner])
        at = pl.ds(pl.multiple_of(u * unit, LANES), unit)
        left[:features, at] = (left[:features, at].astype(F32) * lam).astype(BF)
        top, rest = two_pieces(lam)
        left[features:, at] = jnp.where(
            tail_spot == 0, top, jnp.where(tail_spot == 1, rest, 0.0)
        ).astype(BF)

    chunk_rows = parts.shape[1]
    padded = chunk_rows * parts_per_span
    per_group = WIDE // LANES * parts_per_span
    round_groups = max(1, PLANE // per_group)
    round_planes = max(1, per_group // PLANE)
    rounds = groups // round_groups
    tail_part, tail_at = features // chunk_rows, features % chunk_rows

    def part_copy(owner):
        at, q = owner // PLANE, lax.rem(owner, PLANE)
        slot = lax.rem(place + PLANE - q, PLANE) - 1
        return remote(
            parts.at[owner], arr_xy.at[at, slot], send_p, recv_p.at[at], plane * PLANE + q, core
        )

    def part_arrivals(at):
        return remote(arr_xy.at[at], arr_xy.at[at], send_p, recv_p.at[at], me, core)

    def mid_copy(at):
        slot = lax.rem(plane + outer - at, outer) - 1
        return remote(mid.at[at], arr_z.at[slot], send_m, recv_m, at * PLANE + place, core)

    def all_mids():
        return remote(arr_z, arr_z, send_m, recv_m, me, core)

    def tail_of(total):
        rows = total[tail_at : tail_at + 4]
        return tail_rows(rows[0:1] + rows[2:3], rows[1:2] + rows[3:4])

    def round_of(i):
        return lax.rem(plane // round_planes + 1 + i, rounds)

    def reduce_round(i):
        for j in range(round_planes):
            at = round_of(i) * round_planes + j
            total = parts[at * PLANE + place].astype(F32)
            part_arrivals(at).wait_recv()
            for d in range(PLANE - 1):
                total = total + arr_xy[at, d].astype(F32)

            @pl.when(at == plane)
            def _():
                own[...] = total

            @pl.when(at != plane)
            def _():
                mid[at] = total.astype(BF)

                @pl.when(lax.rem(at * PLANE + place, parts_per_span) == tail_part)
                def _():
                    mid[at, tail_at : tail_at + 16, :] = tail_of(total)

                mid_copy(at).start()

    @pl.loop(0, rounds)
    def _(i):
        for gg in range(round_groups):
            group = round_of(i) * round_groups + lax.rem(place // 2 + 1 + gg, round_groups)
            half_wo = 0.5 * wo_ref[group]
            sums = jnp.dot(left[...], g_all[group], preferred_element_type=F32)
            sums_o = jnp.dot(left[features:, :], h_all[group], preferred_element_type=F32)
            grad_b = jnp.sum(sums[features:], axis=0, keepdims=True) * half_wo
            grad_o = 0.5 * jnp.sum(sums_o, axis=0, keepdims=True)
            pieces = [(sums[:features] * half_wo).astype(BF), tail_rows(grad_b, grad_o)]
            if padded > features + 16:
                pieces.append(jnp.zeros((padded - features - 16, WIDE), BF))
            block = jnp.concatenate(pieces, axis=0)
            for j in range(per_group):
                span, part = j // parts_per_span, j % parts_per_span
                parts[group * per_group + j] = block[
                    part * chunk_rows : (part + 1) * chunk_rows, span * LANES : (span + 1) * LANES
                ]
            for j in range(per_group):
                owner = group * per_group + j

                @pl.when(lax.rem(owner, PLANE) != place)
                def _():
                    part_copy(owner).start()

        @pl.when(i > 0)
        def _():
            reduce_round(i - 1)

    reduce_round(rounds - 1)

    total = own[...]
    all_mids().wait_recv()
    for i in range(outer - 1):
        total = total + arr_z[i].astype(F32)
    out_ref[me] = total.astype(BF)

    @pl.when(lax.rem(me, parts_per_span) == tail_part)
    def _():
        out_ref[me, tail_at : tail_at + 16, :] = tail_of(total)

    cut = chunk_rows // 32 * 16
    halves = [pl.ds(0, cut), pl.ds(cut, chunk_rows - cut)]
    near = [flip(place, 1), flip(place, 2)]

    def piece(at, q, h):
        return out_ref.at[at * PLANE + q, halves[h]]

    def along(at, h, d, to_plane):
        rows = piece(at, place, h)
        return remote(
            rows, rows, send_z.at[d, h, at], recv_z.at[h, at], to_plane * PLANE + place, core
        )

    def beside(at, h, w):
        rows = piece(at, place, h)
        return remote(
            rows, rows, send_n, recv_n.at[w, h, at], plane * PLANE + near[w], core
        )

    def beside_arrival(at, h, w):
        rows = piece(at, near[w], h)
        return remote(
            rows, rows, send_n, recv_n.at[w, h, at], plane * PLANE + near[w], core
        )

    def passed(at, w):
        rows = piece(at, near[w], w)
        return remote(
            rows, rows, send_d, recv_d, plane * PLANE + near[1 - w], core
        )

    def all_passed():
        some = out_ref.at[pl.ds(0, outer)]
        return remote(some, some, send_d, recv_d, me, core)

    def spread_own(h):
        for d, to in ((0, plane + 1), (1, plane - 1)):
            @pl.when((to >= 0) & (to < outer))
            def _():
                along(plane, h, d, to).start()
        for w in range(2):
            beside(plane, h, w).start()

    def spread_far(dist, h):
        for d, sign in ((0, 1), (1, -1)):
            at, to = plane - sign * dist, plane + sign

            @pl.when((at >= 0) & (at < outer))
            def _():
                along(at, h, d, plane).wait_recv()

                @pl.when((to >= 0) & (to < outer))
                def _():
                    along(at, h, d, to).start()

                for w in range(2):
                    beside(at, h, w).start()

    def at_distance(dist, do):
        for sign in (1, -1) if dist else (1,):
            at = plane - sign * dist

            @pl.when((at >= 0) & (at < outer))
            def _():
                do(at)

    def pass_on(at):
        for w in range(2):
            beside_arrival(at, w, w).wait_recv()
            passed(at, w).start()

    def finish(at):
        for w in range(2):
            beside_arrival(at, 1 - w, w).wait_recv()

    for h in range(2):
        spread_own(h)
    for dist in range(1, outer):
        spread_far(dist, 0)
        at_distance(dist - 1, pass_on)
        spread_far(dist, 1)
    at_distance(outer - 1, pass_on)
    for dist in range(outer):
        at_distance(dist, finish)
    all_passed().wait_recv()

    doc_copy().wait_send()
    all_slots().wait_send()
    all_scores().wait_send()
    all_lams().wait_send()
    all_mids().wait_send()
    some = parts.at[pl.ds(0, n - outer)]
    remote(some, some, send_p, recv_p.at[0], me, core).wait_send()
    some = out_ref.at[pl.ds(0, 2 * outer)]
    remote(some, some, send_n, recv_n.at[0, 0, 0], me, core).wait_send()
    all_passed().wait_send()

    @pl.loop(0, outer)
    def _(at):
        for h in range(2):
            for d, sign in ((0, 1), (1, -1)):
                to = plane + sign

                @pl.when((to >= 0) & (to < outer) & (sign * (plane - at) >= 0))
                def _():
                    along(at, h, d, to).wait_send()


def weight_pieces(groups):
    return min(4, groups)


def gradients(n, cores, rows, weights, bias, wo, qid, rank, gains, disc, counts, lengths, parts_per_span, chunk_rows):
    total, features = rows.shape
    hidden = weights.shape[1]
    groups = hidden // WIDE
    lists, list_width = gains.shape
    per_list = list_width // LANES
    half_rows = lists * per_list // 2
    units, _, unit = qid.shape
    step_rows = 2 * unit if units % 2 == 0 else unit
    outer = n // PLANE
    vmem = pl.BlockSpec(memory_space=pltpu.VMEM)
    smem = pl.BlockSpec(memory_space=pltpu.SMEM)
    hbm = pl.BlockSpec(memory_space=pl.ANY)
    chunk = (chunk_rows, LANES)
    dma = pltpu.SemaphoreType.DMA
    return pl.pallas_call(
        functools.partial(step_kernel, n, cores, 1.0 / (lists * n), parts_per_span),
        in_specs=[hbm, hbm, vmem, vmem, vmem, vmem, vmem, vmem, smem, smem],
        out_specs=[vmem, vmem],
        out_shape=[
            jax.ShapeDtypeStruct((n,) + chunk, BF),
            jax.ShapeDtypeStruct((lists, list_width), F32),
        ],
        scratch_shapes=[
            pltpu.VMEM((2, step_rows, features), BF),
            pltpu.VMEM((2, features, hidden // weight_pieces(groups)), F32),
            pltpu.VMEM((features, hidden), BF),
            pltpu.VMEM((hidden, LANES), BF),
            pltpu.VMEM((list_width, list_width), F32),
            pltpu.VMEM((groups, total, WIDE), BF),
            pltpu.VMEM((groups, total, WIDE), BF),
            pltpu.VMEM((features + 16, total), BF),
            pltpu.VMEM((n, 1, unit), jnp.int32),
            pltpu.VMEM((n, 1, unit), jnp.int32),
            pltpu.VMEM((n, 2, half_rows, LANES), F32),
            pltpu.VMEM((cores * n, half_rows, LANES), F32),
            pltpu.VMEM((half_rows, LANES), F32),
            pltpu.VMEM((half_rows, LANES), F32),
            pltpu.VMEM((half_rows, LANES), F32),
            pltpu.VMEM((n, 1, unit), F32),
            pltpu.VMEM((2 * n, 1, unit), F32),
            pltpu.VMEM((n,) + chunk, BF),
            pltpu.VMEM((outer, PLANE - 1) + chunk, BF),
            pltpu.VMEM((outer,) + chunk, BF),
            pltpu.VMEM((outer - 1,) + chunk, BF),
            pltpu.VMEM(chunk, F32),
            dma((2,)), dma((4,)), dma, dma,
            dma, dma, dma((2,)), dma, dma,
            dma, dma((outer,)), dma, dma,
            dma((2, 2, outer)), dma((2, outer)), dma, dma((2, 2, outer)), dma, dma,
        ],
        compiler_params=pltpu.CompilerParams(
            collective_id=0, has_side_effects=True, vmem_limit_bytes=63 << 20
        ),
    )(rows, weights, bias, wo, qid, rank, gains, disc, counts, lengths)


def adam_step(weights, moment, second, gradient):
    moment_next = beta_one * moment + (1.0 - beta_one) * gradient
    second_next = beta_two * second + (1.0 - beta_two) * gradient * gradient
    weights_next = weights - learn_rate * moment_next / (jnp.sqrt(second_next) + adam_eps)
    return (weights_next, moment_next, second_next)


def adam_kernel(steps, wide, g_ref, doc_ref, *refs):
    ins, doc_out, outs = refs[:9], refs[9], refs[10:19]
    matrix, vector, in_sem, vector_sem, out_sem, back_sem, doc_sem = refs[19:]
    features, hidden = matrix.shape[1:]
    rows = features // steps
    parts = [slice(r * rows, (r + 1) * rows) for r in range(steps)]

    def whole(ref, sem):
        return pltpu.make_async_copy(ref, ref, sem)

    doc_copy = pltpu.make_async_copy(doc_ref, doc_out, doc_sem)
    for r, at in enumerate(parts):
        for i in range(3):
            pltpu.make_async_copy(ins[i].at[at], matrix.at[i, at], in_sem.at[r]).start()
        if r == 0:
            for i in range(6):
                pltpu.make_async_copy(ins[3 + i], vector.at[i], vector_sem).start()
    doc_copy.start()
    for r, at in enumerate(parts):
        whole(matrix.at[:, at], in_sem.at[r]).wait()
        for k in range(0, g_ref.shape[0], wide):
            cols = slice(k * LANES, (k + wide) * LANES)
            grad = jnp.concatenate([g_ref[k + j, at, :] for j in range(wide)], axis=1).astype(F32)
            matrix[0, at, cols], matrix[1, at, cols], matrix[2, at, cols] = adam_step(
                matrix[0, at, cols], matrix[1, at, cols], matrix[2, at, cols], grad
            )
        for i in range(3):
            pltpu.make_async_copy(matrix.at[i, at], outs[i].at[at], out_sem).start()
        if r == 0:
            whole(vector, vector_sem).wait()
            for first, row in ((0, 0), (3, 1)):
                grad = jnp.concatenate(
                    [
                        g_ref[k, features : features + 16, :].astype(F32)[row : row + 1]
                        + g_ref[k, features : features + 16, :].astype(F32)[row + 2 : row + 3]
                        for k in range(g_ref.shape[0])
                    ],
                    axis=1,
                )
                vector[first], vector[first + 1], vector[first + 2] = adam_step(
                    vector[first], vector[first + 1], vector[first + 2], grad
                )
            for i in range(6):
                pltpu.make_async_copy(vector.at[i], outs[3 + i], back_sem).start()
    doc_copy.wait()
    whole(vector, back_sem).wait()
    whole(matrix, out_sem).wait()


def adam(grads, doc, matrices, vectors):
    features, hidden = matrices[0].shape
    steps = 4
    vmem = pl.BlockSpec(memory_space=pltpu.VMEM)
    hbm = pl.BlockSpec(memory_space=pl.ANY)
    dma = pltpu.SemaphoreType.DMA
    operands = [*matrices, *(v.reshape(1, hidden) for v in vectors)]
    outs = pl.pallas_call(
        functools.partial(adam_kernel, steps, 4),
        in_specs=[vmem, vmem] + [hbm] * 9,
        out_specs=[hbm] * 10,
        out_shape=[jax.ShapeDtypeStruct(a.shape, F32) for a in [doc] + operands],
        scratch_shapes=[
            pltpu.VMEM((3, features, hidden), F32), pltpu.VMEM((6, 1, hidden), F32),
            dma((steps,)), dma, dma, dma, dma,
        ],
        compiler_params=pltpu.CompilerParams(vmem_limit_bytes=60 << 20),
    )(grads, doc, *operands)
    return (*outs[:4], *(v.reshape(hidden) for v in outs[4:]))


def per_device(
    log_rows, query_ids, doc_ranks, row_counts, list_lengths, gains,
    weight_in, bias_in, weight_out, moment_w, second_w,
    moment_b, second_b, moment_o, second_o,
):
    n, cores = lax.axis_size("dp"), lax.axis_size("mp")
    total, features = log_rows.shape
    cap = total // n
    hidden = weight_in.shape[1]
    list_width = gains.shape[1]
    unit = math.lcm(cap, LANES)
    units = total // unit

    disc = (1.0 / np.log2(2.0 + np.arange(list_width))).astype(np.float32).reshape(1, list_width)
    spans = hidden // LANES
    row_parts = max(1, n // spans)
    whole_tile = 16 * row_parts
    padded = (features + 16 + whole_tile - 1) // whole_tile * whole_tile
    grads, doc = gradients(
        n, cores, log_rows, weight_in, bias_in.reshape(1, hidden), weight_out.reshape(hidden // WIDE, 1, WIDE),
        query_ids.reshape(units, 1, unit), doc_ranks.reshape(units, 1, unit),
        gains, jnp.asarray(disc), row_counts, list_lengths, row_parts, padded // row_parts,
    )
    return adam(
        grads.reshape(spans, padded, LANES), doc, (weight_in, moment_w, second_w),
        (bias_in, moment_b, second_b, weight_out, moment_o, second_o),
    )


def solution(mesh):
    dp, mp, both = P("dp"), P("mp"), P(None, "mp")
    rows = P("dp", None)
    return jax.shard_map(
        per_device,
        mesh=mesh,
        in_specs=(rows, dp, dp, rows, dp, rows, both, mp, mp, both, both, mp, mp, mp, mp),
        out_specs=(rows, both, both, both, mp, mp, mp, mp, mp, mp),
        check_vma=False,
    )
```

```python
import functools
import math

import jax
import jax.numpy as jnp
import numpy as np
from jax import lax
from jax.experimental import pallas as pl
from jax.experimental.pallas import tpu as pltpu
from jax.sharding import PartitionSpec as P

beta_one = 0.9
beta_two = 0.95
learn_rate = 0.001
adam_eps = 1e-08

C0 = math.sqrt(2.0 / math.pi)
C1 = C0 * 0.044715
MESH = pl.DeviceIdType.MESH
LANES = 128
WIDE = 256
PLANE = 4
BF = jnp.bfloat16
F32 = jnp.float32


def flip(index, mask):
    bit = 1
    while bit <= mask:
        if mask & bit:
            index = index + bit - 2 * bit * lax.rem(index // bit, 2)
        bit *= 2
    return index


def columns(row):
    return jnp.broadcast_to(row, (LANES, LANES)).T


def two_pieces(values):
    top = values.astype(BF).astype(F32)
    return top, values - top


def tail_rows(grad_b, grad_o):
    spot = lax.broadcasted_iota(jnp.int32, (16, grad_b.shape[1]), 0)
    top_b, rest_b = two_pieces(grad_b)
    top_o, rest_o = two_pieces(grad_o)
    tail = jnp.where(spot == 0, top_b, jnp.where(spot == 1, top_o, 0.0))
    tail = jnp.where(spot == 2, rest_b, jnp.where(spot == 3, rest_o, tail))
    return tail.astype(BF)


def step_kernel(
    n, cores, scale, parts_per_span,
    x_hbm, w_hbm, b_ref, wo_ref, qid_ref, rank_ref, gain_ref, disc_ref, counts, lengths,
    out_ref, doc_ref,
    x_buf, w_buf, w_low, wo_pair, pair_w, h_all, g_all, left,
    slot_out, slot_in, msg, arrive, s_row, l_row, doc_in, ans_out, ans_in,
    parts, arr_xy, mid, arr_z, own,
    x_sem, w_sem, send_i, recv_i, send_s, recv_s, doc_sem, send_l, recv_l,
    send_p, recv_p, send_m, recv_m, send_z, recv_z, send_n, recv_n, send_d, recv_d,
):
    me = lax.axis_index("dp")
    core = lax.axis_index("mp")
    side = lax.rem(core, 2)
    pair_core = core + 1 - 2 * side
    outer = n // PLANE
    plane, place = me // PLANE, lax.rem(me, PLANE)

    total_rows, features = x_hbm.shape
    groups = g_all.shape[0]
    step_rows = x_buf.shape[1]
    steps = total_rows // step_rows
    units, _, unit = qid_ref.shape
    step_units = step_rows // unit
    cap = total_rows // n
    unit_owners = unit // cap
    lists, list_width = gain_ref.shape
    per_list = list_width // LANES
    half_rows = lists * per_list // 2
    half_lists = lists // 2
    first_step = me // (step_units * unit_owners) + 1

    def remote(source, target, send, recv, peer, to_core):
        return pltpu.make_async_remote_copy(
            src_ref=source, dst_ref=target, send_sem=send, recv_sem=recv,
            device_id=(peer, to_core), device_id_type=MESH,
        )

    barrier = pltpu.get_barrier_semaphore()

    def x_fetch(s):
        at = lax.rem(first_step + s, steps) * step_rows
        slot = lax.rem(s, 2)
        return pltpu.make_async_copy(
            x_hbm.at[pl.ds(pl.multiple_of(at, step_rows), step_rows), :], x_buf.at[slot], x_sem.at[slot]
        )

    staging = [w_buf.at[0], w_buf.at[1], pair_w.at[:features], pair_w.at[features : 2 * features]]
    pieces = weight_pieces(groups)
    span = groups * WIDE // pieces

    def w_fetch(k):
        return pltpu.make_async_copy(
            w_hbm.at[:, k * span : (k + 1) * span], staging[k], w_sem.at[k]
        )

    for k in range(pieces):
        w_fetch(k).start()
    x_fetch(0).start()

    @pl.loop(1, n)
    def _(k):
        peer = lax.rem(me + k, n)
        for d in range(cores):
            pl.semaphore_signal(
                barrier, inc=1, device_id=(peer, lax.rem(core + d, cores)), device_id_type=MESH
            )

    for d in range(1, cores):
        pl.semaphore_signal(
            barrier, inc=1, device_id=(me, lax.rem(core + d, cores)), device_id_type=MESH
        )

    lane = lax.broadcasted_iota(jnp.int32, (LANES, LANES), 1)
    for k in range(groups * WIDE // LANES):
        at = k * LANES
        wo_row = 0.5 * wo_ref[at // WIDE, :, at % WIDE : at % WIDE + LANES]
        top, rest = two_pieces(columns(wo_row))
        wo_pair[at : at + LANES, :] = jnp.where(lane == 0, top, jnp.where(lane == 1, rest, 0.0)).astype(BF)
    for k in range(pieces):
        w_fetch(k).wait()
        w_low[:, k * span : (k + 1) * span] = staging[k][...].astype(BF)
    for k in range(per_list):
        col = columns(disc_ref[:, k * LANES : (k + 1) * LANES])
        for m in range(per_list):
            at = slice(m * LANES, (m + 1) * LANES)
            pair_w[k * LANES : (k + 1) * LANES, at] = jnp.abs(col - disc_ref[:, at])

    unit_iota = lax.broadcasted_iota(jnp.int32, (1, unit), 1)
    low_iota = lax.broadcasted_iota(jnp.int32, (LANES, unit), 0)

    @pl.loop(0, units)
    def _(u):
        for o in range(unit_owners):
            owner = u * unit_owners + o
            live = (unit_iota >= o * cap) & (unit_iota < o * cap + counts[0, owner])
            slot = (qid_ref[u] - owner * lists) * list_width + rank_ref[u]
            slot_out[owner] = jnp.where(live, slot, -1)

    slot_in[me] = slot_out[me]

    def low_of(slot):
        return ((slot & (LANES - 1)) == low_iota).astype(F32).astype(BF)

    def high_of(slot):
        return lax.shift_right_arithmetic(slot, LANES.bit_length() - 1)

    def slot_copy(peer):
        return remote(slot_out.at[peer], slot_in.at[me], send_i, recv_i, peer, core)

    def all_slots():
        some = slot_in.at[pl.ds(0, n - 1)]
        return remote(some, some, send_i, recv_i, me, core)

    def score_copy(peer, c):
        return remote(msg.at[peer, c % 2], arrive.at[core * n + me], send_s, recv_s, peer, c)

    def all_scores():
        some = arrive.at[pl.ds(0, cores * n - 1)]
        return remote(some, some, send_s, recv_s, me, core)

    hi_iota = lax.broadcasted_iota(jnp.int32, (2 * half_rows, unit), 0)

    @pl.loop(0, steps)
    def _(s):
        p = lax.rem(first_step + s, steps)
        slot = lax.rem(s, 2)

        @pl.when(s + 1 < steps)
        def _():
            x_fetch(s + 1).start()

        x_fetch(s).wait()
        at = pl.ds(pl.multiple_of(p * step_rows, step_rows), step_rows)
        x = x_buf[slot]
        left[:features, at] = x.T
        acc = jnp.zeros((step_rows, LANES), F32)
        for k in range(groups):
            cols = slice(k * WIDE, (k + 1) * WIDE)
            v = (jnp.dot(x, w_low[:, cols], preferred_element_type=F32) + b_ref[:, cols]).astype(BF)
            v2 = v * v
            t = jnp.tanh(v * (BF(C1) * v2 + BF(C0)))
            up = BF(1.0) + t
            h = v * up
            h_all[k, at, :] = h
            g_all[k, at, :] = up + (h * (BF(1.0) - t)) * (BF(3.0 * C1) * v2 + BF(C0))
            acc = acc + jnp.dot(h, wo_pair[cols, :], preferred_element_type=F32)
        values = jnp.sum(acc.T, axis=0, keepdims=True)
        for i in range(step_units):
            top, rest = two_pieces(values[:, i * unit : (i + 1) * unit])
            for o in range(unit_owners):
                owner = (p * step_units + i) * unit_owners + o
                slot = slot_out[owner]
                hit = high_of(slot) == hi_iota
                spread = jnp.concatenate(
                    [jnp.where(hit, top, 0.0).astype(BF), jnp.where(hit, rest, 0.0).astype(BF)], axis=0
                )
                sums = lax.dot_general(
                    spread, low_of(slot), (((1,), (1,)), ((), ())), preferred_element_type=F32
                )
                placed = sums[: 2 * half_rows] + sums[2 * half_rows :]
                msg[owner, 0] = placed[:half_rows]
                msg[owner, 1] = placed[half_rows:]

        @pl.when(s == 0)
        def _():
            pl.semaphore_wait(barrier, cores * n - 1)

            @pl.loop(1, n)
            def _(k):
                slot_copy(lax.rem(me + k, n)).start()

        for i in range(step_units * unit_owners):
            owner = p * step_units * unit_owners + i
            for c in range(cores):
                @pl.when((owner != me) | (c != core))
                def _():
                    score_copy(owner, c).start()

    all_scores().wait_recv()
    arrive[core * n + me] = msg[me, side]
    s_row[...] = 0.5 * lax.fori_loop(
        1, cores * n, lambda k, total: total + arrive[k], arrive[0]
    )
    lane_row = lax.broadcasted_iota(jnp.int32, (1, LANES), 1)

    @pl.loop(0, half_lists)
    def _(q):
        base = q * per_list
        length = lengths[side * half_lists + q]
        rows_s, rows_g = [], []
        gain = gain_ref[pl.ds(side * half_lists + q, 1), :]
        for k in range(per_list):
            keep = lane_row + k * LANES < length
            rows_s.append(jnp.where(keep, s_row[pl.ds(base + k, 1), :], -1e30))
            rows_g.append(jnp.where(keep, gain[:, k * LANES : (k + 1) * LANES], 0.0))
        row_s = jnp.concatenate(rows_s, axis=1)
        row_g = jnp.concatenate(rows_g, axis=1)
        sums = jnp.zeros((8, list_width), F32)
        for k in range(per_list):
            col_s = columns(rows_s[k])
            col_g = columns(rows_g[k])
            for r in range(0, LANES, 8):
                cs = jnp.concatenate([col_s[r : r + 8]] * per_list, axis=1)
                cg = jnp.concatenate([col_g[r : r + 8]] * per_list, axis=1)
                delta_g = cg - row_g
                delta_t = jnp.tanh(cs - row_s)
                sums = sums + pair_w[k * LANES + r : k * LANES + r + 8, :] * (delta_g - jnp.abs(delta_g) * delta_t)
        lam = 0.5 * jnp.sum(sums, axis=0, keepdims=True)
        for k in range(per_list):
            l_row[pl.ds(base + k, 1), :] = lam[:, k * LANES : (k + 1) * LANES]

    def doc_copy():
        return remote(l_row, doc_in, doc_sem.at[0], doc_sem.at[1], me, pair_core)

    doc_copy().start()
    table = jnp.concatenate(two_pieces(l_row[...] * scale), axis=0).astype(BF)
    spot = lax.broadcasted_iota(jnp.int32, (2 * half_rows, unit), 0)
    spot = jnp.where(spot >= half_rows, spot - half_rows, spot) + side * half_rows

    def lam_copy(peer, c):
        return remote(ans_out.at[peer], ans_in.at[side * n + me], send_l, recv_l, peer, c)

    def all_lams():
        some = ans_in.at[pl.ds(0, 2 * n - 1)]
        return remote(some, some, send_l, recv_l, me, core)

    def answer(shard):
        slot = slot_in[shard]
        found = jnp.dot(table, low_of(slot), preferred_element_type=F32)
        return jnp.sum(jnp.where(high_of(slot) == spot, found, 0.0), axis=0, keepdims=True)

    all_slots().wait_recv()

    @pl.loop(0, (n - 1) // 3)
    def _(k):
        peers = [lax.rem(me + 1 + 3 * k + j, n) for j in range(3)]
        replies = [answer(peer) for peer in peers]
        for peer, reply in zip(peers, replies):
            ans_out[peer] = reply
        for peer in peers:
            lam_copy(peer, core).start()
            lam_copy(peer, pair_core).start()

    ans_out[me] = answer(me)
    lam_copy(me, pair_core).start()
    ans_in[side * n + me] = ans_out[me]
    doc_copy().wait_recv()
    mine_first = jnp.full((half_rows, LANES), side) == 0
    ordered = [
        jnp.where(mine_first, l_row[...], doc_in[...]), jnp.where(mine_first, doc_in[...], l_row[...])
    ]
    for half in range(2):
        for q in range(half_lists):
            for k in range(per_list):
                doc_ref[half * half_lists + q : half * half_lists + q + 1, k * LANES : (k + 1) * LANES] = (
                    ordered[half][q * per_list + k : q * per_list + k + 1]
                )

    tail_spot = lax.broadcasted_iota(jnp.int32, (16, unit), 0)

    all_lams().wait_recv()

    @pl.loop(0, units)
    def _(u):
        lam = jnp.zeros((1, unit), F32)
        for o in range(unit_owners):
            owner = u * unit_owners + o
            lam = lam + (ans_in[owner] + ans_in[n + owner])
        at = pl.ds(pl.multiple_of(u * unit, LANES), unit)
        left[:features, at] = (left[:features, at].astype(F32) * lam).astype(BF)
        top, rest = two_pieces(lam)
        left[features:, at] = jnp.where(
            tail_spot == 0, top, jnp.where(tail_spot == 1, rest, 0.0)
        ).astype(BF)

    chunk_rows = parts.shape[1]
    padded = chunk_rows * parts_per_span
    per_group = WIDE // LANES * parts_per_span
    round_groups = max(1, PLANE // per_group)
    round_planes = max(1, per_group // PLANE)
    rounds = groups // round_groups
    tail_part, tail_at = features // chunk_rows, features % chunk_rows

    def part_copy(owner):
        at, q = owner // PLANE, lax.rem(owner, PLANE)
        slot = lax.rem(place + PLANE - q, PLANE) - 1
        return remote(
            parts.at[owner], arr_xy.at[at, slot], send_p, recv_p.at[at], plane * PLANE + q, core
        )

    def part_arrivals(at):
        return remote(arr_xy.at[at], arr_xy.at[at], send_p, recv_p.at[at], me, core)

    def mid_copy(at):
        slot = lax.rem(plane + outer - at, outer) - 1
        return remote(mid.at[at], arr_z.at[slot], send_m, recv_m, at * PLANE + place, core)

    def all_mids():
        return remote(arr_z, arr_z, send_m, recv_m, me, core)

    def tail_of(total):
        rows = total[tail_at : tail_at + 4]
        return tail_rows(rows[0:1] + rows[2:3], rows[1:2] + rows[3:4])

    def round_of(i):
        return lax.rem(plane // round_planes + 1 + i, rounds)

    def reduce_round(i):
        for j in range(round_planes):
            at = round_of(i) * round_planes + j
            total = parts[at * PLANE + place].astype(F32)
            part_arrivals(at).wait_recv()
            for d in range(PLANE - 1):
                total = total + arr_xy[at, d].astype(F32)

            @pl.when(at == plane)
            def _():
                own[...] = total

            @pl.when(at != plane)
            def _():
                mid[at] = total.astype(BF)

                @pl.when(lax.rem(at * PLANE + place, parts_per_span) == tail_part)
                def _():
                    mid[at, tail_at : tail_at + 16, :] = tail_of(total)

                mid_copy(at).start()

    @pl.loop(0, rounds)
    def _(i):
        for gg in range(round_groups):
            group = round_of(i) * round_groups + lax.rem(place // 2 + 1 + gg, round_groups)
            half_wo = 0.5 * wo_ref[group]
            sums = jnp.dot(left[...], g_all[group], preferred_element_type=F32)
            sums_o = jnp.dot(left[features:, :], h_all[group], preferred_element_type=F32)
            grad_b = jnp.sum(sums[features:], axis=0, keepdims=True) * half_wo
            grad_o = 0.5 * jnp.sum(sums_o, axis=0, keepdims=True)
            pieces = [(sums[:features] * half_wo).astype(BF), tail_rows(grad_b, grad_o)]
            if padded > features + 16:
                pieces.append(jnp.zeros((padded - features - 16, WIDE), BF))
            block = jnp.concatenate(pieces, axis=0)
            for j in range(per_group):
                span, part = j // parts_per_span, j % parts_per_span
                parts[group * per_group + j] = block[
                    part * chunk_rows : (part + 1) * chunk_rows, span * LANES : (span + 1) * LANES
                ]
            for j in range(per_group):
                owner = group * per_group + j

                @pl.when(lax.rem(owner, PLANE) != place)
                def _():
                    part_copy(owner).start()

        @pl.when(i > 0)
        def _():
            reduce_round(i - 1)

    reduce_round(rounds - 1)

    total = own[...]
    all_mids().wait_recv()
    for i in range(outer - 1):
        total = total + arr_z[i].astype(F32)
    out_ref[me] = total.astype(BF)

    @pl.when(lax.rem(me, parts_per_span) == tail_part)
    def _():
        out_ref[me, tail_at : tail_at + 16, :] = tail_of(total)

    cut = chunk_rows // 32 * 16
    halves = [pl.ds(0, cut), pl.ds(cut, chunk_rows - cut)]
    near = [flip(place, 1), flip(place, 2)]

    def piece(at, q, h):
        return out_ref.at[at * PLANE + q, halves[h]]

    def along(at, h, d, to_plane):
        rows = piece(at, place, h)
        return remote(
            rows, rows, send_z.at[d, h, at], recv_z.at[h, at], to_plane * PLANE + place, core
        )

    def beside(at, h, w):
        rows = piece(at, place, h)
        return remote(
            rows, rows, send_n, recv_n.at[w, h, at], plane * PLANE + near[w], core
        )

    def beside_arrival(at, h, w):
        rows = piece(at, near[w], h)
        return remote(
            rows, rows, send_n, recv_n.at[w, h, at], plane * PLANE + near[w], core
        )

    def passed(at, w):
        rows = piece(at, near[w], w)
        return remote(
            rows, rows, send_d, recv_d, plane * PLANE + near[1 - w], core
        )

    def all_passed():
        some = out_ref.at[pl.ds(0, outer)]
        return remote(some, some, send_d, recv_d, me, core)

    def spread_own(h):
        for d, to in ((0, plane + 1), (1, plane - 1)):
            @pl.when((to >= 0) & (to < outer))
            def _():
                along(plane, h, d, to).start()
        for w in range(2):
            beside(plane, h, w).start()

    def spread_far(dist, h):
        for d, sign in ((0, 1), (1, -1)):
            at, to = plane - sign * dist, plane + sign

            @pl.when((at >= 0) & (at < outer))
            def _():
                along(at, h, d, plane).wait_recv()

                @pl.when((to >= 0) & (to < outer))
                def _():
                    along(at, h, d, to).start()

                for w in range(2):
                    beside(at, h, w).start()

    def at_distance(dist, do):
        for sign in (1, -1) if dist else (1,):
            at = plane - sign * dist

            @pl.when((at >= 0) & (at < outer))
            def _():
                do(at)

    def pass_on(at):
        for w in range(2):
            beside_arrival(at, w, w).wait_recv()
            passed(at, w).start()

    def finish(at):
        for w in range(2):
            beside_arrival(at, 1 - w, w).wait_recv()

    for h in range(2):
        spread_own(h)
    for dist in range(1, outer):
        spread_far(dist, 0)
        spread_far(dist, 1)
        at_distance(dist - 1, pass_on)
    at_distance(outer - 1, pass_on)
    for dist in range(outer):
        at_distance(dist, finish)
    all_passed().wait_recv()

    doc_copy().wait_send()
    all_slots().wait_send()
    all_scores().wait_send()
    all_lams().wait_send()
    all_mids().wait_send()
    some = parts.at[pl.ds(0, n - outer)]
    remote(some, some, send_p, recv_p.at[0], me, core).wait_send()
    some = out_ref.at[pl.ds(0, 2 * outer)]
    remote(some, some, send_n, recv_n.at[0, 0, 0], me, core).wait_send()
    all_passed().wait_send()

    @pl.loop(0, outer)
    def _(at):
        for h in range(2):
            for d, sign in ((0, 1), (1, -1)):
                to = plane + sign

                @pl.when((to >= 0) & (to < outer) & (sign * (plane - at) >= 0))
                def _():
                    along(at, h, d, to).wait_send()


def weight_pieces(groups):
    return min(4, groups)


def gradients(n, cores, rows, weights, bias, wo, qid, rank, gains, disc, counts, lengths, parts_per_span, chunk_rows):
    total, features = rows.shape
    hidden = weights.shape[1]
    groups = hidden // WIDE
    lists, list_width = gains.shape
    per_list = list_width // LANES
    half_rows = lists * per_list // 2
    units, _, unit = qid.shape
    step_rows = 2 * unit if units % 2 == 0 else unit
    outer = n // PLANE
    vmem = pl.BlockSpec(memory_space=pltpu.VMEM)
    smem = pl.BlockSpec(memory_space=pltpu.SMEM)
    hbm = pl.BlockSpec(memory_space=pl.ANY)
    chunk = (chunk_rows, LANES)
    dma = pltpu.SemaphoreType.DMA
    return pl.pallas_call(
        functools.partial(step_kernel, n, cores, 1.0 / (lists * n), parts_per_span),
        in_specs=[hbm, hbm, vmem, vmem, vmem, vmem, vmem, vmem, smem, smem],
        out_specs=[vmem, vmem],
        out_shape=[
            jax.ShapeDtypeStruct((n,) + chunk, BF),
            jax.ShapeDtypeStruct((lists, list_width), F32),
        ],
        scratch_shapes=[
            pltpu.VMEM((2, step_rows, features), BF),
            pltpu.VMEM((2, features, hidden // weight_pieces(groups)), F32),
            pltpu.VMEM((features, hidden), BF),
            pltpu.VMEM((hidden, LANES), BF),
            pltpu.VMEM((list_width, list_width), F32),
            pltpu.VMEM((groups, total, WIDE), BF),
            pltpu.VMEM((groups, total, WIDE), BF),
            pltpu.VMEM((features + 16, total), BF),
            pltpu.VMEM((n, 1, unit), jnp.int32),
            pltpu.VMEM((n, 1, unit), jnp.int32),
            pltpu.VMEM((n, 2, half_rows, LANES), F32),
            pltpu.VMEM((cores * n, half_rows, LANES), F32),
            pltpu.VMEM((half_rows, LANES), F32),
            pltpu.VMEM((half_rows, LANES), F32),
            pltpu.VMEM((half_rows, LANES), F32),
            pltpu.VMEM((n, 1, unit), F32),
            pltpu.VMEM((2 * n, 1, unit), F32),
            pltpu.VMEM((n,) + chunk, BF),
            pltpu.VMEM((outer, PLANE - 1) + chunk, BF),
            pltpu.VMEM((outer,) + chunk, BF),
            pltpu.VMEM((outer - 1,) + chunk, BF),
            pltpu.VMEM(chunk, F32),
            dma((2,)), dma((4,)), dma, dma,
            dma, dma, dma((2,)), dma, dma,
            dma, dma((outer,)), dma, dma,
            dma((2, 2, outer)), dma((2, outer)), dma, dma((2, 2, outer)), dma, dma,
        ],
        compiler_params=pltpu.CompilerParams(
            collective_id=0, has_side_effects=True, vmem_limit_bytes=63 << 20
        ),
    )(rows, weights, bias, wo, qid, rank, gains, disc, counts, lengths)


def adam_step(weights, moment, second, gradient):
    moment_next = beta_one * moment + (1.0 - beta_one) * gradient
    second_next = beta_two * second + (1.0 - beta_two) * gradient * gradient
    weights_next = weights - learn_rate * moment_next / (jnp.sqrt(second_next) + adam_eps)
    return (weights_next, moment_next, second_next)


def adam_kernel(steps, wide, g_ref, doc_ref, *refs):
    ins, doc_out, outs = refs[:9], refs[9], refs[10:19]
    matrix, vector, in_sem, vector_sem, out_sem, back_sem, doc_sem = refs[19:]
    features, hidden = matrix.shape[1:]
    rows = features // steps
    parts = [slice(r * rows, (r + 1) * rows) for r in range(steps)]

    def whole(ref, sem):
        return pltpu.make_async_copy(ref, ref, sem)

    doc_copy = pltpu.make_async_copy(doc_ref, doc_out, doc_sem)
    for r, at in enumerate(parts):
        for i in range(3):
            pltpu.make_async_copy(ins[i].at[at], matrix.at[i, at], in_sem.at[r]).start()
        if r == 0:
            for i in range(6):
                pltpu.make_async_copy(ins[3 + i], vector.at[i], vector_sem).start()
    doc_copy.start()
    for r, at in enumerate(parts):
        whole(matrix.at[:, at], in_sem.at[r]).wait()
        for k in range(0, g_ref.shape[0], wide):
            cols = slice(k * LANES, (k + wide) * LANES)
            grad = jnp.concatenate([g_ref[k + j, at, :] for j in range(wide)], axis=1).astype(F32)
            matrix[0, at, cols], matrix[1, at, cols], matrix[2, at, cols] = adam_step(
                matrix[0, at, cols], matrix[1, at, cols], matrix[2, at, cols], grad
            )
        for i in range(3):
            pltpu.make_async_copy(matrix.at[i, at], outs[i].at[at], out_sem).start()
        if r == 0:
            whole(vector, vector_sem).wait()
            for first, row in ((0, 0), (3, 1)):
                grad = jnp.concatenate(
                    [
                        g_ref[k, features : features + 16, :].astype(F32)[row : row + 1]
                        + g_ref[k, features : features + 16, :].astype(F32)[row + 2 : row + 3]
                        for k in range(g_ref.shape[0])
                    ],
                    axis=1,
                )
                vector[first], vector[first + 1], vector[first + 2] = adam_step(
                    vector[first], vector[first + 1], vector[first + 2], grad
                )
            for i in range(6):
                pltpu.make_async_copy(vector.at[i], outs[3 + i], back_sem).start()
    doc_copy.wait()
    whole(vector, back_sem).wait()
    whole(matrix, out_sem).wait()


def adam(grads, doc, matrices, vectors):
    features, hidden = matrices[0].shape
    steps = 4
    vmem = pl.BlockSpec(memory_space=pltpu.VMEM)
    hbm = pl.BlockSpec(memory_space=pl.ANY)
    dma = pltpu.SemaphoreType.DMA
    operands = [*matrices, *(v.reshape(1, hidden) for v in vectors)]
    outs = pl.pallas_call(
        functools.partial(adam_kernel, steps, 4),
        in_specs=[vmem, vmem] + [hbm] * 9,
        out_specs=[hbm] * 10,
        out_shape=[jax.ShapeDtypeStruct(a.shape, F32) for a in [doc] + operands],
        scratch_shapes=[
            pltpu.VMEM((3, features, hidden), F32), pltpu.VMEM((6, 1, hidden), F32),
            dma((steps,)), dma, dma, dma, dma,
        ],
        compiler_params=pltpu.CompilerParams(vmem_limit_bytes=60 << 20),
    )(grads, doc, *operands)
    return (*outs[:4], *(v.reshape(hidden) for v in outs[4:]))


def per_device(
    log_rows, query_ids, doc_ranks, row_counts, list_lengths, gains,
    weight_in, bias_in, weight_out, moment_w, second_w,
    moment_b, second_b, moment_o, second_o,
):
    n, cores = lax.axis_size("dp"), lax.axis_size("mp")
    total, features = log_rows.shape
    cap = total // n
    hidden = weight_in.shape[1]
    list_width = gains.shape[1]
    unit = math.lcm(cap, LANES)
    units = total // unit

    disc = (1.0 / np.log2(2.0 + np.arange(list_width))).astype(np.float32).reshape(1, list_width)
    spans = hidden // LANES
    row_parts = max(1, n // spans)
    whole_tile = 16 * row_parts
    padded = (features + 16 + whole_tile - 1) // whole_tile * whole_tile
    grads, doc = gradients(
        n, cores, log_rows, weight_in, bias_in.reshape(1, hidden), weight_out.reshape(hidden // WIDE, 1, WIDE),
        query_ids.reshape(units, 1, unit), doc_ranks.reshape(units, 1, unit),
        gains, jnp.asarray(disc), row_counts, list_lengths, row_parts, padded // row_parts,
    )
    return adam(
        grads.reshape(spans, padded, LANES), doc, (weight_in, moment_w, second_w),
        (bias_in, moment_b, second_b, weight_out, moment_o, second_o),
    )


def solution(mesh):
    dp, mp, both = P("dp"), P("mp"), P(None, "mp")
    rows = P("dp", None)
    return jax.shard_map(
        per_device,
        mesh=mesh,
        in_specs=(rows, dp, dp, rows, dp, rows, both, mp, mp, both, both, mp, mp, mp, mp),
        out_specs=(rows, both, both, both, mp, mp, mp, mp, mp, mp),
        check_vma=False,
    )
```

```python
import functools
import math

import jax
import jax.numpy as jnp
import numpy as np
from jax import lax
from jax.experimental import pallas as pl
from jax.experimental.pallas import tpu as pltpu
from jax.sharding import PartitionSpec as P

beta_one = 0.9
beta_two = 0.95
learn_rate = 0.001
adam_eps = 1e-08

C0 = math.sqrt(2.0 / math.pi)
C1 = C0 * 0.044715
MESH = pl.DeviceIdType.MESH
LANES = 128
WIDE = 256
PLANE = 4
BF = jnp.bfloat16
F32 = jnp.float32


def flip(index, mask):
    bit = 1
    while bit <= mask:
        if mask & bit:
            index = index + bit - 2 * bit * lax.rem(index // bit, 2)
        bit *= 2
    return index


def columns(row):
    return jnp.broadcast_to(row, (LANES, LANES)).T


def two_pieces(values):
    top = values.astype(BF).astype(F32)
    return top, values - top


def tail_rows(grad_b, grad_o):
    spot = lax.broadcasted_iota(jnp.int32, (16, grad_b.shape[1]), 0)
    top_b, rest_b = two_pieces(grad_b)
    top_o, rest_o = two_pieces(grad_o)
    tail = jnp.where(spot == 0, top_b, jnp.where(spot == 1, top_o, 0.0))
    tail = jnp.where(spot == 2, rest_b, jnp.where(spot == 3, rest_o, tail))
    return tail.astype(BF)


def step_kernel(
    n, cores, scale, parts_per_span,
    x_hbm, w_hbm, b_ref, wo_ref, qid_ref, rank_ref, gain_ref, disc_ref, counts, lengths,
    out_ref, doc_ref,
    x_buf, w_buf, w_low, wo_pair, pair_w, h_all, g_all, left,
    slot_out, slot_in, msg, arrive, s_row, l_row, doc_in, ans_out, ans_in,
    parts, arr_xy, mid, arr_z, own,
    x_sem, w_sem, send_i, recv_i, send_s, recv_s, doc_sem, send_l, recv_l,
    send_p, recv_p, send_m, recv_m, send_z, recv_z, send_n, recv_n, send_d, recv_d,
):
    me = lax.axis_index("dp")
    core = lax.axis_index("mp")
    side = lax.rem(core, 2)
    pair_core = core + 1 - 2 * side
    outer = n // PLANE
    plane, place = me // PLANE, lax.rem(me, PLANE)

    total_rows, features = x_hbm.shape
    groups = g_all.shape[0]
    step_rows = x_buf.shape[1]
    steps = total_rows // step_rows
    units, _, unit = qid_ref.shape
    step_units = step_rows // unit
    cap = total_rows // n
    unit_owners = unit // cap
    lists, list_width = gain_ref.shape
    per_list = list_width // LANES
    half_rows = lists * per_list // 2
    half_lists = lists // 2
    first_step = me // (step_units * unit_owners) + 1

    def remote(source, target, send, recv, peer, to_core):
        return pltpu.make_async_remote_copy(
            src_ref=source, dst_ref=target, send_sem=send, recv_sem=recv,
            device_id=(peer, to_core), device_id_type=MESH,
        )

    barrier = pltpu.get_barrier_semaphore()

    def x_fetch(s):
        at = lax.rem(first_step + s, steps) * step_rows
        slot = lax.rem(s, 2)
        return pltpu.make_async_copy(
            x_hbm.at[pl.ds(pl.multiple_of(at, step_rows), step_rows), :], x_buf.at[slot], x_sem.at[slot]
        )

    staging = [w_buf.at[0], w_buf.at[1], pair_w.at[:features], pair_w.at[features : 2 * features]]
    pieces = weight_pieces(groups)
    span = groups * WIDE // pieces

    def w_fetch(k):
        return pltpu.make_async_copy(
            w_hbm.at[:, k * span : (k + 1) * span], staging[k], w_sem.at[k]
        )

    for k in range(pieces):
        w_fetch(k).start()
    x_fetch(0).start()

    @pl.loop(1, n)
    def _(k):
        peer = lax.rem(me + k, n)
        for d in range(cores):
            pl.semaphore_signal(
                barrier, inc=1, device_id=(peer, lax.rem(core + d, cores)), device_id_type=MESH
            )

    for d in range(1, cores):
        pl.semaphore_signal(
            barrier, inc=1, device_id=(me, lax.rem(core + d, cores)), device_id_type=MESH
        )

    lane = lax.broadcasted_iota(jnp.int32, (LANES, LANES), 1)
    for k in range(groups * WIDE // LANES):
        at = k * LANES
        wo_row = 0.5 * wo_ref[at // WIDE, :, at % WIDE : at % WIDE + LANES]
        top, rest = two_pieces(columns(wo_row))
        wo_pair[at : at + LANES, :] = jnp.where(lane == 0, top, jnp.where(lane == 1, rest, 0.0)).astype(BF)
    for k in range(pieces):
        w_fetch(k).wait()
        w_low[:, k * span : (k + 1) * span] = staging[k][...].astype(BF)
    for k in range(per_list):
        col = columns(disc_ref[:, k * LANES : (k + 1) * LANES])
        for m in range(per_list):
            at = slice(m * LANES, (m + 1) * LANES)
            pair_w[k * LANES : (k + 1) * LANES, at] = jnp.abs(col - disc_ref[:, at])

    unit_iota = lax.broadcasted_iota(jnp.int32, (1, unit), 1)
    low_iota = lax.broadcasted_iota(jnp.int32, (LANES, unit), 0)

    @pl.loop(0, units)
    def _(u):
        for o in range(unit_owners):
            owner = u * unit_owners + o
            live = (unit_iota >= o * cap) & (unit_iota < o * cap + counts[0, owner])
            slot = (qid_ref[u] - owner * lists) * list_width + rank_ref[u]
            slot_out[owner] = jnp.where(live, slot, -1)

    slot_in[me] = slot_out[me]

    def low_of(slot):
        return ((slot & (LANES - 1)) == low_iota).astype(F32).astype(BF)

    def high_of(slot):
        return lax.shift_right_arithmetic(slot, LANES.bit_length() - 1)

    def slot_copy(peer):
        return remote(slot_out.at[peer], slot_in.at[me], send_i, recv_i, peer, core)

    def all_slots():
        some = slot_in.at[pl.ds(0, n - 1)]
        return remote(some, some, send_i, recv_i, me, core)

    def score_copy(peer, c):
        return remote(msg.at[peer, c % 2], arrive.at[core * n + me], send_s, recv_s, peer, c)

    def all_scores():
        some = arrive.at[pl.ds(0, cores * n - 1)]
        return remote(some, some, send_s, recv_s, me, core)

    hi_iota = lax.broadcasted_iota(jnp.int32, (2 * half_rows, unit), 0)

    @pl.loop(0, steps)
    def _(s):
        p = lax.rem(first_step + s, steps)
        slot = lax.rem(s, 2)

        @pl.when(s + 1 < steps)
        def _():
            x_fetch(s + 1).start()

        x_fetch(s).wait()
        at = pl.ds(pl.multiple_of(p * step_rows, step_rows), step_rows)
        x = x_buf[slot]
        left[:features, at] = x.T
        acc = jnp.zeros((step_rows, LANES), F32)
        for k in range(groups):
            cols = slice(k * WIDE, (k + 1) * WIDE)
            v = (jnp.dot(x, w_low[:, cols], preferred_element_type=F32) + b_ref[:, cols]).astype(BF)
            v2 = v * v
            t = jnp.tanh(v * (BF(C1) * v2 + BF(C0)))
            up = BF(1.0) + t
            h = v * up
            h_all[k, at, :] = h
            g_all[k, at, :] = up + (h * (BF(1.0) - t)) * (BF(3.0 * C1) * v2 + BF(C0))
            acc = acc + jnp.dot(h, wo_pair[cols, :], preferred_element_type=F32)
        values = jnp.sum(acc.T, axis=0, keepdims=True)
        for i in range(step_units):
            top, rest = two_pieces(values[:, i * unit : (i + 1) * unit])
            for o in range(unit_owners):
                owner = (p * step_units + i) * unit_owners + o
                slot = slot_out[owner]
                hit = high_of(slot) == hi_iota
                spread = jnp.concatenate(
                    [jnp.where(hit, top, 0.0).astype(BF), jnp.where(hit, rest, 0.0).astype(BF)], axis=0
                )
                sums = lax.dot_general(
                    spread, low_of(slot), (((1,), (1,)), ((), ())), preferred_element_type=F32
                )
                placed = sums[: 2 * half_rows] + sums[2 * half_rows :]
                msg[owner, 0] = placed[:half_rows]
                msg[owner, 1] = placed[half_rows:]

        @pl.when(s == 0)
        def _():
            pl.semaphore_wait(barrier, cores * n - 1)

            @pl.loop(1, n)
            def _(k):
                slot_copy(lax.rem(me + k, n)).start()

        for i in range(step_units * unit_owners):
            owner = p * step_units * unit_owners + i
            for c in range(cores):
                @pl.when((owner != me) | (c != core))
                def _():
                    score_copy(owner, c).start()

    all_scores().wait_recv()
    arrive[core * n + me] = msg[me, side]
    s_row[...] = 0.5 * lax.fori_loop(
        1, cores * n, lambda k, total: total + arrive[k], arrive[0]
    )
    lane_row = lax.broadcasted_iota(jnp.int32, (1, LANES), 1)

    @pl.loop(0, half_lists)
    def _(q):
        base = q * per_list
        length = lengths[side * half_lists + q]
        rows_s, rows_g = [], []
        gain = gain_ref[pl.ds(side * half_lists + q, 1), :]
        for k in range(per_list):
            keep = lane_row + k * LANES < length
            rows_s.append(jnp.where(keep, s_row[pl.ds(base + k, 1), :], -1e30))
            rows_g.append(jnp.where(keep, gain[:, k * LANES : (k + 1) * LANES], 0.0))
        row_s = jnp.concatenate(rows_s, axis=1)
        row_g = jnp.concatenate(rows_g, axis=1)
        sums = jnp.zeros((8, list_width), F32)
        for k in range(per_list):
            col_s = columns(rows_s[k])
            col_g = columns(rows_g[k])
            for r in range(0, LANES, 8):
                cs = jnp.concatenate([col_s[r : r + 8]] * per_list, axis=1)
                cg = jnp.concatenate([col_g[r : r + 8]] * per_list, axis=1)
                delta_g = cg - row_g
                delta_t = jnp.tanh(cs - row_s)
                sums = sums + pair_w[k * LANES + r : k * LANES + r + 8, :] * (delta_g - jnp.abs(delta_g) * delta_t)
        lam = 0.5 * jnp.sum(sums, axis=0, keepdims=True)
        for k in range(per_list):
            l_row[pl.ds(base + k, 1), :] = lam[:, k * LANES : (k + 1) * LANES]

    def doc_copy():
        return remote(l_row, doc_in, doc_sem.at[0], doc_sem.at[1], me, pair_core)

    doc_copy().start()
    table = jnp.concatenate(two_pieces(l_row[...] * scale), axis=0).astype(BF)
    spot = lax.broadcasted_iota(jnp.int32, (2 * half_rows, unit), 0)
    spot = jnp.where(spot >= half_rows, spot - half_rows, spot) + side * half_rows

    def lam_copy(peer, c):
        return remote(ans_out.at[peer], ans_in.at[side * n + me], send_l, recv_l, peer, c)

    def all_lams():
        some = ans_in.at[pl.ds(0, 2 * n - 1)]
        return remote(some, some, send_l, recv_l, me, core)

    def answer(shard):
        slot = slot_in[shard]
        found = jnp.dot(table, low_of(slot), preferred_element_type=F32)
        return jnp.sum(jnp.where(high_of(slot) == spot, found, 0.0), axis=0, keepdims=True)

    all_slots().wait_recv()

    @pl.loop(0, (n - 1) // 3)
    def _(k):
        peers = [lax.rem(me + 1 + 3 * k + j, n) for j in range(3)]
        replies = [answer(peer) for peer in peers]
        for peer, reply in zip(peers, replies):
            ans_out[peer] = reply
        for peer in peers:
            lam_copy(peer, core).start()
            lam_copy(peer, pair_core).start()

    ans_out[me] = answer(me)
    lam_copy(me, pair_core).start()
    ans_in[side * n + me] = ans_out[me]

    tail_spot = lax.broadcasted_iota(jnp.int32, (16, unit), 0)

    all_lams().wait_recv()

    @pl.loop(0, units)
    def _(u):
        lam = jnp.zeros((1, unit), F32)
        for o in range(unit_owners):
            owner = u * unit_owners + o
            lam = lam + (ans_in[owner] + ans_in[n + owner])
        at = pl.ds(pl.multiple_of(u * unit, LANES), unit)
        left[:features, at] = (left[:features, at].astype(F32) * lam).astype(BF)
        top, rest = two_pieces(lam)
        left[features:, at] = jnp.where(
            tail_spot == 0, top, jnp.where(tail_spot == 1, rest, 0.0)
        ).astype(BF)

    chunk_rows = parts.shape[1]
    padded = chunk_rows * parts_per_span
    per_group = WIDE // LANES * parts_per_span
    round_groups = max(1, PLANE // per_group)
    round_planes = max(1, per_group // PLANE)
    rounds = groups // round_groups
    tail_part, tail_at = features // chunk_rows, features % chunk_rows

    def part_copy(owner):
        at, q = owner // PLANE, lax.rem(owner, PLANE)
        slot = lax.rem(place + PLANE - q, PLANE) - 1
        return remote(
            parts.at[owner], arr_xy.at[at, slot], send_p, recv_p.at[at], plane * PLANE + q, core
        )

    def part_arrivals(at):
        return remote(arr_xy.at[at], arr_xy.at[at], send_p, recv_p.at[at], me, core)

    def mid_copy(at):
        slot = lax.rem(plane + outer - at, outer) - 1
        return remote(mid.at[at], arr_z.at[slot], send_m, recv_m, at * PLANE + place, core)

    def all_mids():
        return remote(arr_z, arr_z, send_m, recv_m, me, core)

    def tail_of(total):
        rows = total[tail_at : tail_at + 4]
        return tail_rows(rows[0:1] + rows[2:3], rows[1:2] + rows[3:4])

    def round_of(i):
        return lax.rem(plane // round_planes + 1 + i, rounds)

    def reduce_round(i):
        for j in range(round_planes):
            at = round_of(i) * round_planes + j
            total = parts[at * PLANE + place].astype(F32)
            part_arrivals(at).wait_recv()
            for d in range(PLANE - 1):
                total = total + arr_xy[at, d].astype(F32)

            @pl.when(at == plane)
            def _():
                own[...] = total

            @pl.when(at != plane)
            def _():
                mid[at] = total.astype(BF)

                @pl.when(lax.rem(at * PLANE + place, parts_per_span) == tail_part)
                def _():
                    mid[at, tail_at : tail_at + 16, :] = tail_of(total)

                mid_copy(at).start()

    @pl.loop(0, rounds)
    def _(i):
        for gg in range(round_groups):
            group = round_of(i) * round_groups + lax.rem(place // 2 + 1 + gg, round_groups)
            half_wo = 0.5 * wo_ref[group]
            sums = jnp.dot(left[...], g_all[group], preferred_element_type=F32)
            sums_o = jnp.dot(left[features:, :], h_all[group], preferred_element_type=F32)
            grad_b = jnp.sum(sums[features:], axis=0, keepdims=True) * half_wo
            grad_o = 0.5 * jnp.sum(sums_o, axis=0, keepdims=True)
            pieces = [(sums[:features] * half_wo).astype(BF), tail_rows(grad_b, grad_o)]
            if padded > features + 16:
                pieces.append(jnp.zeros((padded - features - 16, WIDE), BF))
            block = jnp.concatenate(pieces, axis=0)
            for j in range(per_group):
                span, part = j // parts_per_span, j % parts_per_span
                parts[group * per_group + j] = block[
                    part * chunk_rows : (part + 1) * chunk_rows, span * LANES : (span + 1) * LANES
                ]
            for j in range(per_group):
                owner = group * per_group + j

                @pl.when(lax.rem(owner, PLANE) != place)
                def _():
                    part_copy(owner).start()

        @pl.when(i > 0)
        def _():
            reduce_round(i - 1)

    reduce_round(rounds - 1)

    total = own[...]
    all_mids().wait_recv()
    for i in range(outer - 1):
        total = total + arr_z[i].astype(F32)
    out_ref[me] = total.astype(BF)

    @pl.when(lax.rem(me, parts_per_span) == tail_part)
    def _():
        out_ref[me, tail_at : tail_at + 16, :] = tail_of(total)

    cut = chunk_rows // 32 * 16
    halves = [pl.ds(0, cut), pl.ds(cut, chunk_rows - cut)]
    near = [flip(place, 1), flip(place, 2)]

    def piece(at, q, h):
        return out_ref.at[at * PLANE + q, halves[h]]

    def along(at, h, d, to_plane):
        rows = piece(at, place, h)
        return remote(
            rows, rows, send_z.at[d, h, at], recv_z.at[h, at], to_plane * PLANE + place, core
        )

    def beside(at, h, w):
        rows = piece(at, place, h)
        return remote(
            rows, rows, send_n, recv_n.at[w, h, at], plane * PLANE + near[w], core
        )

    def beside_arrival(at, h, w):
        rows = piece(at, near[w], h)
        return remote(
            rows, rows, send_n, recv_n.at[w, h, at], plane * PLANE + near[w], core
        )

    def passed(at, w):
        rows = piece(at, near[w], w)
        return remote(
            rows, rows, send_d, recv_d, plane * PLANE + near[1 - w], core
        )

    def all_passed():
        some = out_ref.at[pl.ds(0, outer)]
        return remote(some, some, send_d, recv_d, me, core)

    def spread_own(h):
        for d, to in ((0, plane + 1), (1, plane - 1)):
            @pl.when((to >= 0) & (to < outer))
            def _():
                along(plane, h, d, to).start()
        for w in range(2):
            beside(plane, h, w).start()

    def spread_far(dist, h):
        for d, sign in ((0, 1), (1, -1)):
            at, to = plane - sign * dist, plane + sign

            @pl.when((at >= 0) & (at < outer))
            def _():
                along(at, h, d, plane).wait_recv()

                @pl.when((to >= 0) & (to < outer))
                def _():
                    along(at, h, d, to).start()

                for w in range(2):
                    beside(at, h, w).start()

    def at_distance(dist, do):
        for sign in (1, -1) if dist else (1,):
            at = plane - sign * dist

            @pl.when((at >= 0) & (at < outer))
            def _():
                do(at)

    def pass_on(at):
        for w in range(2):
            beside_arrival(at, w, w).wait_recv()
            passed(at, w).start()

    def finish(at):
        for w in range(2):
            beside_arrival(at, 1 - w, w).wait_recv()

    for h in range(2):
        spread_own(h)

    doc_copy().wait_recv()
    mine_first = jnp.full((half_rows, LANES), side) == 0
    ordered = [
        jnp.where(mine_first, l_row[...], doc_in[...]), jnp.where(mine_first, doc_in[...], l_row[...])
    ]
    for half in range(2):
        for q in range(half_lists):
            for k in range(per_list):
                doc_ref[half * half_lists + q : half * half_lists + q + 1, k * LANES : (k + 1) * LANES] = (
                    ordered[half][q * per_list + k : q * per_list + k + 1]
                )

    for dist in range(1, outer):
        spread_far(dist, 0)
        spread_far(dist, 1)
        at_distance(dist - 1, pass_on)
    at_distance(outer - 1, pass_on)
    for dist in range(outer):
        at_distance(dist, finish)
    all_passed().wait_recv()

    doc_copy().wait_send()
    all_slots().wait_send()
    all_scores().wait_send()
    all_lams().wait_send()
    all_mids().wait_send()
    some = parts.at[pl.ds(0, n - outer)]
    remote(some, some, send_p, recv_p.at[0], me, core).wait_send()
    some = out_ref.at[pl.ds(0, 2 * outer)]
    remote(some, some, send_n, recv_n.at[0, 0, 0], me, core).wait_send()
    all_passed().wait_send()

    @pl.loop(0, outer)
    def _(at):
        for h in range(2):
            for d, sign in ((0, 1), (1, -1)):
                to = plane + sign

                @pl.when((to >= 0) & (to < outer) & (sign * (plane - at) >= 0))
                def _():
                    along(at, h, d, to).wait_send()


def weight_pieces(groups):
    return min(4, groups)


def gradients(n, cores, rows, weights, bias, wo, qid, rank, gains, disc, counts, lengths, parts_per_span, chunk_rows):
    total, features = rows.shape
    hidden = weights.shape[1]
    groups = hidden // WIDE
    lists, list_width = gains.shape
    per_list = list_width // LANES
    half_rows = lists * per_list // 2
    units, _, unit = qid.shape
    step_rows = 2 * unit if units % 2 == 0 else unit
    outer = n // PLANE
    vmem = pl.BlockSpec(memory_space=pltpu.VMEM)
    smem = pl.BlockSpec(memory_space=pltpu.SMEM)
    hbm = pl.BlockSpec(memory_space=pl.ANY)
    chunk = (chunk_rows, LANES)
    dma = pltpu.SemaphoreType.DMA
    return pl.pallas_call(
        functools.partial(step_kernel, n, cores, 1.0 / (lists * n), parts_per_span),
        in_specs=[hbm, hbm, vmem, vmem, vmem, vmem, vmem, vmem, smem, smem],
        out_specs=[vmem, vmem],
        out_shape=[
            jax.ShapeDtypeStruct((n,) + chunk, BF),
            jax.ShapeDtypeStruct((lists, list_width), F32),
        ],
        scratch_shapes=[
            pltpu.VMEM((2, step_rows, features), BF),
            pltpu.VMEM((2, features, hidden // weight_pieces(groups)), F32),
            pltpu.VMEM((features, hidden), BF),
            pltpu.VMEM((hidden, LANES), BF),
            pltpu.VMEM((list_width, list_width), F32),
            pltpu.VMEM((groups, total, WIDE), BF),
            pltpu.VMEM((groups, total, WIDE), BF),
            pltpu.VMEM((features + 16, total), BF),
            pltpu.VMEM((n, 1, unit), jnp.int32),
            pltpu.VMEM((n, 1, unit), jnp.int32),
            pltpu.VMEM((n, 2, half_rows, LANES), F32),
            pltpu.VMEM((cores * n, half_rows, LANES), F32),
            pltpu.VMEM((half_rows, LANES), F32),
            pltpu.VMEM((half_rows, LANES), F32),
            pltpu.VMEM((half_rows, LANES), F32),
            pltpu.VMEM((n, 1, unit), F32),
            pltpu.VMEM((2 * n, 1, unit), F32),
            pltpu.VMEM((n,) + chunk, BF),
            pltpu.VMEM((outer, PLANE - 1) + chunk, BF),
            pltpu.VMEM((outer,) + chunk, BF),
            pltpu.VMEM((outer - 1,) + chunk, BF),
            pltpu.VMEM(chunk, F32),
            dma((2,)), dma((4,)), dma, dma,
            dma, dma, dma((2,)), dma, dma,
            dma, dma((outer,)), dma, dma,
            dma((2, 2, outer)), dma((2, outer)), dma, dma((2, 2, outer)), dma, dma,
        ],
        compiler_params=pltpu.CompilerParams(
            collective_id=0, has_side_effects=True, vmem_limit_bytes=63 << 20
        ),
    )(rows, weights, bias, wo, qid, rank, gains, disc, counts, lengths)


def adam_step(weights, moment, second, gradient):
    moment_next = beta_one * moment + (1.0 - beta_one) * gradient
    second_next = beta_two * second + (1.0 - beta_two) * gradient * gradient
    weights_next = weights - learn_rate * moment_next / (jnp.sqrt(second_next) + adam_eps)
    return (weights_next, moment_next, second_next)


def adam_kernel(steps, wide, g_ref, doc_ref, *refs):
    ins, doc_out, outs = refs[:9], refs[9], refs[10:19]
    matrix, vector, in_sem, vector_sem, out_sem, back_sem, doc_sem = refs[19:]
    features, hidden = matrix.shape[1:]
    rows = features // steps
    parts = [slice(r * rows, (r + 1) * rows) for r in range(steps)]

    def whole(ref, sem):
        return pltpu.make_async_copy(ref, ref, sem)

    doc_copy = pltpu.make_async_copy(doc_ref, doc_out, doc_sem)
    for r, at in enumerate(parts):
        for i in range(3):
            pltpu.make_async_copy(ins[i].at[at], matrix.at[i, at], in_sem.at[r]).start()
        if r == 0:
            for i in range(6):
                pltpu.make_async_copy(ins[3 + i], vector.at[i], vector_sem).start()
    doc_copy.start()
    for r, at in enumerate(parts):
        whole(matrix.at[:, at], in_sem.at[r]).wait()
        for k in range(0, g_ref.shape[0], wide):
            cols = slice(k * LANES, (k + wide) * LANES)
            grad = jnp.concatenate([g_ref[k + j, at, :] for j in range(wide)], axis=1).astype(F32)
            matrix[0, at, cols], matrix[1, at, cols], matrix[2, at, cols] = adam_step(
                matrix[0, at, cols], matrix[1, at, cols], matrix[2, at, cols], grad
            )
        for i in range(3):
            pltpu.make_async_copy(matrix.at[i, at], outs[i].at[at], out_sem).start()
        if r == 0:
            whole(vector, vector_sem).wait()
            for first, row in ((0, 0), (3, 1)):
                grad = jnp.concatenate(
                    [
                        g_ref[k, features : features + 16, :].astype(F32)[row : row + 1]
                        + g_ref[k, features : features + 16, :].astype(F32)[row + 2 : row + 3]
                        for k in range(g_ref.shape[0])
                    ],
                    axis=1,
                )
                vector[first], vector[first + 1], vector[first + 2] = adam_step(
                    vector[first], vector[first + 1], vector[first + 2], grad
                )
            for i in range(6):
                pltpu.make_async_copy(vector.at[i], outs[3 + i], back_sem).start()
    doc_copy.wait()
    whole(vector, back_sem).wait()
    whole(matrix, out_sem).wait()


def adam(grads, doc, matrices, vectors):
    features, hidden = matrices[0].shape
    steps = 4
    vmem = pl.BlockSpec(memory_space=pltpu.VMEM)
    hbm = pl.BlockSpec(memory_space=pl.ANY)
    dma = pltpu.SemaphoreType.DMA
    operands = [*matrices, *(v.reshape(1, hidden) for v in vectors)]
    outs = pl.pallas_call(
        functools.partial(adam_kernel, steps, 4),
        in_specs=[vmem, vmem] + [hbm] * 9,
        out_specs=[hbm] * 10,
        out_shape=[jax.ShapeDtypeStruct(a.shape, F32) for a in [doc] + operands],
        scratch_shapes=[
            pltpu.VMEM((3, features, hidden), F32), pltpu.VMEM((6, 1, hidden), F32),
            dma((steps,)), dma, dma, dma, dma,
        ],
        compiler_params=pltpu.CompilerParams(vmem_limit_bytes=60 << 20),
    )(grads, doc, *operands)
    return (*outs[:4], *(v.reshape(hidden) for v in outs[4:]))


def per_device(
    log_rows, query_ids, doc_ranks, row_counts, list_lengths, gains,
    weight_in, bias_in, weight_out, moment_w, second_w,
    moment_b, second_b, moment_o, second_o,
):
    n, cores = lax.axis_size("dp"), lax.axis_size("mp")
    total, features = log_rows.shape
    cap = total // n
    hidden = weight_in.shape[1]
    list_width = gains.shape[1]
    unit = math.lcm(cap, LANES)
    units = total // unit

    disc = (1.0 / np.log2(2.0 + np.arange(list_width))).astype(np.float32).reshape(1, list_width)
    spans = hidden // LANES
    row_parts = max(1, n // spans)
    whole_tile = 16 * row_parts
    padded = (features + 16 + whole_tile - 1) // whole_tile * whole_tile
    grads, doc = gradients(
        n, cores, log_rows, weight_in, bias_in.reshape(1, hidden), weight_out.reshape(hidden // WIDE, 1, WIDE),
        query_ids.reshape(units, 1, unit), doc_ranks.reshape(units, 1, unit),
        gains, jnp.asarray(disc), row_counts, list_lengths, row_parts, padded // row_parts,
    )
    return adam(
        grads.reshape(spans, padded, LANES), doc, (weight_in, moment_w, second_w),
        (bias_in, moment_b, second_b, weight_out, moment_o, second_o),
    )


def solution(mesh):
    dp, mp, both = P("dp"), P("mp"), P(None, "mp")
    rows = P("dp", None)
    return jax.shard_map(
        per_device,
        mesh=mesh,
        in_specs=(rows, dp, dp, rows, dp, rows, both, mp, mp, both, both, mp, mp, mp, mp),
        out_specs=(rows, both, both, both, mp, mp, mp, mp, mp, mp),
        check_vma=False,
    )
```
